32 devices in a mesh: event: 4 (over z), terrain: 8 (over y, x, core).
Axes of the slice: x: 2, y: 2, z: 4, core: 2. Of those that a mesh axis runs over, the one named last changes fastest.
Arguments:
- level_start: float32 [4, 256, 1024], P('event', 'terrain'), may hold values from -18 to 18
- bed_depth: float32 [256, 1024], P('terrain'), may hold values from 0.5 to 2
- wet_bits: int32 [4, 256, 1024], P('event', 'terrain'), may hold values from 0 to 255
- tile_owner: int32 [2048, 1], P('terrain'), may hold values from 0 to 7; in each aligned block of 256 rows (0 to 255, 256 to 511, ...) at most 48 rows name the same one
- vuln_weight: bfloat16 [128, 256], replicated, may hold values from -0.5 to 0.5
- vuln_bias: float32 [256], replicated, may hold values from -2 to 2
- account_index: int32 [3072, 128], P('terrain'), may hold values from 0 to 1023
- bin_index: int32 [3072, 128], P('terrain'), may hold values from 0 to 255
- exposure_value: bfloat16 [3072, 128], P('terrain'), may hold values from 1 to 10
- deductible: float32 [1024], replicated, may hold values from 0 to 0.8
- limit: float32 [1024], replicated, may hold values from 0.5 to 1.5
Outputs:
- level: float32 [4, 256, 1024], P('event', 'terrain')
- net_loss: bfloat16 [4, 1024, 256], P('event')
- portfolio: float32 [1024, 256], P('terrain')
The draws below stay inside these ranges and needn't reach their ends.
Inputs may be any that keep to these rules, and one draw needn't show every extreme that they name: `tile_owner`: among the 256 tiles of one device no owner is named more than 48 times; in some devices one owner is named exactly 48 times. `wet_bits`: bit s (the value // 2**s, mod 2) is 1 where the cell is wet in substep s. `account_index`: rows of an owner's records that no tile reaches are not read.
All inputs are finite; a program needn't handle non-finite values.
Results may differ from the reference program's by a relative error of at most 0.0004.
The reference program's roundings to bfloat16 on the way (of `pieces` and `ratio`) count: a program that leaves them out, or rounds other values in their place, can miss the bound.
Values may be sent and summed in bfloat16 or wider, within the bound.
A program may use at most 64 MiB of HBM per device.

```python
import math
import jax
import jax.numpy as jnp
import numpy as np
from jax import lax

NY = 1024
TILE = 128
BINS = 256
ACCOUNTS = 1024
SUBSTEPS = 8
GROUPS = 4
ROWS = 256
TILES_DEV = 256
TILES = 2048
CAP = 48
SLOTS = 384
N_TERRAIN = 8


def set_ends(array, stream_key, least, top_value):
    longest = array.shape.index(max(array.shape))
    spots = []
    for shift in (0, 1):
        where = [jax.random.randint(jax.random.fold_in(stream_key, axis), (), 0, length) for axis, length in enumerate(array.shape)]
        where[longest] = (where[longest] + shift) % array.shape[longest]
        spots.append(tuple(where))
    return array.at[spots[0]].set(least).at[spots[1]].set(top_value)


def level_of(stream_key, extent, shards, low, top_value):
    loudness, own = 1.0, jax.random.fold_in(stream_key, 6)
    for dim, shards_of in shards:
        draws = jnp.exp(jax.random.uniform(jax.random.fold_in(own, dim), (shards_of,), jnp.float32, low / len(shards), top_value / len(shards)))
        loudness = loudness * jnp.repeat(draws, extent[dim] // shards_of).reshape([-1 if axis == dim else 1 for axis in range(len(extent))])
    return loudness


def routed_block(stream_key, own, number, rows, count, top, bound, lean):
    order = jax.random.permutation(stream_key, count)
    packed, common = shares(count, rows * top, bound, lean, True), shares(count, rows * top, bound, lean, False)
    places = jnp.arange(count)

    def named(lengths, offset_by):
        used = int((lengths > 0).sum())
        fixed = max(1, used // 4)
        passed = fixed + (places - fixed + offset_by * (used - fixed)) % max(1, count - fixed)
        return jnp.zeros((count,), jnp.int32).at[order[jnp.where(places < fixed, places, passed)]].set(jnp.asarray(lengths, jnp.int32))

    lengths = jnp.where(number % 4 == 0, named(packed, number // 4), named(common, number - number // 4 - 1))
    mixed = jax.random.permutation(jax.random.fold_in(own, 3), count)
    donor, sink = mixed[0:count // 2 * 2:2], mixed[1:count // 2 * 2:2]
    room = jnp.minimum(lengths[donor] - 1, bound - lengths[sink]) // 2
    room = jnp.where((donor == order[0]) | (sink == order[0]) | (lengths[sink] == 0), 0, jnp.maximum(room, 0))
    passed = jax.random.randint(jax.random.fold_in(own, 4), (count // 2,), 0, 1 << 20) % (room + 1)
    lengths = lengths.at[donor].add(-passed).at[sink].add(passed)
    items = jnp.searchsorted(jnp.cumsum(lengths), jnp.arange(rows * top), side="right").astype(jnp.int32)
    table = items.reshape(top, rows).T
    table = table[jax.random.permutation(jax.random.fold_in(own, 1), rows)]
    offset_by = jax.random.randint(jax.random.fold_in(own, 2), (rows, 1), 0, top)
    return jnp.take_along_axis(table, (jnp.arange(top)[None, :] + offset_by) % top, axis=1)


def shares(number_of, total, most, lean, full):
    loads = [(1 << 20) // math.isqrt(grade ** lean) + 1 for grade in range(1, number_of + 1)]
    largest = most if full else min(most, max(-(-total // number_of), total * loads[0] // sum(loads)))
    least = 1 if total - largest >= number_of - 1 else 0
    holding, spare = [largest] + [least] * (number_of - 1), total - largest - least * (number_of - 1)
    while spare > 0:
        candidates = [i for i in range(1, number_of) if holding[i] < largest] or [i for i in range(1, number_of) if holding[i] < most]
        whole, remaining = sum([loads[i] for i in candidates]), spare
        for i in candidates:
            addition = min(most - holding[i], max(1, remaining * loads[i] // whole), spare)
            holding[i] = holding[i] + addition
            spare = spare - addition
    return np.array(holding)


def bell_draw(own_key, shape, width, reach, split=(), held_as=jnp.bfloat16):
    loudness = level_of(own_key, shape, split, -0.22, 0.18) if split else 1.0
    result = jax.random.normal(own_key, shape, jnp.float32) * width * loudness
    return jnp.minimum(jnp.maximum(result, -reach), reach).astype(held_as)


def setup_inputs(seed: int = 0) -> dict:
    splits = jax.random.split(jax.random.key(seed), 12)
    level_start = bell_draw(splits[0], (GROUPS, ROWS, NY), 3.0, 18.0, ((0, 4), (1, 8)), jnp.float32)
    bed_depth = jnp.clip(jnp.exp(math.log(2.0) - 1.3862944 * jax.random.uniform(splits[1], (ROWS, NY), jnp.float32) ** level_of(splits[1], (ROWS, NY), ((0, 8),), -0.2, 0.2)), 0.5, 2.0)
    wet_bits = set_ends(jax.random.randint(splits[2], (GROUPS, ROWS, NY), 0, 2 ** SUBSTEPS), jax.random.fold_in(splits[2], 1), 0, (2 ** SUBSTEPS) - 1).astype(jnp.int32)
    tile_owner_keys = jax.random.split(jax.random.fold_in(splits[3], 1), TILES // TILES_DEV)
    tile_owner_turns = jax.random.permutation(jax.random.fold_in(splits[3], 3), TILES // TILES_DEV)
    tile_owner = jax.vmap(lambda own, number: routed_block(jax.random.fold_in(splits[3], 2), own, number, TILES_DEV, N_TERRAIN, 1, CAP, 2))(tile_owner_keys, tile_owner_turns).reshape((TILES, 1))
    vuln_weight = bell_draw(splits[4], (TILE, BINS), TILE ** -0.5, 0.5)
    vuln_bias = jnp.clip(jax.random.uniform(splits[5], (BINS,), jnp.float32, -2.0, 2.0), -2.0, 2.0)
    account_index = set_ends(jax.random.randint(splits[6], (N_TERRAIN * SLOTS, TILE), 0, ACCOUNTS), jax.random.fold_in(splits[6], 1), 0, ACCOUNTS - 1).astype(jnp.int32)
    bin_index = set_ends(jax.random.randint(splits[7], (N_TERRAIN * SLOTS, TILE), 0, BINS), jax.random.fold_in(splits[7], 1), 0, BINS - 1).astype(jnp.int32)
    exposure_value = jnp.clip(jnp.exp(math.log(10.0) - 2.3025851 * jax.random.uniform(splits[8], (N_TERRAIN * SLOTS, TILE), jnp.float32) ** level_of(splits[8], (N_TERRAIN * SLOTS, TILE), ((0, 8),), -0.2, 0.2)), 1.0, 10.0).astype(jnp.bfloat16)
    deductible = jnp.clip(jax.random.uniform(splits[9], (ACCOUNTS,), jnp.float32, 0.0, 0.8), 0.0, 0.8)
    limit = jnp.clip(jax.random.uniform(splits[10], (ACCOUNTS,), jnp.float32, 0.5, 1.5), 0.5, 1.5)
    return dict(level_start=level_start, bed_depth=bed_depth, wet_bits=wet_bits, tile_owner=tile_owner, vuln_weight=vuln_weight, vuln_bias=vuln_bias, account_index=account_index, bin_index=bin_index, exposure_value=exposure_value, deductible=deductible, limit=limit)


courant = 0.5
gravity = 1.0


def pad_columns(field):
    return jnp.pad(field[:, 1:-1, :], ((0, 0), (0, 0), (1, 1)))


def neighbour_mean(field):
    inner = pad_columns(field)
    return 0.25 * (field[:, 2:, :] + field[:, :-2, :] + inner[:, :, 2:] + inner[:, :, :-2])


def friedrichs_step(level, row_speed, col_speed, bed_depth, wet_factor):
    row_flow = bed_depth * row_speed
    col_flow = pad_columns(bed_depth * col_speed)
    level_pad = pad_columns(level)
    new_level = neighbour_mean(level) - 0.5 * courant * ((row_flow[:, 2:, :] - row_flow[:, :-2, :]) + (col_flow[:, :, 2:] - col_flow[:, :, :-2]))
    new_row = (neighbour_mean(row_speed) - 0.5 * courant * gravity * (level[:, 2:, :] - level[:, :-2, :])) * wet_factor
    new_col = (neighbour_mean(col_speed) - 0.5 * courant * gravity * (level_pad[:, :, 2:] - level_pad[:, :, :-2])) * wet_factor
    return new_level, new_row, new_col


def pad_rows(field):
    return jnp.pad(field, ((0, 0), (1, 1), (0, 0)))


def reference(level_start, bed_depth, wet_bits, tile_owner, vuln_weight, vuln_bias, account_index, bin_index, exposure_value, deductible, limit):
    level = level_start
    row_speed = jnp.zeros_like(level_start)
    col_speed = jnp.zeros_like(level_start)
    bed_pad = jnp.pad(bed_depth, ((1, 1), (0, 0)))
    for step in range(SUBSTEPS):
        wet_factor = ((wet_bits // (2 ** step)) % 2).astype(jnp.float32)
        level, row_speed, col_speed = friedrichs_step(pad_rows(level), pad_rows(row_speed), pad_rows(col_speed), bed_pad, wet_factor)
    pieces = level.astype(jnp.bfloat16).reshape(GROUPS, TILES, TILE)
    owner = tile_owner[:, 0].reshape(N_TERRAIN, TILES_DEV)
    onehot = (owner[:, :, None] == jnp.arange(N_TERRAIN, dtype=jnp.int32)[None, None, :]).astype(jnp.int32)
    rank = jnp.sum((jnp.cumsum(onehot, axis=1) - onehot) * onehot, axis=2)
    source = jnp.arange(N_TERRAIN, dtype=jnp.int32)[:, None]
    record = (owner * SLOTS + source * CAP + rank).reshape(TILES).astype(jnp.int32)
    accounts = account_index[record]
    thresholds = bin_index[record]
    values = exposure_value[record]
    block = math.gcd(TILES, 256)
    bin_range = jnp.arange(BINS, dtype=jnp.int32)

    def group_loss(tiles_group):
        ratio = jax.nn.sigmoid(jnp.dot(tiles_group, vuln_weight, preferred_element_type=jnp.float32) + vuln_bias).astype(jnp.bfloat16)

        def add_block(total, block_id):
            start = (block_id * block).astype(jnp.int32)
            ratio_part = lax.dynamic_slice_in_dim(ratio, start, block, 0).astype(jnp.float32)
            account_part = lax.dynamic_slice_in_dim(accounts, start, block, 0)
            threshold_part = lax.dynamic_slice_in_dim(thresholds, start, block, 0)
            value_part = lax.dynamic_slice_in_dim(values, start, block, 0).astype(jnp.float32)
            inside = (bin_range[None, None, :] >= threshold_part[:, :, None]).astype(jnp.float32)
            weight = value_part[:, :, None] * ratio_part[:, None, :] * inside
            total = total + jax.ops.segment_sum(weight.reshape(-1, BINS), account_part.reshape(-1), num_segments=ACCOUNTS)
            return total, None

        total, _ = lax.scan(add_block, jnp.zeros((ACCOUNTS, BINS), jnp.float32), jnp.arange(TILES // block, dtype=jnp.int32))
        return total

    gross = lax.map(group_loss, pieces)
    scaled = gross * (ACCOUNTS / (ROWS * NY))
    net = jnp.minimum(jnp.maximum(scaled - deductible[None, :, None], 0.0), limit[None, :, None])
    portfolio = jnp.sum(net, axis=0) / GROUPS
    return level, net.astype(jnp.bfloat16), portfolio
```

```python
import functools

import jax
import jax.numpy as jnp
from jax import lax
from jax.experimental import pallas as pl
from jax.experimental.pallas import tpu as pltpu
from jax.sharding import PartitionSpec as P

SUBSTEPS = 8
CHUNK = 8
HALVES = 2
GROUPS = 4

courant = 0.5
gravity = 1.0

VMEM = pl.BlockSpec(memory_space=pltpu.VMEM)
SMEM = pl.BlockSpec(memory_space=pltpu.SMEM)
MESH = pl.DeviceIdType.MESH


def exchange_kernel(jobs, *refs):
    count = len(jobs)
    sources, targets, sems = refs[:count], refs[count : 2 * count], refs[2 * count :]
    barrier = pltpu.get_barrier_semaphore()
    greeted = 0
    for axis in dict.fromkeys(axis for axis, _ in jobs):
        size = lax.axis_size(axis)
        me = lax.axis_index(axis)
        for hop in range(1, size):
            pl.semaphore_signal(
                barrier, inc=1, device_id={axis: lax.rem(me + hop, size)}, device_id_type=MESH
            )
        greeted += size - 1
    pl.semaphore_wait(barrier, greeted)
    copies = []
    for job, (axis, spread) in enumerate(jobs):
        source, target = sources[job], targets[job]
        local, sent, received = sems[3 * job : 3 * job + 3]
        size = lax.axis_size(axis)
        me = lax.axis_index(axis)
        for hop in range(1, size):
            peer = lax.rem(me + hop, size)
            copy = pltpu.make_async_remote_copy(
                src_ref=source if spread else source.at[peer],
                dst_ref=target.at[me],
                send_sem=sent.at[hop],
                recv_sem=received.at[hop],
                device_id={axis: peer},
                device_id_type=MESH,
            )
            copy.start()
            copies.append(copy)
        own = pltpu.make_async_copy(source if spread else source.at[me], target.at[me], local)
        own.start()
        copies.append(own)
    for copy in copies:
        copy.wait()


def exchange(arrays, jobs, number):
    shapes, scratch = [], []
    for array, (axis, spread) in zip(arrays, jobs):
        size = lax.axis_size(axis)
        shape = (size,) + array.shape if spread else array.shape
        shapes.append(jax.ShapeDtypeStruct(shape, array.dtype))
        scratch += [
            pltpu.SemaphoreType.DMA,
            pltpu.SemaphoreType.DMA((size,)),
            pltpu.SemaphoreType.DMA((size,)),
        ]
    return pl.pallas_call(
        functools.partial(exchange_kernel, jobs),
        out_shape=shapes,
        in_specs=[VMEM] * len(arrays),
        out_specs=[VMEM] * len(arrays),
        scratch_shapes=scratch,
        compiler_params=pltpu.CompilerParams(collective_id=number, has_side_effects=True),
        name="exchange" + str(number),
    )(*arrays)


def settle_kernel(
    scale, parts, floor, roof, net_loss, portfolio,
    made, made_low, kept, kept_low, arrived, summed, kept_sum, local,
    sent_low, got_low, sent_net, got_net, sent_sum, got_sum,
):
    owners, share_rows, _ = parts.shape
    events = lax.axis_size("event")
    me, group = lax.axis_index("terrain"), lax.axis_index("event")
    barrier = pltpu.get_barrier_semaphore()
    for axis, size, mine in (("terrain", owners, me), ("event", events, group)):
        for hop in range(1, size):
            pl.semaphore_signal(
                barrier, inc=1, device_id={axis: lax.rem(mine + hop, size)}, device_id_type=MESH
            )
    whole = parts[0]
    for n in range(1, owners):
        whole = whole + parts[n]
    picked = (share_rows, floor.shape[1])
    account = lax.broadcasted_iota(jnp.int32, picked, 1)
    mine = account == lax.broadcasted_iota(jnp.int32, picked, 0) + me * share_rows

    def of_share(terms):
        return jnp.sum(jnp.where(mine, terms[...], 0.0), axis=1, keepdims=True)

    net = jnp.minimum(jnp.maximum(whole * scale - of_share(floor), 0.0), of_share(roof))
    made[...] = net.reshape(made.shape)
    made_low[...] = net.astype(made_low.dtype)
    first = [
        pltpu.make_async_copy(made, kept, local.at[0]),
        pltpu.make_async_copy(made_low, kept_low, local.at[1]),
    ]
    for copy in first:
        copy.start()
    pl.semaphore_wait(barrier, owners + events - 2)
    for copy in first:
        copy.wait()

    def push(axis, size, index, source, target, sent, received, split):
        copies = []
        for hop in range(1, size):
            peer = lax.rem(index + hop, size)
            copy = pltpu.make_async_remote_copy(
                src_ref=source.at[peer] if split else source,
                dst_ref=target.at[index],
                send_sem=sent.at[hop],
                recv_sem=received.at[hop],
                device_id={axis: peer},
                device_id_type=MESH,
            )
            copy.start()
            copies.append(copy)
        return copies

    nets = push("event", events, group, kept, arrived, sent_net, got_net, True)
    own_net = pltpu.make_async_copy(kept.at[group], arrived.at[group], local.at[2])
    own_net.start()
    lows = push("terrain", owners, me, kept_low, net_loss, sent_low, got_low, False)
    own_low = pltpu.make_async_copy(kept_low, net_loss.at[me], local.at[3])
    own_low.start()
    for copy in nets + [own_net]:
        copy.wait()
    total = arrived[0]
    for n in range(1, events):
        total = total + arrived[n]
    summed[...] = total / events
    last = pltpu.make_async_copy(summed, kept_sum, local.at[4])
    last.start()
    last.wait()
    sums = push("event", events, group, kept_sum, portfolio, sent_sum, got_sum, False)
    own_sum = pltpu.make_async_copy(kept_sum, portfolio.at[group], local.at[5])
    own_sum.start()
    for copy in sums + [own_sum] + lows + [own_low]:
        copy.wait()


def settle(parts, floor, roof, scale, number):
    owners, share_rows, bins = parts.shape
    events = lax.axis_size("event")
    split = (events, share_rows // events, bins)
    dma = pltpu.SemaphoreType.DMA
    return pl.pallas_call(
        functools.partial(settle_kernel, scale),
        out_shape=(
            jax.ShapeDtypeStruct((owners, share_rows, bins), jnp.bfloat16),
            jax.ShapeDtypeStruct(split, jnp.float32),
        ),
        in_specs=[VMEM] * 3,
        out_specs=(VMEM, VMEM),
        scratch_shapes=[
            pltpu.VMEM(split, jnp.float32),
            pltpu.VMEM((share_rows, bins), jnp.bfloat16),
            pltpu.VMEM(split, jnp.float32),
            pltpu.VMEM((share_rows, bins), jnp.bfloat16),
            pltpu.VMEM(split, jnp.float32),
            pltpu.VMEM(split[1:], jnp.float32),
            pltpu.VMEM(split[1:], jnp.float32),
            dma((6,)),
        ]
        + [dma((owners,))] * 2
        + [dma((events,))] * 4,
        compiler_params=pltpu.CompilerParams(collective_id=number, has_side_effects=True),
        name="settle",
    )(parts, floor, roof)


def padded(count, unit):
    return -(-count // unit) * unit


def front_kernel(
    level_here, bed_here, wet_here, account, threshold, value, owner_row, weight, bias,
    level_out, ratio_out, low_out, bin_out, value_out,
    made, kept, got, level_above, bed_above, wet_above, level_below, bed_below, wet_below,
    halo_sent, halo_got, cell_sent, cell_got, local,
):
    size = lax.axis_size("terrain")
    me = lax.axis_index("terrain")
    barrier = pltpu.get_barrier_semaphore()
    for hop in range(1, size):
        pl.semaphore_signal(
            barrier, inc=1, device_id={"terrain": lax.rem(me + hop, size)}, device_id_type=MESH
        )
    rows, width = level_here.shape
    capacity = account.shape[0] // size
    room = made.shape[2]

    accounts = account[...]
    low = (accounts & 255) - ((accounts >> 8) & 1) * 256
    bound = threshold[...] - (accounts >> 9) * 256
    fields = (low.astype(jnp.float32), bound.astype(jnp.float32), value[...].astype(jnp.float32))
    if room != capacity:
        made[...] = jnp.zeros(made.shape, made.dtype)
    for n in range(size):
        for f in range(3):
            made[n, f, :capacity, :] = fields[f][n * capacity : (n + 1) * capacity].astype(
                made.dtype
            )
    keep = pltpu.make_async_copy(made, kept, local.at[0])
    keep.start()
    pl.semaphore_wait(barrier, size - 1)

    later, earlier = lax.rem(me + 1, size), lax.rem(me + size - 1, size)
    strips = (level_here, bed_here, wet_here)
    above = (level_above, bed_above, wet_above)
    below = (level_below, bed_below, wet_below)
    edges = []
    for side, (peer, targets) in enumerate(((later, above), (earlier, below))):
        for i in range(3):
            first = 0 if side else rows - SUBSTEPS
            copy = pltpu.make_async_remote_copy(
                src_ref=strips[i].at[pl.ds(first, SUBSTEPS)],
                dst_ref=targets[i],
                send_sem=halo_sent.at[side * 3 + i],
                recv_sem=halo_got.at[side * 3 + i],
                device_id={"terrain": peer},
                device_id_type=MESH,
            )
            copy.start()
            edges.append(copy)
    keep.wait()
    cells = []
    for hop in range(1, size):
        peer = lax.rem(me + hop, size)
        copy = pltpu.make_async_remote_copy(
            src_ref=kept.at[peer],
            dst_ref=got.at[me],
            send_sem=cell_sent.at[hop],
            recv_sem=cell_got.at[hop],
            device_id={"terrain": peer},
            device_id_type=MESH,
        )
        copy.start()
        cells.append(copy)
    own = pltpu.make_async_copy(kept.at[me], got.at[me], local.at[1])
    own.start()
    cells.append(own)

    tile = weight.shape[0]
    blocks = width // tile
    tiles = rows * blocks
    number = lax.broadcasted_iota(jnp.int32, (tiles, tiles), 0)
    number = (number % rows) * blocks + number // rows
    along = lax.broadcasted_iota(jnp.int32, (tiles, tiles), 1)
    owner = owner_row[...].astype(jnp.float32)
    owner_column = jnp.sum(jnp.where(along == number, owner, 0.0), axis=1, keepdims=True)
    same = (owner_column == owner) & (along < number)
    rank = jnp.sum(jnp.where(same, 1.0, 0.0), axis=1, keepdims=True)
    slot = lax.broadcasted_iota(jnp.int32, (tiles, size * room), 1).astype(jnp.float32)
    chosen = jnp.where(slot == owner_column * room + rank, 1.0, 0.0).astype(jnp.bfloat16)

    for copy in edges:
        copy.wait()
    first_row = me * rows - SUBSTEPS
    total_rows = rows * size
    level = jnp.concatenate([level_above[...], level_here[...], level_below[...]], axis=0)
    bed = jnp.concatenate([bed_above[...], bed_here[...], bed_below[...]], axis=0)
    wet = jnp.concatenate([wet_above[...], wet_here[...], wet_below[...]], axis=0)
    shape = level.shape
    tall = shape[0]
    row_id = first_row + lax.broadcasted_iota(jnp.int32, shape, 0)
    column = lax.broadcasted_iota(jnp.int32, shape, 1)
    inside = ((row_id >= 0) & (row_id < total_rows)).astype(jnp.float32)
    not_first = (column > 0).astype(jnp.float32)
    not_last = (column < width - 1).astype(jnp.float32)

    def down(field):
        return pltpu.roll(field, tall - 1, 0)

    def up(field):
        return pltpu.roll(field, 1, 0)

    def right(field):
        return pltpu.roll(field, width - 1, 1) * not_last

    def left(field):
        return pltpu.roll(field, 1, 1) * not_first

    quarter = 0.25
    assert courant * gravity == 0.5
    level = level * inside
    row_speed = jnp.zeros(shape, jnp.float32)
    col_speed = jnp.zeros(shape, jnp.float32)
    for step in range(SUBSTEPS):
        wet_factor = ((wet >> step) & 1).astype(jnp.float32) * (inside * quarter)
        if step:
            row_flow, col_flow = bed * row_speed, bed * col_speed
            new_level = (
                down(level - row_flow) + up(level + row_flow)
                + (right(level - col_flow) + left(level + col_flow))
            )
            new_row = (
                down(row_speed - level) + up(row_speed + level)
                + (right(row_speed) + left(row_speed))
            )
            new_col = (
                down(col_speed) + up(col_speed)
                + (right(col_speed - level) + left(col_speed + level))
            )
            row_speed, col_speed = new_row * wet_factor, new_col * wet_factor
        else:
            ld, lu, lr, ll = down(level), up(level), right(level), left(level)
            new_level = ld + lu + (lr + ll)
            row_speed = (lu - ld) * wet_factor
            col_speed = (ll - lr) * wet_factor
        level = new_level * (inside * quarter)
    level = level[SUBSTEPS : SUBSTEPS + rows]
    level_out[...] = level
    pieces = jnp.concatenate(
        [level[:, j * tile : (j + 1) * tile] for j in range(blocks)], axis=0
    ).astype(jnp.bfloat16)
    ratio_out[...] = jax.nn.sigmoid(
        jnp.dot(pieces, weight[...], preferred_element_type=jnp.float32) + bias[...]
    ).astype(jnp.bfloat16)
    for copy in cells:
        copy.wait()
    for f, target in enumerate((low_out, bin_out, value_out)):
        records = jnp.concatenate([got[n, f] for n in range(size)], axis=0)
        target[...] = jnp.dot(chosen, records, preferred_element_type=jnp.float32).astype(
            target.dtype
        )


def front(strips, records, owner_row, weight, bias, number):
    rows, width = strips[0].shape
    slots, cells = records[0].shape
    size = lax.axis_size("terrain")
    tiles = rows * width // cells
    packed = (size, 3, padded(slots // size, 16), cells)
    edge = (SUBSTEPS, width)
    dma = pltpu.SemaphoreType.DMA
    edges = [pltpu.VMEM(edge, f.dtype) for f in strips]
    return pl.pallas_call(
        front_kernel,
        out_shape=(
            jax.ShapeDtypeStruct((rows, width), jnp.float32),
            jax.ShapeDtypeStruct((tiles, weight.shape[1]), jnp.bfloat16),
        )
        + (jax.ShapeDtypeStruct((tiles, cells), jnp.bfloat16),) * 3,
        in_specs=[VMEM] * 9,
        out_specs=(VMEM,) * 5,
        scratch_shapes=[pltpu.VMEM(packed, jnp.bfloat16)] * 3
        + edges * 2
        + [dma((6,))] * 2
        + [dma((size,))] * 2
        + [dma((2,))],
        compiler_params=pltpu.CompilerParams(collective_id=number, has_side_effects=True),
        name="front",
    )(*strips, *records, owner_row, weight, bias)


def rowed(row, height):
    packed = jnp.broadcast_to(row, (16, row.shape[1])).astype(jnp.bfloat16)
    return jnp.concatenate([packed] * (height // 16), axis=0)


def numbered(height, width, axis):
    return (
        lax.broadcasted_iota(jnp.int32, (height, width), axis)
        .astype(jnp.float32)
        .astype(jnp.bfloat16)
    )


def loss_kernel(
    low_in, bin_in, value_in, ratio_in, total,
    ratio, meta, places, lows, bounds, values, *halves,
):
    accounts, bins = total.shape
    tiles, cells = low_in.shape
    groups = lows.shape[0]
    group_size = accounts // groups
    capacity = 2 * cells // groups
    together = cells // capacity
    bundles = tiles // together
    zero = jnp.zeros((), jnp.bfloat16)
    one = jnp.ones((), jnp.bfloat16)

    low = low_in[...].astype(jnp.float32)
    bound = bin_in[...].astype(jnp.float32)
    high = jnp.where(low < 0, 1, 0) + jnp.where(bound < 0, 2, 0)
    low = jnp.where(low < 0, low + 256.0, low).astype(jnp.int32) + high * 256
    bound = jnp.where(bound < 0, bound + 256.0, bound)
    group = low // group_size
    low = low % group_size
    value = value_in[...].astype(jnp.float32)
    ratio[...] = ratio_in[...].astype(jnp.float32)
    earlier = jnp.where(
        lax.broadcasted_iota(jnp.int32, (cells, cells), 0)
        < lax.broadcasted_iota(jnp.int32, (cells, cells), 1),
        1.0,
        0.0,
    ).astype(jnp.bfloat16)
    turn = lax.broadcasted_iota(jnp.int32, (tiles, cells), 0) % together
    rank = jnp.zeros((tiles, cells), jnp.float32)
    for h in range(groups):
        mine = group == h
        count = jnp.dot(
            jnp.where(mine, 1.0, 0.0).astype(jnp.bfloat16),
            earlier,
            preferred_element_type=jnp.float32,
        )
        rank = jnp.where(mine, count, rank)
    base = (group // together) * cells + ((group + turn) % together) * capacity
    fits = rank < capacity
    places[...] = jnp.where(fits, base.astype(jnp.float32) + rank, -1.0)
    meta[:, 0, :] = low.astype(jnp.float32)
    meta[:, 1, :] = bound
    meta[:, 2, :] = value
    meta[:, 3, :] = group.astype(jnp.float32)
    spilled = jnp.max(rank) >= capacity

    place_id = numbered(2 * cells, cells, 0)
    lane = lax.broadcasted_iota(jnp.int32, (8, cells), 1) // capacity

    def gather(bundle, _):
        found = []
        for j in range(together):
            t = bundle * together + j
            here = rowed(places[pl.ds(t, 1), :], 2 * cells) == place_id
            found.append(
                lax.dot_general(
                    meta[t].astype(jnp.bfloat16),
                    jnp.where(here, one, zero),
                    (((1,), (1,)), ((), ())),
                    preferred_element_type=jnp.float32,
                )
            )
        for q in range(2):
            parts = [f[:, q * cells : (q + 1) * cells] for f in found]
            for r in range(together):
                mixed = parts[(0 - r) % together]
                for e in range(1, together):
                    mixed = jnp.where(lane == e, parts[(e - r) % together], mixed)
                h = q * together + r
                lows[h, pl.ds(bundle, 1), :] = mixed[0:1]
                bounds[h, pl.ds(bundle, 1), :] = mixed[1:2]
                values[h, pl.ds(bundle, 1), :] = mixed[2:3]
        return 0

    lax.fori_loop(0, bundles, gather, 0)

    total[...] = jnp.zeros(total.shape, jnp.float32)
    account_id = numbered(group_size, cells, 0)
    bin_row = numbered(16, bins, 1)
    bin_id = jnp.concatenate([bin_row] * (cells // 16), axis=0)
    count = len(halves) // 2
    half = halves[1].shape[0] // cells

    for h in range(groups):
        rows = pl.ds(h * group_size, group_size)

        def chunk(number, _):
            first = pl.multiple_of(number * CHUNK, CHUNK)
            first_tile = pl.multiple_of(number * CHUNK * together, CHUNK * together)
            low_rows = lows[h, pl.ds(first, CHUNK), :]
            value_rows = values[h, pl.ds(first, CHUNK), :]
            columns = jnp.transpose(bounds[h, pl.ds(first, CHUNK), :])
            ratios = ratio[pl.ds(first_tile, CHUNK * together), :]
            for i in range(CHUNK):
                left, right = halves[i // half * 2 : i // half * 2 + 2]
                spot = slice(i % half * cells, (i % half + 1) * cells)
                left[:, spot] = jnp.where(
                    rowed(low_rows[i : i + 1], group_size) == account_id,
                    rowed(value_rows[i : i + 1], group_size),
                    zero,
                )
                bound = jnp.broadcast_to(columns[:, i : i + 1], (cells, bins)).astype(jnp.bfloat16)
                shown = []
                for e in range(together):
                    t = i * together + (e - h) % together
                    shown.append(rowed(ratios[t : t + 1], capacity))
                right[spot, :] = jnp.where(
                    bin_id >= bound, jnp.concatenate(shown, axis=0), zero
                )
            for n in range(count):
                total[rows, :] += jnp.dot(
                    halves[2 * n][...], halves[2 * n + 1][...], preferred_element_type=jnp.float32
                )
            return 0

        lax.fori_loop(0, bundles // CHUNK, chunk, 0)

    @pl.when(spilled)
    def _():
        def dense(t, _):
            fields = meta[t]
            rest = jnp.where(places[pl.ds(t, 1), :] < 0, fields[2:3], 0.0)

            @pl.when(jnp.max(rest) > 0)
            def _():
                hit = rowed(fields[0:1], group_size) == account_id
                column = jnp.transpose(fields)[:, 1:2]
                bound = jnp.broadcast_to(column, (cells, bins)).astype(jnp.bfloat16)
                right = jnp.where(bin_id >= bound, rowed(ratio[pl.ds(t, 1), :], cells), zero)
                for h in range(groups):
                    part = jnp.where(fields[3:4] == h, rest, 0.0)
                    left = jnp.where(hit, rowed(part, group_size), zero)
                    total[pl.ds(h * group_size, group_size), :] += jnp.dot(
                        left, right, preferred_element_type=jnp.float32
                    )

            return 0

        lax.fori_loop(0, tiles, dense, 0)


def losses(low, bound, value, ratio, account_count):
    tiles, cells = low.shape
    bins = ratio.shape[1]
    groups = GROUPS
    together = groups // 2
    gathered = pltpu.VMEM((groups, tiles // together, cells), jnp.float32)
    return pl.pallas_call(
        loss_kernel,
        out_shape=jax.ShapeDtypeStruct((account_count, bins), jnp.float32),
        in_specs=[VMEM] * 4,
        out_specs=VMEM,
        scratch_shapes=[
            pltpu.VMEM((tiles, bins), jnp.float32),
            pltpu.VMEM((tiles, 8, cells), jnp.float32),
            pltpu.VMEM((tiles, cells), jnp.float32),
            gathered, gathered, gathered,
        ]
        + [
            pltpu.VMEM((account_count // groups, CHUNK // HALVES * cells), jnp.bfloat16),
            pltpu.VMEM((CHUNK // HALVES * cells, bins), jnp.bfloat16),
        ]
        * HALVES,
        name="losses",
    )(low, bound, value, ratio)


def per_device(
    level_start,
    bed_depth,
    wet_bits,
    tile_owner,
    vuln_weight,
    vuln_bias,
    account_index,
    bin_index,
    exposure_value,
    deductible,
    limit,
):
    _, rows, width = level_start.shape
    tile_cells, bin_count = vuln_weight.shape
    account_count = deductible.shape[0]
    owners = lax.axis_size("terrain")
    events = lax.axis_size("event")
    share_rows = account_count // owners
    tiles = rows * width // tile_cells
    level, ratio, low, bound, value = front(
        [level_start[0], bed_depth, wet_bits[0]],
        [account_index, bin_index, exposure_value],
        tile_owner.reshape(1, tiles),
        vuln_weight,
        vuln_bias[None, :],
        1,
    )
    total = losses(low, bound, value, ratio, account_count)
    (parts,) = exchange(
        [total.reshape(owners, share_rows, bin_count)], [("terrain", False)], 2
    )
    scale = account_count / (rows * width * owners)
    net_loss, portfolio = settle(parts, deductible[None, :], limit[None, :], scale, 3)
    portfolio = portfolio.reshape(share_rows, bin_count)
    return (level[None], net_loss.reshape(1, account_count, bin_count), portfolio)


def solution(mesh):
    placed = (
        P("event", "terrain", None),
        P("terrain", None),
        P("event", "terrain", None),
        P("terrain", None),
        P(),
        P(),
        P("terrain", None),
        P("terrain", None),
        P("terrain", None),
        P(),
        P(),
    )
    return jax.shard_map(
        per_device,
        mesh=mesh,
        in_specs=placed,
        out_specs=(P("event", "terrain", None), P("event", None, None), P("terrain", None)),
        check_vma=False,
    )
```

```python
import functools

import jax
import jax.numpy as jnp
from jax import lax
from jax.experimental import pallas as pl
from jax.experimental.pallas import tpu as pltpu
from jax.sharding import PartitionSpec as P

SUBSTEPS = 8
CHUNK = 8
GROUPS = 8
SPAN = 32
BUFFERS = 2
UNROLL = 8

courant = 0.5
gravity = 1.0

VMEM = pl.BlockSpec(memory_space=pltpu.VMEM)
SMEM = pl.BlockSpec(memory_space=pltpu.SMEM)
MESH = pl.DeviceIdType.MESH


def exchange_kernel(jobs, *refs):
    count = len(jobs)
    sources, targets, sems = refs[:count], refs[count : 2 * count], refs[2 * count :]
    barrier = pltpu.get_barrier_semaphore()
    greeted = 0
    for axis in dict.fromkeys(axis for axis, _ in jobs):
        size = lax.axis_size(axis)
        me = lax.axis_index(axis)
        for hop in range(1, size):
            pl.semaphore_signal(
                barrier, inc=1, device_id={axis: lax.rem(me + hop, size)}, device_id_type=MESH
            )
        greeted += size - 1
    pl.semaphore_wait(barrier, greeted)
    copies = []
    for job, (axis, spread) in enumerate(jobs):
        source, target = sources[job], targets[job]
        local, sent, received = sems[3 * job : 3 * job + 3]
        size = lax.axis_size(axis)
        me = lax.axis_index(axis)
        for hop in range(1, size):
            peer = lax.rem(me + hop, size)
            copy = pltpu.make_async_remote_copy(
                src_ref=source if spread else source.at[peer],
                dst_ref=target.at[me],
                send_sem=sent.at[hop],
                recv_sem=received.at[hop],
                device_id={axis: peer},
                device_id_type=MESH,
            )
            copy.start()
            copies.append(copy)
        own = pltpu.make_async_copy(source if spread else source.at[me], target.at[me], local)
        own.start()
        copies.append(own)
    for copy in copies:
        copy.wait()


def exchange(arrays, jobs, number):
    shapes, scratch = [], []
    for array, (axis, spread) in zip(arrays, jobs):
        size = lax.axis_size(axis)
        shape = (size,) + array.shape if spread else array.shape
        shapes.append(jax.ShapeDtypeStruct(shape, array.dtype))
        scratch += [
            pltpu.SemaphoreType.DMA,
            pltpu.SemaphoreType.DMA((size,)),
            pltpu.SemaphoreType.DMA((size,)),
        ]
    return pl.pallas_call(
        functools.partial(exchange_kernel, jobs),
        out_shape=shapes,
        in_specs=[VMEM] * len(arrays),
        out_specs=[VMEM] * len(arrays),
        scratch_shapes=scratch,
        compiler_params=pltpu.CompilerParams(collective_id=number, has_side_effects=True),
        name="exchange" + str(number),
    )(*arrays)


def settle_kernel(
    scale, parts, floor, roof, net_loss, portfolio,
    made, made_low, kept, kept_low, arrived, summed, kept_sum, local,
    sent_low, got_low, sent_net, got_net, sent_sum, got_sum,
):
    owners, share_rows, _ = parts.shape
    events = lax.axis_size("event")
    me, group = lax.axis_index("terrain"), lax.axis_index("event")
    barrier = pltpu.get_barrier_semaphore()
    for axis, size, mine in (("terrain", owners, me), ("event", events, group)):
        for hop in range(1, size):
            pl.semaphore_signal(
                barrier, inc=1, device_id={axis: lax.rem(mine + hop, size)}, device_id_type=MESH
            )
    whole = parts[0]
    for n in range(1, owners):
        whole = whole + parts[n]
    picked = (share_rows, floor.shape[1])
    account = lax.broadcasted_iota(jnp.int32, picked, 1)
    mine = account == lax.broadcasted_iota(jnp.int32, picked, 0) + me * share_rows

    def of_share(terms):
        return jnp.sum(jnp.where(mine, terms[...], 0.0), axis=1, keepdims=True)

    net = jnp.minimum(jnp.maximum(whole * scale - of_share(floor), 0.0), of_share(roof))
    made[...] = net.reshape(made.shape)
    made_low[...] = net.astype(made_low.dtype)
    first = [
        pltpu.make_async_copy(made, kept, local.at[0]),
        pltpu.make_async_copy(made_low, kept_low, local.at[1]),
    ]
    for copy in first:
        copy.start()
    pl.semaphore_wait(barrier, owners + events - 2)
    for copy in first:
        copy.wait()

    def push(axis, size, index, source, target, sent, received, split):
        copies = []
        for hop in range(1, size):
            peer = lax.rem(index + hop, size)
            copy = pltpu.make_async_remote_copy(
                src_ref=source.at[peer] if split else source,
                dst_ref=target.at[index],
                send_sem=sent.at[hop],
                recv_sem=received.at[hop],
                device_id={axis: peer},
                device_id_type=MESH,
            )
            copy.start()
            copies.append(copy)
        return copies

    nets = push("event", events, group, kept, arrived, sent_net, got_net, True)
    own_net = pltpu.make_async_copy(kept.at[group], arrived.at[group], local.at[2])
    own_net.start()
    lows = push("terrain", owners, me, kept_low, net_loss, sent_low, got_low, False)
    own_low = pltpu.make_async_copy(kept_low, net_loss.at[me], local.at[3])
    own_low.start()
    for copy in nets + [own_net]:
        copy.wait()
    total = arrived[0]
    for n in range(1, events):
        total = total + arrived[n]
    summed[...] = total / events
    last = pltpu.make_async_copy(summed, kept_sum, local.at[4])
    last.start()
    last.wait()
    sums = push("event", events, group, kept_sum, portfolio, sent_sum, got_sum, False)
    own_sum = pltpu.make_async_copy(kept_sum, portfolio.at[group], local.at[5])
    own_sum.start()
    for copy in sums + [own_sum] + lows + [own_low]:
        copy.wait()


def settle(parts, floor, roof, scale, number):
    owners, share_rows, bins = parts.shape
    events = lax.axis_size("event")
    split = (events, share_rows // events, bins)
    dma = pltpu.SemaphoreType.DMA
    return pl.pallas_call(
        functools.partial(settle_kernel, scale),
        out_shape=(
            jax.ShapeDtypeStruct((owners, share_rows, bins), jnp.bfloat16),
            jax.ShapeDtypeStruct(split, jnp.float32),
        ),
        in_specs=[VMEM] * 3,
        out_specs=(VMEM, VMEM),
        scratch_shapes=[
            pltpu.VMEM(split, jnp.float32),
            pltpu.VMEM((share_rows, bins), jnp.bfloat16),
            pltpu.VMEM(split, jnp.float32),
            pltpu.VMEM((share_rows, bins), jnp.bfloat16),
            pltpu.VMEM(split, jnp.float32),
            pltpu.VMEM(split[1:], jnp.float32),
            pltpu.VMEM(split[1:], jnp.float32),
            dma((6,)),
        ]
        + [dma((owners,))] * 2
        + [dma((events,))] * 4,
        compiler_params=pltpu.CompilerParams(collective_id=number, has_side_effects=True),
        name="settle",
    )(parts, floor, roof)


def padded(count, unit):
    return -(-count // unit) * unit


def front_kernel(
    level_here, bed_here, wet_here, account, threshold, value, owner_row, weight, bias,
    level_out, ratio_out, low_out, bin_out, value_out,
    made, kept, got, level_above, bed_above, wet_above, level_below, bed_below, wet_below,
    halo_sent, halo_got, cell_sent, cell_got, local,
):
    size = lax.axis_size("terrain")
    me = lax.axis_index("terrain")
    barrier = pltpu.get_barrier_semaphore()
    for hop in range(1, size):
        pl.semaphore_signal(
            barrier, inc=1, device_id={"terrain": lax.rem(me + hop, size)}, device_id_type=MESH
        )
    rows, width = level_here.shape
    capacity = account.shape[0] // size
    room = made.shape[2]

    accounts = account[...]
    low = (accounts & 255) - ((accounts >> 8) & 1) * 256
    bound = threshold[...] - (accounts >> 9) * 256
    fields = (low.astype(jnp.float32), bound.astype(jnp.float32), value[...].astype(jnp.float32))
    if room != capacity:
        made[...] = jnp.zeros(made.shape, made.dtype)
    for n in range(size):
        for f in range(3):
            made[n, f, :capacity, :] = fields[f][n * capacity : (n + 1) * capacity].astype(
                made.dtype
            )
    keep = pltpu.make_async_copy(made, kept, local.at[0])
    keep.start()
    pl.semaphore_wait(barrier, size - 1)

    later, earlier = lax.rem(me + 1, size), lax.rem(me + size - 1, size)
    strips = (level_here, bed_here, wet_here)
    above = (level_above, bed_above, wet_above)
    below = (level_below, bed_below, wet_below)
    edges = []
    for side, (peer, targets) in enumerate(((later, above), (earlier, below))):
        for i in range(3):
            first = 0 if side else rows - SUBSTEPS
            copy = pltpu.make_async_remote_copy(
                src_ref=strips[i].at[pl.ds(first, SUBSTEPS)],
                dst_ref=targets[i],
                send_sem=halo_sent.at[side * 3 + i],
                recv_sem=halo_got.at[side * 3 + i],
                device_id={"terrain": peer},
                device_id_type=MESH,
            )
            copy.start()
            edges.append(copy)
    keep.wait()
    cells = []
    for hop in range(1, size):
        peer = lax.rem(me + hop, size)
        copy = pltpu.make_async_remote_copy(
            src_ref=kept.at[peer],
            dst_ref=got.at[me],
            send_sem=cell_sent.at[hop],
            recv_sem=cell_got.at[hop],
            device_id={"terrain": peer},
            device_id_type=MESH,
        )
        copy.start()
        cells.append(copy)
    own = pltpu.make_async_copy(kept.at[me], got.at[me], local.at[1])
    own.start()
    cells.append(own)

    tile = weight.shape[0]
    blocks = width // tile
    tiles = rows * blocks
    number = lax.broadcasted_iota(jnp.int32, (tiles, tiles), 0)
    number = (number % rows) * blocks + number // rows
    along = lax.broadcasted_iota(jnp.int32, (tiles, tiles), 1)
    owner = owner_row[...].astype(jnp.float32)
    owner_column = jnp.sum(jnp.where(along == number, owner, 0.0), axis=1, keepdims=True)
    same = (owner_column == owner) & (along < number)
    rank = jnp.sum(jnp.where(same, 1.0, 0.0), axis=1, keepdims=True)
    slot = lax.broadcasted_iota(jnp.int32, (tiles, size * room), 1).astype(jnp.float32)
    chosen = jnp.where(slot == owner_column * room + rank, 1.0, 0.0).astype(jnp.bfloat16)

    for copy in edges:
        copy.wait()
    first_row = me * rows - SUBSTEPS
    total_rows = rows * size
    level = jnp.concatenate([level_above[...], level_here[...], level_below[...]], axis=0)
    bed = jnp.concatenate([bed_above[...], bed_here[...], bed_below[...]], axis=0)
    wet = jnp.concatenate([wet_above[...], wet_here[...], wet_below[...]], axis=0)
    shape = level.shape
    tall = shape[0]
    row_id = first_row + lax.broadcasted_iota(jnp.int32, shape, 0)
    column = lax.broadcasted_iota(jnp.int32, shape, 1)
    inside = ((row_id >= 0) & (row_id < total_rows)).astype(jnp.float32)
    not_first = (column > 0).astype(jnp.float32)
    not_last = (column < width - 1).astype(jnp.float32)

    def down(field):
        return pltpu.roll(field, tall - 1, 0)

    def up(field):
        return pltpu.roll(field, 1, 0)

    def right(field):
        return pltpu.roll(field, width - 1, 1) * not_last

    def left(field):
        return pltpu.roll(field, 1, 1) * not_first

    quarter = 0.25
    assert courant * gravity == 0.5
    level = level * inside
    row_speed = jnp.zeros(shape, jnp.float32)
    col_speed = jnp.zeros(shape, jnp.float32)
    for step in range(SUBSTEPS):
        wet_factor = ((wet >> step) & 1).astype(jnp.float32) * (inside * quarter)
        if step:
            row_flow, col_flow = bed * row_speed, bed * col_speed
            new_level = (
                down(level - row_flow) + up(level + row_flow)
                + (right(level - col_flow) + left(level + col_flow))
            )
            new_row = (
                down(row_speed - level) + up(row_speed + level)
                + (right(row_speed) + left(row_speed))
            )
            new_col = (
                down(col_speed) + up(col_speed)
                + (right(col_speed - level) + left(col_speed + level))
            )
            row_speed, col_speed = new_row * wet_factor, new_col * wet_factor
        else:
            ld, lu, lr, ll = down(level), up(level), right(level), left(level)
            new_level = ld + lu + (lr + ll)
            row_speed = (lu - ld) * wet_factor
            col_speed = (ll - lr) * wet_factor
        level = new_level * (inside * quarter)
    level = level[SUBSTEPS : SUBSTEPS + rows]
    level_out[...] = level
    pieces = jnp.concatenate(
        [level[:, j * tile : (j + 1) * tile] for j in range(blocks)], axis=0
    ).astype(jnp.bfloat16)
    ratio_out[...] = jax.nn.sigmoid(
        jnp.dot(pieces, weight[...], preferred_element_type=jnp.float32) + bias[...]
    ).astype(jnp.bfloat16)
    for copy in cells:
        copy.wait()
    for f, target in enumerate((low_out, bin_out, value_out)):
        records = jnp.concatenate([got[n, f] for n in range(size)], axis=0)
        target[...] = jnp.dot(chosen, records, preferred_element_type=jnp.float32).astype(
            target.dtype
        )


def front(strips, records, owner_row, weight, bias, number):
    rows, width = strips[0].shape
    slots, cells = records[0].shape
    size = lax.axis_size("terrain")
    tiles = rows * width // cells
    packed = (size, 3, padded(slots // size, 16), cells)
    edge = (SUBSTEPS, width)
    dma = pltpu.SemaphoreType.DMA
    edges = [pltpu.VMEM(edge, f.dtype) for f in strips]
    return pl.pallas_call(
        front_kernel,
        out_shape=(
            jax.ShapeDtypeStruct((rows, width), jnp.float32),
            jax.ShapeDtypeStruct((tiles, weight.shape[1]), jnp.bfloat16),
        )
        + (jax.ShapeDtypeStruct((tiles, cells), jnp.bfloat16),) * 3,
        in_specs=[VMEM] * 9,
        out_specs=(VMEM,) * 5,
        scratch_shapes=[pltpu.VMEM(packed, jnp.bfloat16)] * 3
        + edges * 2
        + [dma((6,))] * 2
        + [dma((size,))] * 2
        + [dma((2,))],
        compiler_params=pltpu.CompilerParams(collective_id=number, has_side_effects=True),
        name="front",
    )(*strips, *records, owner_row, weight, bias)


def rowed(row, height):
    packed = jnp.broadcast_to(row, (16, row.shape[1])).astype(jnp.bfloat16)
    return jnp.concatenate([packed] * (height // 16), axis=0)


def numbered(height, width, axis):
    return (
        lax.broadcasted_iota(jnp.int32, (height, width), axis)
        .astype(jnp.float32)
        .astype(jnp.bfloat16)
    )


def loss_kernel(
    low_in, bin_in, value_in, ratio_in, total,
    ratio, low_all, bound_all, value_all, places, lows, bounds, values, *halves,
):
    accounts, bins = total.shape
    tiles, cells = low_in.shape
    groups = lows.shape[0]
    group_size = accounts // groups
    capacity = 2 * cells // groups
    together = cells // capacity
    bundles = tiles // together
    zero = jnp.zeros((), jnp.bfloat16)
    one = jnp.ones((), jnp.bfloat16)

    low = low_in[...].astype(jnp.float32)
    bound = bin_in[...].astype(jnp.float32)
    high = jnp.where(low < 0, 256.0, 0.0) + jnp.where(bound < 0, 512.0, 0.0)
    low = jnp.where(low < 0, low + 256.0, low) + high
    group = low.astype(jnp.int32) // group_size
    low_all[...] = low - (group * group_size).astype(jnp.float32)
    bound_all[...] = jnp.where(bound < 0, bound + 256.0, bound)
    value_all[...] = value_in[...].astype(jnp.float32)
    ratio[...] = ratio_in[...].astype(jnp.float32)
    earlier = jnp.where(
        lax.broadcasted_iota(jnp.int32, (cells, cells), 0)
        < lax.broadcasted_iota(jnp.int32, (cells, cells), 1),
        1.0,
        0.0,
    ).astype(jnp.bfloat16)
    turn = lax.broadcasted_iota(jnp.int32, (tiles, cells), 0) % together
    rank = jnp.zeros((tiles, cells), jnp.float32)
    for h in range(groups):
        mine = group == h
        count = jnp.dot(
            jnp.where(mine, 1.0, 0.0).astype(jnp.bfloat16),
            earlier,
            preferred_element_type=jnp.float32,
        )
        rank = jnp.where(mine, count, rank)
    base = (group // together) * cells + ((group + turn) % together) * capacity
    fits = rank < capacity
    places[...] = jnp.where(fits, base.astype(jnp.float32) + rank, -1.0 - group.astype(jnp.float32))

    place_id = numbered(2 * cells, cells, 0)
    lane = lax.broadcasted_iota(jnp.int32, (8, cells), 1) // capacity
    field = lax.broadcasted_iota(jnp.int32, (8, cells), 0)
    unroll = max(1, UNROLL // together)

    def spread(ref, t):
        return jnp.broadcast_to(ref[pl.ds(t, 1), :], (8, cells))

    def gather(number, _):
        for u in range(unroll):
            bundle = number * unroll + u
            found = []
            for j in range(together):
                t = bundle * together + j
                here = rowed(places[pl.ds(t, 1), :], 2 * cells) == place_id
                fields = jnp.where(
                    field == 0,
                    spread(low_all, t),
                    jnp.where(field == 1, spread(bound_all, t), spread(value_all, t)),
                )
                found.append(
                    lax.dot_general(
                        fields.astype(jnp.bfloat16),
                        jnp.where(here, one, zero),
                        (((1,), (1,)), ((), ())),
                        preferred_element_type=jnp.float32,
                    )
                )
            for q in range(2):
                parts = [f[:, q * cells : (q + 1) * cells] for f in found]
                for r in range(together):
                    mixed = parts[(0 - r) % together]
                    for e in range(1, together):
                        mixed = jnp.where(lane == e, parts[(e - r) % together], mixed)
                    h = q * together + r
                    lows[h, pl.ds(bundle, 1), :] = mixed[0:1]
                    bounds[h, pl.ds(bundle, 1), :] = mixed[1:2]
                    values[h, pl.ds(bundle, 1), :] = mixed[2:3]
        return 0

    lax.fori_loop(0, bundles // unroll, gather, 0)

    account_id = numbered(group_size, cells, 0)
    bin_id = jnp.concatenate([numbered(16, bins, 1)] * (cells // 16), axis=0)
    buffers = len(halves) // 2
    span = halves[1].shape[0] // cells

    def one_group(h, _):
        rows = pl.ds(pl.multiple_of(h * group_size, group_size), group_size)
        summed = None
        for c in range(bundles // span):
            left, right = halves[c % buffers * 2 : c % buffers * 2 + 2]
            for block in range(span // CHUNK):
                first = c * span + block * CHUNK
                columns = jnp.transpose(bounds[h, first : first + CHUNK, :]).astype(jnp.bfloat16)
                for i in range(CHUNK):
                    bundle = first + i
                    spot = slice((block * CHUNK + i) * cells, (block * CHUNK + i + 1) * cells)
                    left[:, spot] = jnp.where(
                        rowed(lows[h, bundle : bundle + 1, :], group_size) == account_id,
                        rowed(values[h, bundle : bundle + 1, :], group_size),
                        zero,
                    )
                    shown = []
                    for e in range(together):
                        t = bundle * together + lax.rem(e + groups - h, together)
                        shown.append(rowed(ratio[pl.ds(t, 1), :], capacity))
                    right[spot, :] = jnp.where(
                        bin_id >= jnp.broadcast_to(columns[:, i : i + 1], (cells, bins)),
                        jnp.concatenate(shown, axis=0),
                        zero,
                    )
            part = jnp.dot(left[...], right[...], preferred_element_type=jnp.float32)
            summed = part if summed is None else summed + part
        total[rows, :] = summed
        return 0

    lax.fori_loop(0, groups, one_group, 0)

    spilled = jnp.max(rank) >= capacity

    @pl.when(spilled)
    def _():
        tile_id = lax.broadcasted_iota(jnp.int32, (tiles, cells), 0).astype(jnp.float32)

        def dense(left_over):
            t = left_over.astype(jnp.int32)
            place = places[pl.ds(t, 1), :]
            rest = jnp.where(place < 0, value_all[pl.ds(t, 1), :], 0.0)
            hit = rowed(low_all[pl.ds(t, 1), :], group_size) == account_id
            column = jnp.transpose(spread(bound_all, t)).astype(jnp.bfloat16)[:, 0:1]
            right = jnp.where(
                bin_id >= jnp.broadcast_to(column, (cells, bins)),
                rowed(ratio[pl.ds(t, 1), :], cells),
                zero,
            )
            for h in range(groups):
                part = jnp.where(place == -1.0 - h, rest, 0.0)
                left = jnp.where(hit, rowed(part, group_size), zero)
                total[pl.ds(h * group_size, group_size), :] += jnp.dot(
                    left, right, preferred_element_type=jnp.float32
                )
            return jnp.max(jnp.where((places[...] < 0) & (tile_id < left_over), tile_id, -1.0))

        lax.while_loop(
            lambda t: t >= 0, dense, jnp.max(jnp.where(places[...] < 0, tile_id, -1.0))
        )


def losses(low, bound, value, ratio, account_count):
    tiles, cells = low.shape
    bins = ratio.shape[1]
    groups = GROUPS
    together = groups // 2
    gathered = pltpu.VMEM((groups, tiles // together, cells), jnp.float32)
    whole = pltpu.VMEM((tiles, cells), jnp.float32)
    return pl.pallas_call(
        loss_kernel,
        out_shape=jax.ShapeDtypeStruct((account_count, bins), jnp.float32),
        in_specs=[VMEM] * 4,
        out_specs=VMEM,
        scratch_shapes=[pltpu.VMEM((tiles, bins), jnp.float32)]
        + [whole] * 4
        + [gathered] * 3
        + [
            pltpu.VMEM((account_count // groups, SPAN * cells), jnp.bfloat16),
            pltpu.VMEM((SPAN * cells, bins), jnp.bfloat16),
        ]
        * BUFFERS,
        name="losses",
    )(low, bound, value, ratio)


def per_device(
    level_start,
    bed_depth,
    wet_bits,
    tile_owner,
    vuln_weight,
    vuln_bias,
    account_index,
    bin_index,
    exposure_value,
    deductible,
    limit,
):
    _, rows, width = level_start.shape
    tile_cells, bin_count = vuln_weight.shape
    account_count = deductible.shape[0]
    owners = lax.axis_size("terrain")
    events = lax.axis_size("event")
    share_rows = account_count // owners
    tiles = rows * width // tile_cells
    level, ratio, low, bound, value = front(
        [level_start[0], bed_depth, wet_bits[0]],
        [account_index, bin_index, exposure_value],
        tile_owner.reshape(1, tiles),
        vuln_weight,
        vuln_bias[None, :],
        1,
    )
    total = losses(low, bound, value, ratio, account_count)
    (parts,) = exchange(
        [total.reshape(owners, share_rows, bin_count)], [("terrain", False)], 2
    )
    scale = account_count / (rows * width * owners)
    net_loss, portfolio = settle(parts, deductible[None, :], limit[None, :], scale, 3)
    portfolio = portfolio.reshape(share_rows, bin_count)
    return (level[None], net_loss.reshape(1, account_count, bin_count), portfolio)


def solution(mesh):
    placed = (
        P("event", "terrain", None),
        P("terrain", None),
        P("event", "terrain", None),
        P("terrain", None),
        P(),
        P(),
        P("terrain", None),
        P("terrain", None),
        P("terrain", None),
        P(),
        P(),
    )
    return jax.shard_map(
        per_device,
        mesh=mesh,
        in_specs=placed,
        out_specs=(P("event", "terrain", None), P("event", None, None), P("terrain", None)),
        check_vma=False,
    )
```

```python
import functools

import jax
import jax.numpy as jnp
from jax import lax
from jax.experimental import pallas as pl
from jax.experimental.pallas import tpu as pltpu
from jax.sharding import PartitionSpec as P

SUBSTEPS = 8
CHUNK = 8
GROUPS = 8
SPAN = 32
UNROLL = 16

courant = 0.5
gravity = 1.0

VMEM = pl.BlockSpec(memory_space=pltpu.VMEM)
SMEM = pl.BlockSpec(memory_space=pltpu.SMEM)
MESH = pl.DeviceIdType.MESH


def exchange_kernel(jobs, *refs):
    count = len(jobs)
    sources, targets, sems = refs[:count], refs[count : 2 * count], refs[2 * count :]
    barrier = pltpu.get_barrier_semaphore()
    greeted = 0
    for axis in dict.fromkeys(axis for axis, _ in jobs):
        size = lax.axis_size(axis)
        me = lax.axis_index(axis)
        for hop in range(1, size):
            pl.semaphore_signal(
                barrier, inc=1, device_id={axis: lax.rem(me + hop, size)}, device_id_type=MESH
            )
        greeted += size - 1
    pl.semaphore_wait(barrier, greeted)
    copies = []
    for job, (axis, spread) in enumerate(jobs):
        source, target = sources[job], targets[job]
        local, sent, received = sems[3 * job : 3 * job + 3]
        size = lax.axis_size(axis)
        me = lax.axis_index(axis)
        for hop in range(1, size):
            peer = lax.rem(me + hop, size)
            copy = pltpu.make_async_remote_copy(
                src_ref=source if spread else source.at[peer],
                dst_ref=target.at[me],
                send_sem=sent.at[hop],
                recv_sem=received.at[hop],
                device_id={axis: peer},
                device_id_type=MESH,
            )
            copy.start()
            copies.append(copy)
        own = pltpu.make_async_copy(source if spread else source.at[me], target.at[me], local)
        own.start()
        copies.append(own)
    for copy in copies:
        copy.wait()


def exchange(arrays, jobs, number):
    shapes, scratch = [], []
    for array, (axis, spread) in zip(arrays, jobs):
        size = lax.axis_size(axis)
        shape = (size,) + array.shape if spread else array.shape
        shapes.append(jax.ShapeDtypeStruct(shape, array.dtype))
        scratch += [
            pltpu.SemaphoreType.DMA,
            pltpu.SemaphoreType.DMA((size,)),
            pltpu.SemaphoreType.DMA((size,)),
        ]
    return pl.pallas_call(
        functools.partial(exchange_kernel, jobs),
        out_shape=shapes,
        in_specs=[VMEM] * len(arrays),
        out_specs=[VMEM] * len(arrays),
        scratch_shapes=scratch,
        compiler_params=pltpu.CompilerParams(collective_id=number, has_side_effects=True),
        name="exchange" + str(number),
    )(*arrays)


def settle_kernel(
    scale, parts, floor, roof, net_loss, portfolio,
    made, made_low, kept, kept_low, arrived, summed, kept_sum, local,
    sent_low, got_low, sent_net, got_net, sent_sum, got_sum,
):
    owners, share_rows, _ = parts.shape
    events = lax.axis_size("event")
    me, group = lax.axis_index("terrain"), lax.axis_index("event")
    barrier = pltpu.get_barrier_semaphore()
    for axis, size, mine in (("terrain", owners, me), ("event", events, group)):
        for hop in range(1, size):
            pl.semaphore_signal(
                barrier, inc=1, device_id={axis: lax.rem(mine + hop, size)}, device_id_type=MESH
            )
    whole = parts[0]
    for n in range(1, owners):
        whole = whole + parts[n]
    picked = (share_rows, floor.shape[1])
    account = lax.broadcasted_iota(jnp.int32, picked, 1)
    mine = account == lax.broadcasted_iota(jnp.int32, picked, 0) + me * share_rows

    def of_share(terms):
        return jnp.sum(jnp.where(mine, terms[...], 0.0), axis=1, keepdims=True)

    net = jnp.minimum(jnp.maximum(whole * scale - of_share(floor), 0.0), of_share(roof))
    made[...] = net.reshape(made.shape)
    made_low[...] = net.astype(made_low.dtype)
    first = [
        pltpu.make_async_copy(made, kept, local.at[0]),
        pltpu.make_async_copy(made_low, kept_low, local.at[1]),
    ]
    for copy in first:
        copy.start()
    pl.semaphore_wait(barrier, owners + events - 2)
    for copy in first:
        copy.wait()

    def push(axis, size, index, source, target, sent, received, split):
        copies = []
        for hop in range(1, size):
            peer = lax.rem(index + hop, size)
            copy = pltpu.make_async_remote_copy(
                src_ref=source.at[peer] if split else source,
                dst_ref=target.at[index],
                send_sem=sent.at[hop],
                recv_sem=received.at[hop],
                device_id={axis: peer},
                device_id_type=MESH,
            )
            copy.start()
            copies.append(copy)
        return copies

    nets = push("event", events, group, kept, arrived, sent_net, got_net, True)
    own_net = pltpu.make_async_copy(kept.at[group], arrived.at[group], local.at[2])
    own_net.start()
    lows = push("terrain", owners, me, kept_low, net_loss, sent_low, got_low, False)
    own_low = pltpu.make_async_copy(kept_low, net_loss.at[me], local.at[3])
    own_low.start()
    for copy in nets + [own_net]:
        copy.wait()
    total = arrived[0]
    for n in range(1, events):
        total = total + arrived[n]
    summed[...] = total / events
    last = pltpu.make_async_copy(summed, kept_sum, local.at[4])
    last.start()
    last.wait()
    sums = push("event", events, group, kept_sum, portfolio, sent_sum, got_sum, False)
    own_sum = pltpu.make_async_copy(kept_sum, portfolio.at[group], local.at[5])
    own_sum.start()
    for copy in sums + [own_sum] + lows + [own_low]:
        copy.wait()


def settle(parts, floor, roof, scale, number):
    owners, share_rows, bins = parts.shape
    events = lax.axis_size("event")
    split = (events, share_rows // events, bins)
    dma = pltpu.SemaphoreType.DMA
    return pl.pallas_call(
        functools.partial(settle_kernel, scale),
        out_shape=(
            jax.ShapeDtypeStruct((owners, share_rows, bins), jnp.bfloat16),
            jax.ShapeDtypeStruct(split, jnp.float32),
        ),
        in_specs=[VMEM] * 3,
        out_specs=(VMEM, VMEM),
        scratch_shapes=[
            pltpu.VMEM(split, jnp.float32),
            pltpu.VMEM((share_rows, bins), jnp.bfloat16),
            pltpu.VMEM(split, jnp.float32),
            pltpu.VMEM((share_rows, bins), jnp.bfloat16),
            pltpu.VMEM(split, jnp.float32),
            pltpu.VMEM(split[1:], jnp.float32),
            pltpu.VMEM(split[1:], jnp.float32),
            dma((6,)),
        ]
        + [dma((owners,))] * 2
        + [dma((events,))] * 4,
        compiler_params=pltpu.CompilerParams(collective_id=number, has_side_effects=True),
        name="settle",
    )(parts, floor, roof)


def padded(count, unit):
    return -(-count // unit) * unit


def front_kernel(
    level_here, bed_here, wet_here, account, threshold, value, owner_row, weight, bias,
    level_out, ratio_out, low_out, bin_out, value_out,
    made, kept, got, level_above, bed_above, wet_above, level_below, bed_below, wet_below,
    halo_sent, halo_got, cell_sent, cell_got, local,
):
    size = lax.axis_size("terrain")
    me = lax.axis_index("terrain")
    barrier = pltpu.get_barrier_semaphore()
    for hop in range(1, size):
        pl.semaphore_signal(
            barrier, inc=1, device_id={"terrain": lax.rem(me + hop, size)}, device_id_type=MESH
        )
    rows, width = level_here.shape
    capacity = account.shape[0] // size
    room = made.shape[2]

    accounts = account[...]
    low = (accounts & 255) - ((accounts >> 8) & 1) * 256
    bound = threshold[...] - (accounts >> 9) * 256
    fields = (low.astype(jnp.float32), bound.astype(jnp.float32), value[...].astype(jnp.float32))
    if room != capacity:
        made[...] = jnp.zeros(made.shape, made.dtype)
    for n in range(size):
        for f in range(3):
            made[n, f, :capacity, :] = fields[f][n * capacity : (n + 1) * capacity].astype(
                made.dtype
            )
    keep = pltpu.make_async_copy(made, kept, local.at[0])
    keep.start()
    pl.semaphore_wait(barrier, size - 1)

    later, earlier = lax.rem(me + 1, size), lax.rem(me + size - 1, size)
    strips = (level_here, bed_here, wet_here)
    above = (level_above, bed_above, wet_above)
    below = (level_below, bed_below, wet_below)
    edges = []
    for side, (peer, targets) in enumerate(((later, above), (earlier, below))):
        for i in range(3):
            first = 0 if side else rows - SUBSTEPS
            copy = pltpu.make_async_remote_copy(
                src_ref=strips[i].at[pl.ds(first, SUBSTEPS)],
                dst_ref=targets[i],
                send_sem=halo_sent.at[side * 3 + i],
                recv_sem=halo_got.at[side * 3 + i],
                device_id={"terrain": peer},
                device_id_type=MESH,
            )
            copy.start()
            edges.append(copy)
    keep.wait()
    cells = []
    for hop in range(1, size):
        peer = lax.rem(me + hop, size)
        copy = pltpu.make_async_remote_copy(
            src_ref=kept.at[peer],
            dst_ref=got.at[me],
            send_sem=cell_sent.at[hop],
            recv_sem=cell_got.at[hop],
            device_id={"terrain": peer},
            device_id_type=MESH,
        )
        copy.start()
        cells.append(copy)
    own = pltpu.make_async_copy(kept.at[me], got.at[me], local.at[1])
    own.start()
    cells.append(own)

    tile = weight.shape[0]
    blocks = width // tile
    tiles = rows * blocks
    number = lax.broadcasted_iota(jnp.int32, (tiles, tiles), 0)
    number = (number % rows) * blocks + number // rows
    along = lax.broadcasted_iota(jnp.int32, (tiles, tiles), 1)
    owner = owner_row[...].astype(jnp.float32)
    owner_column = jnp.sum(jnp.where(along == number, owner, 0.0), axis=1, keepdims=True)
    same = (owner_column == owner) & (along < number)
    rank = jnp.sum(jnp.where(same, 1.0, 0.0), axis=1, keepdims=True)
    slot = lax.broadcasted_iota(jnp.int32, (tiles, size * room), 1).astype(jnp.float32)
    chosen = jnp.where(slot == owner_column * room + rank, 1.0, 0.0).astype(jnp.bfloat16)

    for copy in edges:
        copy.wait()
    first_row = me * rows - SUBSTEPS
    total_rows = rows * size
    level = jnp.concatenate([level_above[...], level_here[...], level_below[...]], axis=0)
    bed = jnp.concatenate([bed_above[...], bed_here[...], bed_below[...]], axis=0)
    wet = jnp.concatenate([wet_above[...], wet_here[...], wet_below[...]], axis=0)
    shape = level.shape
    tall = shape[0]
    row_id = first_row + lax.broadcasted_iota(jnp.int32, shape, 0)
    column = lax.broadcasted_iota(jnp.int32, shape, 1)
    inside = ((row_id >= 0) & (row_id < total_rows)).astype(jnp.float32)
    not_first = (column > 0).astype(jnp.float32)
    not_last = (column < width - 1).astype(jnp.float32)

    def down(field):
        return pltpu.roll(field, tall - 1, 0)

    def up(field):
        return pltpu.roll(field, 1, 0)

    def right(field):
        return pltpu.roll(field, width - 1, 1) * not_last

    def left(field):
        return pltpu.roll(field, 1, 1) * not_first

    quarter = 0.25
    assert courant * gravity == 0.5
    level = level * inside
    row_speed = jnp.zeros(shape, jnp.float32)
    col_speed = jnp.zeros(shape, jnp.float32)
    for step in range(SUBSTEPS):
        wet_factor = ((wet >> step) & 1).astype(jnp.float32) * (inside * quarter)
        if step:
            row_flow, col_flow = bed * row_speed, bed * col_speed
            new_level = (
                down(level - row_flow) + up(level + row_flow)
                + (right(level - col_flow) + left(level + col_flow))
            )
            new_row = (
                down(row_speed - level) + up(row_speed + level)
                + (right(row_speed) + left(row_speed))
            )
            new_col = (
                down(col_speed) + up(col_speed)
                + (right(col_speed - level) + left(col_speed + level))
            )
            row_speed, col_speed = new_row * wet_factor, new_col * wet_factor
        else:
            ld, lu, lr, ll = down(level), up(level), right(level), left(level)
            new_level = ld + lu + (lr + ll)
            row_speed = (lu - ld) * wet_factor
            col_speed = (ll - lr) * wet_factor
        level = new_level * (inside * quarter)
    level = level[SUBSTEPS : SUBSTEPS + rows]
    level_out[...] = level
    pieces = jnp.concatenate(
        [level[:, j * tile : (j + 1) * tile] for j in range(blocks)], axis=0
    ).astype(jnp.bfloat16)
    ratio_out[...] = jax.nn.sigmoid(
        jnp.dot(pieces, weight[...], preferred_element_type=jnp.float32) + bias[...]
    ).astype(jnp.bfloat16)
    for copy in cells:
        copy.wait()
    for f, target in enumerate((low_out, bin_out, value_out)):
        records = jnp.concatenate([got[n, f] for n in range(size)], axis=0)
        target[...] = jnp.dot(chosen, records, preferred_element_type=jnp.float32).astype(
            target.dtype
        )


def front(strips, records, owner_row, weight, bias, number):
    rows, width = strips[0].shape
    slots, cells = records[0].shape
    size = lax.axis_size("terrain")
    tiles = rows * width // cells
    packed = (size, 3, padded(slots // size, 16), cells)
    edge = (SUBSTEPS, width)
    dma = pltpu.SemaphoreType.DMA
    edges = [pltpu.VMEM(edge, f.dtype) for f in strips]
    return pl.pallas_call(
        front_kernel,
        out_shape=(
            jax.ShapeDtypeStruct((rows, width), jnp.float32),
            jax.ShapeDtypeStruct((tiles, weight.shape[1]), jnp.bfloat16),
        )
        + (jax.ShapeDtypeStruct((tiles, cells), jnp.bfloat16),) * 3,
        in_specs=[VMEM] * 9,
        out_specs=(VMEM,) * 5,
        scratch_shapes=[pltpu.VMEM(packed, jnp.bfloat16)] * 3
        + edges * 2
        + [dma((6,))] * 2
        + [dma((size,))] * 2
        + [dma((2,))],
        compiler_params=pltpu.CompilerParams(collective_id=number, has_side_effects=True),
        name="front",
    )(*strips, *records, owner_row, weight, bias)


def rowed(row, height):
    packed = jnp.broadcast_to(row, (16, row.shape[1])).astype(jnp.bfloat16)
    return jnp.concatenate([packed] * (height // 16), axis=0)


def numbered(height, width, axis):
    return (
        lax.broadcasted_iota(jnp.int32, (height, width), axis)
        .astype(jnp.float32)
        .astype(jnp.bfloat16)
    )


def loss_kernel(
    low_in, bin_in, value_in, ratio_in, total,
    ratio_all, ratio, low_all, bound_all, value_all, places, lows, bounds, values,
):
    accounts, bins = total.shape
    tiles, cells = low_in.shape
    groups = lows.shape[0]
    group_size = accounts // groups
    capacity = 2 * cells // groups
    together = cells // capacity
    bundles = tiles // together
    zero = jnp.zeros((), jnp.bfloat16)
    one = jnp.ones((), jnp.bfloat16)

    low = low_in[...].astype(jnp.float32)
    bound = bin_in[...].astype(jnp.float32)
    high = jnp.where(low < 0, 256.0, 0.0) + jnp.where(bound < 0, 512.0, 0.0)
    low = jnp.where(low < 0, low + 256.0, low) + high
    group = low.astype(jnp.int32) // group_size
    low_all[...] = low - (group * group_size).astype(jnp.float32)
    bound_all[...] = jnp.where(bound < 0, bound + 256.0, bound)
    ratio_all[...] = ratio_in[...].astype(jnp.float32)
    value_all[...] = value_in[...].astype(jnp.float32)
    earlier = jnp.where(
        lax.broadcasted_iota(jnp.int32, (cells, cells), 0)
        < lax.broadcasted_iota(jnp.int32, (cells, cells), 1),
        1.0,
        0.0,
    ).astype(jnp.bfloat16)
    turn = lax.broadcasted_iota(jnp.int32, (tiles, cells), 0) % together
    rank = jnp.zeros((tiles, cells), jnp.float32)
    for h in range(groups):
        mine = group == h
        count = jnp.dot(
            jnp.where(mine, 1.0, 0.0).astype(jnp.bfloat16),
            earlier,
            preferred_element_type=jnp.float32,
        )
        rank = jnp.where(mine, count, rank)
    base = (group // together) * cells + ((group + turn) % together) * capacity
    fits = rank < capacity
    places[...] = jnp.where(fits, base.astype(jnp.float32) + rank, -1.0 - group.astype(jnp.float32))

    place_id = numbered(2 * cells, cells, 0)
    lane = lax.broadcasted_iota(jnp.int32, (8, cells), 1) // capacity
    field = lax.broadcasted_iota(jnp.int32, (8, cells), 0)
    unroll = max(1, UNROLL // together)

    def spread(ref, t):
        return jnp.broadcast_to(ref[pl.ds(t, 1), :], (8, cells))

    def gather(number, _):
        for u in range(unroll):
            bundle = number * unroll + u
            for j in range(together):
                t = bundle * together + j
                ratio[bundle, j] = jnp.broadcast_to(
                    ratio_all[pl.ds(t, 1), :], (16, bins)
                ).astype(jnp.bfloat16)
            found = []
            for j in range(together):
                t = bundle * together + j
                here = rowed(places[pl.ds(t, 1), :], 2 * cells) == place_id
                fields = jnp.where(
                    field == 0,
                    spread(low_all, t),
                    jnp.where(field == 1, spread(bound_all, t), spread(value_all, t)),
                )
                found.append(
                    lax.dot_general(
                        fields.astype(jnp.bfloat16),
                        jnp.where(here, one, zero),
                        (((1,), (1,)), ((), ())),
                        preferred_element_type=jnp.float32,
                    )
                )
            for q in range(2):
                parts = [f[:, q * cells : (q + 1) * cells] for f in found]
                for r in range(together):
                    mixed = parts[(0 - r) % together]
                    for e in range(1, together):
                        mixed = jnp.where(lane == e, parts[(e - r) % together], mixed)
                    h = q * together + r
                    lows[h, pl.ds(bundle, 1), :] = mixed[0:1]
                    bounds[h, pl.ds(bundle, 1), :] = mixed[1:2]
                    values[h, pl.ds(bundle, 1), :] = mixed[2:3]
        return 0

    lax.fori_loop(0, bundles // unroll, gather, 0)

    account_id = numbered(group_size, cells, 0)
    bin_id = jnp.concatenate([numbered(16, bins, 1)] * (cells // 16), axis=0)
    span = min(SPAN, bundles)

    def one_group(h, _):
        rows = pl.ds(pl.multiple_of(h * group_size, group_size), group_size)
        turned = [lax.rem(e + groups - h, together) for e in range(together)]
        summed = None
        for c in range(bundles // span):
            left, right = [], []
            for block in range(span // CHUNK):
                first = c * span + block * CHUNK
                columns = jnp.transpose(bounds[h, first : first + CHUNK, :]).astype(jnp.bfloat16)
                for i in range(CHUNK):
                    bundle = first + i
                    left.append(
                        jnp.where(
                            rowed(lows[h, bundle : bundle + 1, :], group_size) == account_id,
                            rowed(values[h, bundle : bundle + 1, :], group_size),
                            zero,
                        )
                    )
                    shown = []
                    for e in range(together):
                        row = ratio[bundle, turned[e]]
                        shown.extend([row] * (capacity // 16))
                    bound = jnp.broadcast_to(columns[:, i : i + 1], (cells, bins))
                    right.append(
                        jnp.where(bin_id >= bound, jnp.concatenate(shown, axis=0), zero)
                    )
            part = jnp.dot(
                jnp.concatenate(left, axis=1),
                jnp.concatenate(right, axis=0),
                preferred_element_type=jnp.float32,
            )
            summed = part if summed is None else summed + part
        total[rows, :] = summed
        return 0

    lax.fori_loop(0, groups, one_group, 0)

    spilled = jnp.max(rank) >= capacity

    @pl.when(spilled)
    def _():
        tile_id = lax.broadcasted_iota(jnp.int32, (tiles, cells), 0).astype(jnp.float32)

        def dense(left_over):
            t = left_over.astype(jnp.int32)
            place = places[pl.ds(t, 1), :]
            rest = jnp.where(place < 0, value_all[pl.ds(t, 1), :], 0.0)
            hit = rowed(low_all[pl.ds(t, 1), :], group_size) == account_id
            column = jnp.transpose(spread(bound_all, t)).astype(jnp.bfloat16)[:, 0:1]
            right = jnp.where(
                bin_id >= jnp.broadcast_to(column, (cells, bins)),
                rowed(ratio_all[pl.ds(t, 1), :], cells),
                zero,
            )
            for h in range(groups):
                part = jnp.where(place == -1.0 - h, rest, 0.0)
                left = jnp.where(hit, rowed(part, group_size), zero)
                total[pl.ds(h * group_size, group_size), :] += jnp.dot(
                    left, right, preferred_element_type=jnp.float32
                )
            return jnp.max(jnp.where((places[...] < 0) & (tile_id < left_over), tile_id, -1.0))

        lax.while_loop(
            lambda t: t >= 0, dense, jnp.max(jnp.where(places[...] < 0, tile_id, -1.0))
        )


def losses(low, bound, value, ratio, account_count):
    tiles, cells = low.shape
    bins = ratio.shape[1]
    groups = GROUPS
    together = groups // 2
    gathered = pltpu.VMEM((groups, tiles // together, cells), jnp.float32)
    whole = pltpu.VMEM((tiles, cells), jnp.float32)
    return pl.pallas_call(
        loss_kernel,
        out_shape=jax.ShapeDtypeStruct((account_count, bins), jnp.float32),
        in_specs=[VMEM] * 4,
        out_specs=VMEM,
        scratch_shapes=[
            pltpu.VMEM((tiles, bins), jnp.float32),
            pltpu.VMEM((tiles // together, together, 16, bins), jnp.bfloat16),
        ]
        + [whole] * 4
        + [gathered] * 3,
        name="losses",
    )(low, bound, value, ratio)


def per_device(
    level_start,
    bed_depth,
    wet_bits,
    tile_owner,
    vuln_weight,
    vuln_bias,
    account_index,
    bin_index,
    exposure_value,
    deductible,
    limit,
):
    _, rows, width = level_start.shape
    tile_cells, bin_count = vuln_weight.shape
    account_count = deductible.shape[0]
    owners = lax.axis_size("terrain")
    events = lax.axis_size("event")
    share_rows = account_count // owners
    tiles = rows * width // tile_cells
    level, ratio, low, bound, value = front(
        [level_start[0], bed_depth, wet_bits[0]],
        [account_index, bin_index, exposure_value],
        tile_owner.reshape(1, tiles),
        vuln_weight,
        vuln_bias[None, :],
        1,
    )
    total = losses(low, bound, value, ratio, account_count)
    (parts,) = exchange(
        [total.reshape(owners, share_rows, bin_count)], [("terrain", False)], 2
    )
    scale = account_count / (rows * width * owners)
    net_loss, portfolio = settle(parts, deductible[None, :], limit[None, :], scale, 3)
    portfolio = portfolio.reshape(share_rows, bin_count)
    return (level[None], net_loss.reshape(1, account_count, bin_count), portfolio)


def solution(mesh):
    placed = (
        P("event", "terrain", None),
        P("terrain", None),
        P("event", "terrain", None),
        P("terrain", None),
        P(),
        P(),
        P("terrain", None),
        P("terrain", None),
        P("terrain", None),
        P(),
        P(),
    )
    return jax.shard_map(
        per_device,
        mesh=mesh,
        in_specs=placed,
        out_specs=(P("event", "terrain", None), P("event", None, None), P("terrain", None)),
        check_vma=False,
    )
```

```python
import functools

import jax
import jax.numpy as jnp
from jax import lax
from jax.experimental import pallas as pl
from jax.experimental.pallas import tpu as pltpu
from jax.sharding import PartitionSpec as P

SUBSTEPS = 8
CHUNK = 8
GROUPS = 8
SPAN = 32
UNROLL = 16

courant = 0.5
gravity = 1.0

VMEM = pl.BlockSpec(memory_space=pltpu.VMEM)
SMEM = pl.BlockSpec(memory_space=pltpu.SMEM)
MESH = pl.DeviceIdType.MESH


def exchange_kernel(jobs, *refs):
    count = len(jobs)
    sources, targets, sems = refs[:count], refs[count : 2 * count], refs[2 * count :]
    barrier = pltpu.get_barrier_semaphore()
    greeted = 0
    for axis in dict.fromkeys(axis for axis, _ in jobs):
        size = lax.axis_size(axis)
        me = lax.axis_index(axis)
        for hop in range(1, size):
            pl.semaphore_signal(
                barrier, inc=1, device_id={axis: lax.rem(me + hop, size)}, device_id_type=MESH
            )
        greeted += size - 1
    pl.semaphore_wait(barrier, greeted)
    copies = []
    for job, (axis, spread) in enumerate(jobs):
        source, target = sources[job], targets[job]
        local, sent, received = sems[3 * job : 3 * job + 3]
        size = lax.axis_size(axis)
        me = lax.axis_index(axis)
        for hop in range(1, size):
            peer = lax.rem(me + hop, size)
            copy = pltpu.make_async_remote_copy(
                src_ref=source if spread else source.at[peer],
                dst_ref=target.at[me],
                send_sem=sent.at[hop],
                recv_sem=received.at[hop],
                device_id={axis: peer},
                device_id_type=MESH,
            )
            copy.start()
            copies.append(copy)
        own = pltpu.make_async_copy(source if spread else source.at[me], target.at[me], local)
        own.start()
        copies.append(own)
    for copy in copies:
        copy.wait()


def exchange(arrays, jobs, number):
    shapes, scratch = [], []
    for array, (axis, spread) in zip(arrays, jobs):
        size = lax.axis_size(axis)
        shape = (size,) + array.shape if spread else array.shape
        shapes.append(jax.ShapeDtypeStruct(shape, array.dtype))
        scratch += [
            pltpu.SemaphoreType.DMA,
            pltpu.SemaphoreType.DMA((size,)),
            pltpu.SemaphoreType.DMA((size,)),
        ]
    return pl.pallas_call(
        functools.partial(exchange_kernel, jobs),
        out_shape=shapes,
        in_specs=[VMEM] * len(arrays),
        out_specs=[VMEM] * len(arrays),
        scratch_shapes=scratch,
        compiler_params=pltpu.CompilerParams(collective_id=number, has_side_effects=True, vmem_limit_bytes=16*2**20),
        name="exchange" + str(number),
    )(*arrays)


def settle_kernel(
    scale, parts, floor, roof, net_loss, portfolio,
    made, made_low, kept, kept_low, arrived, summed, kept_sum, local,
    sent_low, got_low, sent_net, got_net, sent_sum, got_sum,
):
    owners, share_rows, _ = parts.shape
    events = lax.axis_size("event")
    me, group = lax.axis_index("terrain"), lax.axis_index("event")
    barrier = pltpu.get_barrier_semaphore()
    for axis, size, mine in (("terrain", owners, me), ("event", events, group)):
        for hop in range(1, size):
            pl.semaphore_signal(
                barrier, inc=1, device_id={axis: lax.rem(mine + hop, size)}, device_id_type=MESH
            )
    whole = parts[0]
    for n in range(1, owners):
        whole = whole + parts[n]
    picked = (share_rows, floor.shape[1])
    account = lax.broadcasted_iota(jnp.int32, picked, 1)
    mine = account == lax.broadcasted_iota(jnp.int32, picked, 0) + me * share_rows

    def of_share(terms):
        return jnp.sum(jnp.where(mine, terms[...], 0.0), axis=1, keepdims=True)

    net = jnp.minimum(jnp.maximum(whole * scale - of_share(floor), 0.0), of_share(roof))
    made[...] = net.reshape(made.shape)
    made_low[...] = net.astype(made_low.dtype)
    first = [
        pltpu.make_async_copy(made, kept, local.at[0]),
        pltpu.make_async_copy(made_low, kept_low, local.at[1]),
    ]
    for copy in first:
        copy.start()
    pl.semaphore_wait(barrier, owners + events - 2)
    for copy in first:
        copy.wait()

    def push(axis, size, index, source, target, sent, received, split):
        copies = []
        for hop in range(1, size):
            peer = lax.rem(index + hop, size)
            copy = pltpu.make_async_remote_copy(
                src_ref=source.at[peer] if split else source,
                dst_ref=target.at[index],
                send_sem=sent.at[hop],
                recv_sem=received.at[hop],
                device_id={axis: peer},
                device_id_type=MESH,
            )
            copy.start()
            copies.append(copy)
        return copies

    nets = push("event", events, group, kept, arrived, sent_net, got_net, True)
    own_net = pltpu.make_async_copy(kept.at[group], arrived.at[group], local.at[2])
    own_net.start()
    lows = push("terrain", owners, me, kept_low, net_loss, sent_low, got_low, False)
    own_low = pltpu.make_async_copy(kept_low, net_loss.at[me], local.at[3])
    own_low.start()
    for copy in nets + [own_net]:
        copy.wait()
    total = arrived[0]
    for n in range(1, events):
        total = total + arrived[n]
    summed[...] = total / events
    last = pltpu.make_async_copy(summed, kept_sum, local.at[4])
    last.start()
    last.wait()
    sums = push("event", events, group, kept_sum, portfolio, sent_sum, got_sum, False)
    own_sum = pltpu.make_async_copy(kept_sum, portfolio.at[group], local.at[5])
    own_sum.start()
    for copy in sums + [own_sum] + lows + [own_low]:
        copy.wait()


def settle(parts, floor, roof, scale, number):
    owners, share_rows, bins = parts.shape
    events = lax.axis_size("event")
    split = (events, share_rows // events, bins)
    dma = pltpu.SemaphoreType.DMA
    return pl.pallas_call(
        functools.partial(settle_kernel, scale),
        out_shape=(
            jax.ShapeDtypeStruct((owners, share_rows, bins), jnp.bfloat16),
            jax.ShapeDtypeStruct(split, jnp.float32),
        ),
        in_specs=[VMEM] * 3,
        out_specs=(VMEM, VMEM),
        scratch_shapes=[
            pltpu.VMEM(split, jnp.float32),
            pltpu.VMEM((share_rows, bins), jnp.bfloat16),
            pltpu.VMEM(split, jnp.float32),
            pltpu.VMEM((share_rows, bins), jnp.bfloat16),
            pltpu.VMEM(split, jnp.float32),
            pltpu.VMEM(split[1:], jnp.float32),
            pltpu.VMEM(split[1:], jnp.float32),
            dma((6,)),
        ]
        + [dma((owners,))] * 2
        + [dma((events,))] * 4,
        compiler_params=pltpu.CompilerParams(collective_id=number, has_side_effects=True, vmem_limit_bytes=16*2**20),
        name="settle",
    )(parts, floor, roof)


def padded(count, unit):
    return -(-count // unit) * unit


def front_kernel(
    level_here, bed_here, wet_here, account, threshold, value, owner_row, weight, bias,
    level_out, ratio_out, low_out, bin_out, value_out,
    made, kept, got, level_above, bed_above, wet_above, level_below, bed_below, wet_below,
    halo_sent, halo_got, cell_sent, cell_got, local,
):
    size = lax.axis_size("terrain")
    me = lax.axis_index("terrain")
    barrier = pltpu.get_barrier_semaphore()
    for hop in range(1, size):
        pl.semaphore_signal(
            barrier, inc=1, device_id={"terrain": lax.rem(me + hop, size)}, device_id_type=MESH
        )
    rows, width = level_here.shape
    capacity = account.shape[0] // size
    room = made.shape[2]

    accounts = account[...]
    low = (accounts & 255) - ((accounts >> 8) & 1) * 256
    bound = threshold[...] - (accounts >> 9) * 256
    fields = (low.astype(jnp.float32), bound.astype(jnp.float32), value[...].astype(jnp.float32))
    if room != capacity:
        made[...] = jnp.zeros(made.shape, made.dtype)
    for n in range(size):
        for f in range(3):
            made[n, f, :capacity, :] = fields[f][n * capacity : (n + 1) * capacity].astype(
                made.dtype
            )
    keep = pltpu.make_async_copy(made, kept, local.at[0])
    keep.start()
    pl.semaphore_wait(barrier, size - 1)

    later, earlier = lax.rem(me + 1, size), lax.rem(me + size - 1, size)
    strips = (level_here, bed_here, wet_here)
    above = (level_above, bed_above, wet_above)
    below = (level_below, bed_below, wet_below)
    edges = []
    for side, (peer, targets) in enumerate(((later, above), (earlier, below))):
        for i in range(3):
            first = 0 if side else rows - SUBSTEPS
            copy = pltpu.make_async_remote_copy(
                src_ref=strips[i].at[pl.ds(first, SUBSTEPS)],
                dst_ref=targets[i],
                send_sem=halo_sent.at[side * 3 + i],
                recv_sem=halo_got.at[side * 3 + i],
                device_id={"terrain": peer},
                device_id_type=MESH,
            )
            copy.start()
            edges.append(copy)
    keep.wait()
    cells = []
    for hop in range(1, size):
        peer = lax.rem(me + hop, size)
        copy = pltpu.make_async_remote_copy(
            src_ref=kept.at[peer],
            dst_ref=got.at[me],
            send_sem=cell_sent.at[hop],
            recv_sem=cell_got.at[hop],
            device_id={"terrain": peer},
            device_id_type=MESH,
        )
        copy.start()
        cells.append(copy)
    own = pltpu.make_async_copy(kept.at[me], got.at[me], local.at[1])
    own.start()
    cells.append(own)

    tile = weight.shape[0]
    blocks = width // tile
    tiles = rows * blocks
    number = lax.broadcasted_iota(jnp.int32, (tiles, tiles), 0)
    number = (number % rows) * blocks + number // rows
    along = lax.broadcasted_iota(jnp.int32, (tiles, tiles), 1)
    owner = owner_row[...].astype(jnp.float32)
    owner_column = jnp.sum(jnp.where(along == number, owner, 0.0), axis=1, keepdims=True)
    same = (owner_column == owner) & (along < number)
    rank = jnp.sum(jnp.where(same, 1.0, 0.0), axis=1, keepdims=True)
    slot = lax.broadcasted_iota(jnp.int32, (tiles, size * room), 1).astype(jnp.float32)
    chosen = jnp.where(slot == owner_column * room + rank, 1.0, 0.0).astype(jnp.bfloat16)

    for copy in edges:
        copy.wait()
    first_row = me * rows - SUBSTEPS
    total_rows = rows * size
    level = jnp.concatenate([level_above[...], level_here[...], level_below[...]], axis=0)
    bed = jnp.concatenate([bed_above[...], bed_here[...], bed_below[...]], axis=0)
    wet = jnp.concatenate([wet_above[...], wet_here[...], wet_below[...]], axis=0)
    shape = level.shape
    tall = shape[0]
    row_id = first_row + lax.broadcasted_iota(jnp.int32, shape, 0)
    column = lax.broadcasted_iota(jnp.int32, shape, 1)
    inside = ((row_id >= 0) & (row_id < total_rows)).astype(jnp.float32)
    not_first = (column > 0).astype(jnp.float32)
    not_last = (column < width - 1).astype(jnp.float32)

    def down(field):
        return pltpu.roll(field, tall - 1, 0)

    def up(field):
        return pltpu.roll(field, 1, 0)

    def right(field):
        return pltpu.roll(field, width - 1, 1) * not_last

    def left(field):
        return pltpu.roll(field, 1, 1) * not_first

    quarter = 0.25
    assert courant * gravity == 0.5
    level = level * inside
    row_speed = jnp.zeros(shape, jnp.float32)
    col_speed = jnp.zeros(shape, jnp.float32)
    for step in range(SUBSTEPS):
        wet_factor = ((wet >> step) & 1).astype(jnp.float32) * (inside * quarter)
        if step:
            row_flow, col_flow = bed * row_speed, bed * col_speed
            new_level = (
                down(level - row_flow) + up(level + row_flow)
                + (right(level - col_flow) + left(level + col_flow))
            )
            new_row = (
                down(row_speed - level) + up(row_speed + level)
                + (right(row_speed) + left(row_speed))
            )
            new_col = (
                down(col_speed) + up(col_speed)
                + (right(col_speed - level) + left(col_speed + level))
            )
            row_speed, col_speed = new_row * wet_factor, new_col * wet_factor
        else:
            ld, lu, lr, ll = down(level), up(level), right(level), left(level)
            new_level = ld + lu + (lr + ll)
            row_speed = (lu - ld) * wet_factor
            col_speed = (ll - lr) * wet_factor
        level = new_level * (inside * quarter)
    level = level[SUBSTEPS : SUBSTEPS + rows]
    level_out[...] = level
    pieces = jnp.concatenate(
        [level[:, j * tile : (j + 1) * tile] for j in range(blocks)], axis=0
    ).astype(jnp.bfloat16)
    ratio_out[...] = jax.nn.sigmoid(
        jnp.dot(pieces, weight[...], preferred_element_type=jnp.float32) + bias[...]
    ).astype(jnp.bfloat16)
    for copy in cells:
        copy.wait()
    for f, target in enumerate((low_out, bin_out, value_out)):
        records = jnp.concatenate([got[n, f] for n in range(size)], axis=0)
        target[...] = jnp.dot(chosen, records, preferred_element_type=jnp.float32).astype(
            target.dtype
        )


def front(strips, records, owner_row, weight, bias, number):
    rows, width = strips[0].shape
    slots, cells = records[0].shape
    size = lax.axis_size("terrain")
    tiles = rows * width // cells
    packed = (size, 3, padded(slots // size, 16), cells)
    edge = (SUBSTEPS, width)
    dma = pltpu.SemaphoreType.DMA
    edges = [pltpu.VMEM(edge, f.dtype) for f in strips]
    return pl.pallas_call(
        front_kernel,
        out_shape=(
            jax.ShapeDtypeStruct((rows, width), jnp.float32),
            jax.ShapeDtypeStruct((tiles, weight.shape[1]), jnp.bfloat16),
        )
        + (jax.ShapeDtypeStruct((tiles, cells), jnp.bfloat16),) * 3,
        in_specs=[VMEM] * 9,
        out_specs=(VMEM,) * 5,
        scratch_shapes=[pltpu.VMEM(packed, jnp.bfloat16)] * 3
        + edges * 2
        + [dma((6,))] * 2
        + [dma((size,))] * 2
        + [dma((2,))],
        compiler_params=pltpu.CompilerParams(collective_id=number, has_side_effects=True, vmem_limit_bytes=16*2**20),
        name="front",
    )(*strips, *records, owner_row, weight, bias)


def rowed(row, height):
    packed = jnp.broadcast_to(row, (16, row.shape[1])).astype(jnp.bfloat16)
    return jnp.concatenate([packed] * (height // 16), axis=0)


def numbered(height, width, axis):
    return (
        lax.broadcasted_iota(jnp.int32, (height, width), axis)
        .astype(jnp.float32)
        .astype(jnp.bfloat16)
    )


def loss_kernel(
    low_in, bin_in, value_in, ratio_in, total,
    ratio_all, ratio, low_all, bound_all, value_all, places, lows, bounds, values,
):
    accounts, bins = total.shape
    tiles, cells = low_in.shape
    groups = lows.shape[0]
    group_size = accounts // groups
    capacity = 2 * cells // groups
    together = cells // capacity
    bundles = tiles // together
    zero = jnp.zeros((), jnp.bfloat16)
    one = jnp.ones((), jnp.bfloat16)

    low = low_in[...].astype(jnp.float32)
    bound = bin_in[...].astype(jnp.float32)
    high = jnp.where(low < 0, 256.0, 0.0) + jnp.where(bound < 0, 512.0, 0.0)
    low = jnp.where(low < 0, low + 256.0, low) + high
    group = low.astype(jnp.int32) // group_size
    low_all[...] = low - (group * group_size).astype(jnp.float32)
    bound_all[...] = jnp.where(bound < 0, bound + 256.0, bound)
    ratio_all[...] = ratio_in[...].astype(jnp.float32)
    value_all[...] = value_in[...].astype(jnp.float32)
    earlier = jnp.where(
        lax.broadcasted_iota(jnp.int32, (cells, cells), 0)
        < lax.broadcasted_iota(jnp.int32, (cells, cells), 1),
        1.0,
        0.0,
    ).astype(jnp.bfloat16)
    turn = lax.broadcasted_iota(jnp.int32, (tiles, cells), 0) % together
    rank = jnp.zeros((tiles, cells), jnp.float32)
    for h in range(groups):
        mine = group == h
        count = jnp.dot(
            jnp.where(mine, 1.0, 0.0).astype(jnp.bfloat16),
            earlier,
            preferred_element_type=jnp.float32,
        )
        rank = jnp.where(mine, count, rank)
    base = (group // together) * cells + ((group + turn) % together) * capacity
    fits = rank < capacity
    places[...] = jnp.where(fits, base.astype(jnp.float32) + rank, -1.0 - group.astype(jnp.float32))

    place_id = numbered(2 * cells, cells, 0)
    lane = lax.broadcasted_iota(jnp.int32, (8, cells), 1) // capacity
    field = lax.broadcasted_iota(jnp.int32, (8, cells), 0)
    unroll = max(1, UNROLL // together)

    def spread(ref, t):
        return jnp.broadcast_to(ref[pl.ds(t, 1), :], (8, cells))

    def gather(number, _):
        for u in range(unroll):
            bundle = number * unroll + u
            for j in range(together):
                t = bundle * together + j
                ratio[bundle, j] = jnp.broadcast_to(
                    ratio_all[pl.ds(t, 1), :], (16, bins)
                ).astype(jnp.bfloat16)
            found = []
            for j in range(together):
                t = bundle * together + j
                here = rowed(places[pl.ds(t, 1), :], 2 * cells) == place_id
                fields = jnp.where(
                    field == 0,
                    spread(low_all, t),
                    jnp.where(field == 1, spread(bound_all, t), spread(value_all, t)),
                )
                found.append(
                    lax.dot_general(
                        fields.astype(jnp.bfloat16),
                        jnp.where(here, one, zero),
                        (((1,), (1,)), ((), ())),
                        preferred_element_type=jnp.float32,
                    )
                )
            for q in range(2):
                parts = [f[:, q * cells : (q + 1) * cells] for f in found]
                for r in range(together):
                    mixed = parts[(0 - r) % together]
                    for e in range(1, together):
                        mixed = jnp.where(lane == e, parts[(e - r) % together], mixed)
                    h = q * together + r
                    lows[h, pl.ds(bundle, 1), :] = mixed[0:1]
                    bounds[h, pl.ds(bundle, 1), :] = mixed[1:2]
                    values[h, pl.ds(bundle, 1), :] = mixed[2:3]
        return 0

    lax.fori_loop(0, bundles // unroll, gather, 0)

    account_id = numbered(group_size, cells, 0)
    bin_id = jnp.concatenate([numbered(16, bins, 1)] * (cells // 16), axis=0)
    span = min(SPAN, bundles)

    def one_group(h, _):
        rows = pl.ds(pl.multiple_of(h * group_size, group_size), group_size)
        turned = [lax.rem(e + groups - h, together) for e in range(together)]
        summed = None
        for c in range(bundles // span):
            left, right = [], []
            for block in range(span // CHUNK):
                first = c * span + block * CHUNK
                columns = jnp.transpose(bounds[h, first : first + CHUNK, :]).astype(jnp.bfloat16)
                for i in range(CHUNK):
                    bundle = first + i
                    left.append(
                        jnp.where(
                            rowed(lows[h, bundle : bundle + 1, :], group_size) == account_id,
                            rowed(values[h, bundle : bundle + 1, :], group_size),
                            zero,
                        )
                    )
                    shown = []
                    for e in range(together):
                        row = ratio[bundle, turned[e]]
                        shown.extend([row] * (capacity // 16))
                    bound = jnp.broadcast_to(columns[:, i : i + 1], (cells, bins))
                    right.append(
                        jnp.where(bin_id >= bound, jnp.concatenate(shown, axis=0), zero)
                    )
            part = jnp.dot(
                jnp.concatenate(left, axis=1),
                jnp.concatenate(right, axis=0),
                preferred_element_type=jnp.float32,
            )
            summed = part if summed is None else summed + part
        total[rows, :] = summed
        return 0

    lax.fori_loop(0, groups, one_group, 0)

    spilled = jnp.max(rank) >= capacity

    @pl.when(spilled)
    def _():
        tile_id = lax.broadcasted_iota(jnp.int32, (tiles, cells), 0).astype(jnp.float32)

        def dense(left_over):
            t = left_over.astype(jnp.int32)
            place = places[pl.ds(t, 1), :]
            rest = jnp.where(place < 0, value_all[pl.ds(t, 1), :], 0.0)
            hit = rowed(low_all[pl.ds(t, 1), :], group_size) == account_id
            column = jnp.transpose(spread(bound_all, t)).astype(jnp.bfloat16)[:, 0:1]
            right = jnp.where(
                bin_id >= jnp.broadcast_to(column, (cells, bins)),
                rowed(ratio_all[pl.ds(t, 1), :], cells),
                zero,
            )
            for h in range(groups):
                part = jnp.where(place == -1.0 - h, rest, 0.0)
                left = jnp.where(hit, rowed(part, group_size), zero)
                total[pl.ds(h * group_size, group_size), :] += jnp.dot(
                    left, right, preferred_element_type=jnp.float32
                )
            return jnp.max(jnp.where((places[...] < 0) & (tile_id < left_over), tile_id, -1.0))

        lax.while_loop(
            lambda t: t >= 0, dense, jnp.max(jnp.where(places[...] < 0, tile_id, -1.0))
        )


def losses(low, bound, value, ratio, account_count):
    tiles, cells = low.shape
    bins = ratio.shape[1]
    groups = GROUPS
    together = groups // 2
    gathered = pltpu.VMEM((groups, tiles // together, cells), jnp.float32)
    whole = pltpu.VMEM((tiles, cells), jnp.float32)
    return pl.pallas_call(
        loss_kernel,
        out_shape=jax.ShapeDtypeStruct((account_count, bins), jnp.float32),
        in_specs=[VMEM] * 4,
        out_specs=VMEM,
        scratch_shapes=[
            pltpu.VMEM((tiles, bins), jnp.float32),
            pltpu.VMEM((tiles // together, together, 16, bins), jnp.bfloat16),
        ]
        + [whole] * 4
        + [gathered] * 3,
        compiler_params=pltpu.CompilerParams(vmem_limit_bytes=24*2**20), name="losses",
    )(low, bound, value, ratio)


def per_device(
    level_start,
    bed_depth,
    wet_bits,
    tile_owner,
    vuln_weight,
    vuln_bias,
    account_index,
    bin_index,
    exposure_value,
    deductible,
    limit,
):
    _, rows, width = level_start.shape
    tile_cells, bin_count = vuln_weight.shape
    account_count = deductible.shape[0]
    owners = lax.axis_size("terrain")
    events = lax.axis_size("event")
    share_rows = account_count // owners
    tiles = rows * width // tile_cells
    level, ratio, low, bound, value = front(
        [level_start[0], bed_depth, wet_bits[0]],
        [account_index, bin_index, exposure_value],
        tile_owner.reshape(1, tiles),
        vuln_weight,
        vuln_bias[None, :],
        1,
    )
    total = losses(low, bound, value, ratio, account_count)
    (parts,) = exchange(
        [total.reshape(owners, share_rows, bin_count)], [("terrain", False)], 2
    )
    scale = account_count / (rows * width * owners)
    net_loss, portfolio = settle(parts, deductible[None, :], limit[None, :], scale, 3)
    portfolio = portfolio.reshape(share_rows, bin_count)
    return (level[None], net_loss.reshape(1, account_count, bin_count), portfolio)


def solution(mesh):
    placed = (
        P("event", "terrain", None),
        P("terrain", None),
        P("event", "terrain", None),
        P("terrain", None),
        P(),
        P(),
        P("terrain", None),
        P("terrain", None),
        P("terrain", None),
        P(),
        P(),
    )
    return jax.shard_map(
        per_device,
        mesh=mesh,
        in_specs=placed,
        out_specs=(P("event", "terrain", None), P("event", None, None), P("terrain", None)),
        check_vma=False,
    )
```

```python
import functools

import jax
import jax.numpy as jnp
from jax import lax
from jax.experimental import pallas as pl
from jax.experimental.pallas import tpu as pltpu
from jax.sharding import PartitionSpec as P

SUBSTEPS = 8
CHUNK = 8
LIMIT = 24 * 2**20
GROUPS = 8
SPAN = 32
UNROLL = 16

courant = 0.5
gravity = 1.0

VMEM = pl.BlockSpec(memory_space=pltpu.VMEM)
HBM = pl.BlockSpec(memory_space=pltpu.HBM)
MESH = pl.DeviceIdType.MESH


def far(arrays):
    return [pltpu.with_memory_space_constraint(a, pltpu.HBM) for a in arrays]


def padded(count, unit):
    return -(-count // unit) * unit


def front_kernel(
    level_far, bed_far, wet_far, account_far, threshold_far, value_far, owner_far, weight_far, bias_far,
    level_out, ratio_out, low_out, bin_out, value_out,
    level_here, bed_here, wet_here, account, threshold, value, owner_row, weight, bias, loads,
    made, kept, got, level_above, bed_above, wet_above, level_below, bed_below, wet_below,
    halo_sent, halo_got, cell_sent, cell_got, local,
):
    size = lax.axis_size("terrain")
    me = lax.axis_index("terrain")
    barrier = pltpu.get_barrier_semaphore()
    for hop in range(1, size):
        pl.semaphore_signal(
            barrier, inc=1, device_id={"terrain": lax.rem(me + hop, size)}, device_id_type=MESH
        )
    moved = (
        (account_far, account), (threshold_far, threshold), (value_far, value),
        (owner_far, owner_row), (level_far, level_here), (bed_far, bed_here), (wet_far, wet_here),
        (weight_far, weight), (bias_far, bias),
    )
    reads = [
        pltpu.make_async_copy(far, near, loads.at[n]) for n, (far, near) in enumerate(moved)
    ]
    for copy in reads:
        copy.start()
    for copy in reads[:4]:
        copy.wait()
    rows, width = level_here.shape
    capacity = account.shape[0] // size
    room = made.shape[2]

    accounts = account[...]
    low = (accounts & 255) - ((accounts >> 8) & 1) * 256
    bound = threshold[...] - (accounts >> 9) * 256
    fields = (low.astype(jnp.float32), bound.astype(jnp.float32), value[...].astype(jnp.float32))
    if room != capacity:
        made[...] = jnp.zeros(made.shape, made.dtype)
    for n in range(size):
        for f in range(3):
            made[n, f, :capacity, :] = fields[f][n * capacity : (n + 1) * capacity].astype(
                made.dtype
            )
    keep = pltpu.make_async_copy(made, kept, local.at[0])
    keep.start()
    pl.semaphore_wait(barrier, size - 1)

    later, earlier = lax.rem(me + 1, size), lax.rem(me + size - 1, size)
    strips = (level_far, bed_far, wet_far)
    above = (level_above, bed_above, wet_above)
    below = (level_below, bed_below, wet_below)
    edges = []
    for side, (peer, targets) in enumerate(((later, above), (earlier, below))):
        for i in range(3):
            first = 0 if side else rows - SUBSTEPS
            copy = pltpu.make_async_remote_copy(
                src_ref=strips[i].at[pl.ds(first, SUBSTEPS)],
                dst_ref=targets[i],
                send_sem=halo_sent.at[side * 3 + i],
                recv_sem=halo_got.at[side * 3 + i],
                device_id={"terrain": peer},
                device_id_type=MESH,
            )
            copy.start()
            edges.append(copy)
    keep.wait()
    cells = []
    for hop in range(1, size):
        peer = lax.rem(me + hop, size)
        copy = pltpu.make_async_remote_copy(
            src_ref=kept.at[peer],
            dst_ref=got.at[me],
            send_sem=cell_sent.at[hop],
            recv_sem=cell_got.at[hop],
            device_id={"terrain": peer},
            device_id_type=MESH,
        )
        copy.start()
        cells.append(copy)
    own = pltpu.make_async_copy(kept.at[me], got.at[me], local.at[1])
    own.start()
    cells.append(own)

    tile = weight.shape[0]
    blocks = width // tile
    tiles = rows * blocks
    number = lax.broadcasted_iota(jnp.int32, (tiles, tiles), 0)
    number = (number % rows) * blocks + number // rows
    along = lax.broadcasted_iota(jnp.int32, (tiles, tiles), 1)
    owner = owner_row[...].astype(jnp.float32)
    owner_column = jnp.sum(jnp.where(along == number, owner, 0.0), axis=1, keepdims=True)
    same = (owner_column == owner) & (along < number)
    rank = jnp.sum(jnp.where(same, 1.0, 0.0), axis=1, keepdims=True)
    slot = lax.broadcasted_iota(jnp.int32, (tiles, size * room), 1).astype(jnp.float32)
    chosen = jnp.where(slot == owner_column * room + rank, 1.0, 0.0).astype(jnp.bfloat16)

    for copy in reads[4:] + edges:
        copy.wait()
    first_row = me * rows - SUBSTEPS
    total_rows = rows * size
    level = jnp.concatenate([level_above[...], level_here[...], level_below[...]], axis=0)
    bed = jnp.concatenate([bed_above[...], bed_here[...], bed_below[...]], axis=0)
    wet = jnp.concatenate([wet_above[...], wet_here[...], wet_below[...]], axis=0)
    shape = level.shape
    tall = shape[0]
    row_id = first_row + lax.broadcasted_iota(jnp.int32, shape, 0)
    column = lax.broadcasted_iota(jnp.int32, shape, 1)
    inside = ((row_id >= 0) & (row_id < total_rows)).astype(jnp.float32)
    not_first = (column > 0).astype(jnp.float32)
    not_last = (column < width - 1).astype(jnp.float32)

    def down(field):
        return pltpu.roll(field, tall - 1, 0)

    def up(field):
        return pltpu.roll(field, 1, 0)

    def right(field):
        return pltpu.roll(field, width - 1, 1) * not_last

    def left(field):
        return pltpu.roll(field, 1, 1) * not_first

    quarter = 0.25
    assert courant * gravity == 0.5
    level = level * inside
    row_speed = jnp.zeros(shape, jnp.float32)
    col_speed = jnp.zeros(shape, jnp.float32)
    for step in range(SUBSTEPS):
        wet_factor = ((wet >> step) & 1).astype(jnp.float32) * (inside * quarter)
        if step:
            row_flow, col_flow = bed * row_speed, bed * col_speed
            new_level = (
                down(level - row_flow) + up(level + row_flow)
                + (right(level - col_flow) + left(level + col_flow))
            )
            new_row = (
                down(row_speed - level) + up(row_speed + level)
                + (right(row_speed) + left(row_speed))
            )
            new_col = (
                down(col_speed) + up(col_speed)
                + (right(col_speed - level) + left(col_speed + level))
            )
            row_speed, col_speed = new_row * wet_factor, new_col * wet_factor
        else:
            ld, lu, lr, ll = down(level), up(level), right(level), left(level)
            new_level = ld + lu + (lr + ll)
            row_speed = (lu - ld) * wet_factor
            col_speed = (ll - lr) * wet_factor
        level = new_level * (inside * quarter)
    level = level[SUBSTEPS : SUBSTEPS + rows]
    level_out[...] = level
    pieces = jnp.concatenate(
        [level[:, j * tile : (j + 1) * tile] for j in range(blocks)], axis=0
    ).astype(jnp.bfloat16)
    ratio_out[...] = jax.nn.sigmoid(
        jnp.dot(pieces, weight[...], preferred_element_type=jnp.float32) + bias[...]
    ).astype(jnp.bfloat16)
    for copy in cells:
        copy.wait()
    for f, target in enumerate((low_out, bin_out, value_out)):
        records = jnp.concatenate([got[n, f] for n in range(size)], axis=0)
        target[...] = jnp.dot(chosen, records, preferred_element_type=jnp.float32).astype(
            target.dtype
        )


def front(strips, records, owner_row, weight, bias, number):
    rows, width = strips[0].shape
    slots, cells = records[0].shape
    size = lax.axis_size("terrain")
    tiles = rows * width // cells
    packed = (size, 3, padded(slots // size, 16), cells)
    edge = (SUBSTEPS, width)
    inputs = strips + records + [owner_row, weight, bias]
    dma = pltpu.SemaphoreType.DMA
    edges = [pltpu.VMEM(edge, f.dtype) for f in strips]
    return pl.pallas_call(
        front_kernel,
        out_shape=(
            jax.ShapeDtypeStruct((rows, width), jnp.float32),
            jax.ShapeDtypeStruct((tiles, weight.shape[1]), jnp.bfloat16),
        )
        + (jax.ShapeDtypeStruct((tiles, cells), jnp.bfloat16),) * 3,
        in_specs=[HBM] * 9,
        out_specs=(VMEM,) * 5,
        scratch_shapes=[pltpu.VMEM(a.shape, a.dtype) for a in inputs]
        + [dma((9,))]
        + [pltpu.VMEM(packed, jnp.bfloat16)] * 3
        + edges * 2
        + [dma((6,))] * 2
        + [dma((size,))] * 2
        + [dma((2,))],
        compiler_params=pltpu.CompilerParams(
            collective_id=number, has_side_effects=True, vmem_limit_bytes=LIMIT
        ),
        name="front",
    )(*far(inputs))


def rowed(row, height):
    packed = jnp.broadcast_to(row, (16, row.shape[1])).astype(jnp.bfloat16)
    return jnp.concatenate([packed] * (height // 16), axis=0)


def numbered(height, width, axis):
    return (
        lax.broadcasted_iota(jnp.int32, (height, width), axis)
        .astype(jnp.float32)
        .astype(jnp.bfloat16)
    )


def sort_kernel(
    low_in, bin_in, value_in, ratio_in, level_in,
    lows, bounds, values, ratio, total, level_out,
    ratio_all, low_all, bound_all, value_all, places,
):
    level_out[...] = level_in[...]
    total[...] = jnp.zeros(total.shape, jnp.float32)
    accounts, bins = total.shape
    tiles, cells = low_in.shape
    groups = lows.shape[0]
    group_size = accounts // groups
    capacity = 2 * cells // groups
    together = cells // capacity
    bundles = tiles // together
    zero = jnp.zeros((), jnp.bfloat16)
    one = jnp.ones((), jnp.bfloat16)

    low = low_in[...].astype(jnp.float32)
    bound = bin_in[...].astype(jnp.float32)
    high = jnp.where(low < 0, 256.0, 0.0) + jnp.where(bound < 0, 512.0, 0.0)
    low = jnp.where(low < 0, low + 256.0, low) + high
    group = low.astype(jnp.int32) // group_size
    low_all[...] = low - (group * group_size).astype(jnp.float32)
    bound_all[...] = jnp.where(bound < 0, bound + 256.0, bound)
    ratio_all[...] = ratio_in[...].astype(jnp.float32)
    value_all[...] = value_in[...].astype(jnp.float32)
    earlier = jnp.where(
        lax.broadcasted_iota(jnp.int32, (cells, cells), 0)
        < lax.broadcasted_iota(jnp.int32, (cells, cells), 1),
        1.0,
        0.0,
    ).astype(jnp.bfloat16)
    turn = lax.broadcasted_iota(jnp.int32, (tiles, cells), 0) % together
    rank = jnp.zeros((tiles, cells), jnp.float32)
    for h in range(groups):
        mine = group == h
        count = jnp.dot(
            jnp.where(mine, 1.0, 0.0).astype(jnp.bfloat16),
            earlier,
            preferred_element_type=jnp.float32,
        )
        rank = jnp.where(mine, count, rank)
    base = (group // together) * cells + ((group + turn) % together) * capacity
    fits = rank < capacity
    places[...] = jnp.where(fits, base.astype(jnp.float32) + rank, -1.0 - group.astype(jnp.float32))

    place_id = numbered(2 * cells, cells, 0)
    lane = lax.broadcasted_iota(jnp.int32, (8, cells), 1) // capacity
    field = lax.broadcasted_iota(jnp.int32, (8, cells), 0)
    unroll = max(1, UNROLL // together)

    def spread(ref, t):
        return jnp.broadcast_to(ref[pl.ds(t, 1), :], (8, cells))

    def gather(number, _):
        for u in range(unroll):
            bundle = number * unroll + u
            for j in range(together):
                t = bundle * together + j
                ratio[bundle, j] = jnp.broadcast_to(
                    ratio_all[pl.ds(t, 1), :], (16, bins)
                ).astype(jnp.bfloat16)
            found = []
            for j in range(together):
                t = bundle * together + j
                here = rowed(places[pl.ds(t, 1), :], 2 * cells) == place_id
                fields = jnp.where(
                    field == 0,
                    spread(low_all, t),
                    jnp.where(field == 1, spread(bound_all, t), spread(value_all, t)),
                )
                found.append(
                    lax.dot_general(
                        fields.astype(jnp.bfloat16),
                        jnp.where(here, one, zero),
                        (((1,), (1,)), ((), ())),
                        preferred_element_type=jnp.float32,
                    )
                )
            for q in range(2):
                parts = [f[:, q * cells : (q + 1) * cells] for f in found]
                for r in range(together):
                    mixed = parts[(0 - r) % together]
                    for e in range(1, together):
                        mixed = jnp.where(lane == e, parts[(e - r) % together], mixed)
                    h = q * together + r
                    lows[h, pl.ds(bundle, 1), :] = mixed[0:1]
                    bounds[h, pl.ds(bundle, 1), :] = mixed[1:2]
                    values[h, pl.ds(bundle, 1), :] = mixed[2:3]
        return 0

    lax.fori_loop(0, bundles // unroll, gather, 0)

    spilled = jnp.max(rank) >= capacity

    @pl.when(spilled)
    def _():
        account_id = numbered(group_size, cells, 0)
        bin_id = jnp.concatenate([numbered(16, bins, 1)] * (cells // 16), axis=0)
        tile_id = lax.broadcasted_iota(jnp.int32, (tiles, cells), 0).astype(jnp.float32)

        def dense(left_over):
            t = left_over.astype(jnp.int32)
            place = places[pl.ds(t, 1), :]
            rest = jnp.where(place < 0, value_all[pl.ds(t, 1), :], 0.0)
            hit = rowed(low_all[pl.ds(t, 1), :], group_size) == account_id
            column = jnp.transpose(spread(bound_all, t)).astype(jnp.bfloat16)[:, 0:1]
            right = jnp.where(
                bin_id >= jnp.broadcast_to(column, (cells, bins)),
                rowed(ratio_all[pl.ds(t, 1), :], cells),
                zero,
            )
            for h in range(groups):
                part = jnp.where(place == -1.0 - h, rest, 0.0)
                left = jnp.where(hit, rowed(part, group_size), zero)
                total[pl.ds(h * group_size, group_size), :] += jnp.dot(
                    left, right, preferred_element_type=jnp.float32
                )
            return jnp.max(jnp.where((places[...] < 0) & (tile_id < left_over), tile_id, -1.0))

        lax.while_loop(
            lambda t: t >= 0, dense, jnp.max(jnp.where(places[...] < 0, tile_id, -1.0))
        )


def sort(low, bound, value, ratio, level, account_count):
    tiles, cells = low.shape
    bins = ratio.shape[1]
    together = GROUPS // 2
    bundles = tiles // together
    gathered = jax.ShapeDtypeStruct((GROUPS, bundles, cells), jnp.float32)
    whole = pltpu.VMEM((tiles, cells), jnp.float32)
    return pl.pallas_call(
        sort_kernel,
        out_shape=(
            gathered,
            gathered,
            gathered,
            jax.ShapeDtypeStruct((bundles, together, 16, bins), jnp.bfloat16),
            jax.ShapeDtypeStruct((account_count, bins), jnp.float32),
            jax.ShapeDtypeStruct(level.shape, level.dtype),
        ),
        in_specs=[VMEM] * 5,
        out_specs=(VMEM,) * 6,
        scratch_shapes=[pltpu.VMEM((tiles, bins), jnp.float32)] + [whole] * 4,
        compiler_params=pltpu.CompilerParams(vmem_limit_bytes=LIMIT),
        name="sort",
    )(low, bound, value, ratio, level)


def settle_kernel(
    scale, lows, bounds, values, ratio, spill, floor_far, roof_far,
    net_loss, portfolio,
    floor, roof, total, parts, made, made_low, arrived, summed,
    sent_part, got_part, sent_low, got_low, sent_more, got_more,
    sent_net, got_net, sent_sum, got_sum, local,
):
    accounts, bins = total.shape
    owners, share_rows, _ = parts.shape
    groups, bundles, cells = lows.shape
    group_size = accounts // groups
    capacity = 2 * cells // groups
    together = cells // capacity
    members = owners // groups
    zero = jnp.zeros((), jnp.bfloat16)
    events = lax.axis_size("event")
    me, group = lax.axis_index("terrain"), lax.axis_index("event")
    terms = [
        pltpu.make_async_copy(floor_far, floor, local.at[3]),
        pltpu.make_async_copy(roof_far, roof, local.at[4]),
    ]
    for copy in terms:
        copy.start()
    barrier = pltpu.get_barrier_semaphore()
    for axis, size, mine in (("terrain", owners, me), ("event", events, group)):
        for hop in range(1, size):
            pl.semaphore_signal(
                barrier, inc=1, device_id={axis: lax.rem(mine + hop, size)}, device_id_type=MESH
            )
    pl.semaphore_wait(barrier, owners + events - 2)

    def give(owner):
        hop = lax.rem(owner - me + owners, owners)
        return pltpu.make_async_remote_copy(
            src_ref=total.at[pl.ds(pl.multiple_of(owner * share_rows, share_rows), share_rows)],
            dst_ref=parts.at[me],
            send_sem=sent_part.at[hop],
            recv_sem=got_part.at[hop],
            device_id={"terrain": owner},
            device_id_type=MESH,
        )

    account_id = numbered(group_size, cells, 0)
    bin_id = jnp.concatenate([numbered(16, bins, 1)] * (cells // 16), axis=0)
    span = min(SPAN, bundles)

    def one_group(number, _):
        h = lax.rem(me // members + 1 + number, groups)
        rows = pl.ds(pl.multiple_of(h * group_size, group_size), group_size)
        turned = [lax.rem(e + groups - h, together) for e in range(together)]
        summed = None
        for c in range(bundles // span):
            if c == bundles // span // 2:

                @pl.when(number > 0)
                def _():
                    for j in range(members):
                        give(lax.rem(h + groups - 1, groups) * members + j).start()

            left, right = [], []
            for block in range(span // CHUNK):
                first = c * span + block * CHUNK
                columns = jnp.transpose(bounds[h, first : first + CHUNK, :]).astype(jnp.bfloat16)
                for i in range(CHUNK):
                    bundle = first + i
                    left.append(
                        jnp.where(
                            rowed(lows[h, bundle : bundle + 1, :], group_size) == account_id,
                            rowed(values[h, bundle : bundle + 1, :], group_size),
                            zero,
                        )
                    )
                    shown = []
                    for e in range(together):
                        row = ratio[bundle, turned[e]]
                        shown.extend([row] * (capacity // 16))
                    bound = jnp.broadcast_to(columns[:, i : i + 1], (cells, bins))
                    right.append(
                        jnp.where(bin_id >= bound, jnp.concatenate(shown, axis=0), zero)
                    )
            part = jnp.dot(
                jnp.concatenate(left, axis=1),
                jnp.concatenate(right, axis=0),
                preferred_element_type=jnp.float32,
            )
            summed = part if summed is None else summed + part
        total[rows, :] = spill[rows, :] + summed
        return 0

    lax.fori_loop(0, groups, one_group, 0)
    for j in range(1, members):
        give(me // members * members + lax.rem(me + j, members)).start()

    own = pl.ds(pl.multiple_of(me * share_rows, share_rows), share_rows)
    picked = (share_rows, accounts)
    account = lax.broadcasted_iota(jnp.int32, picked, 1)
    mine = account == lax.broadcasted_iota(jnp.int32, picked, 0) + me * share_rows

    def of_share(terms):
        return jnp.sum(jnp.where(mine, terms[...], 0.0), axis=1, keepdims=True)

    for copy in terms:
        copy.wait()
    least, most = of_share(floor), of_share(roof)
    whole = total[own, :]
    for hop in range(1, owners):
        give(lax.rem(me + hop, owners)).wait()
        whole = whole + parts[lax.rem(me + owners - hop, owners)]
    net = jnp.minimum(jnp.maximum(whole * scale - least, 0.0), most)
    made[...] = net.reshape(made.shape)
    made_low[...] = net.astype(made_low.dtype)

    def push(axis, peer, source, target, sent, received):
        copy = pltpu.make_async_remote_copy(
            src_ref=source,
            dst_ref=target,
            send_sem=sent,
            recv_sem=received,
            device_id={axis: peer},
            device_id_type=MESH,
        )
        copy.start()
        return copy

    nets, sums = [], []
    for hop in range(1, events):
        peer = lax.rem(group + hop, events)
        nets.append(
            push("event", peer, made.at[peer], arrived.at[group], sent_net.at[hop], got_net.at[hop])
        )
    chips = owners // 2
    partner = me + 1 - 2 * lax.rem(me, 2)
    lows_sent = []
    for k in range(1, chips):
        peer = lax.rem(me + 2 * k, owners)
        lows_sent.append(
            push("terrain", peer, made_low, net_loss.at[me], sent_low.at[k], got_low.at[k])
        )
    beside = [
        push("terrain", partner, made_low, net_loss.at[me], sent_more.at[0], got_more.at[0])
    ]
    kept = [
        pltpu.make_async_copy(made_low, net_loss.at[me], local.at[0]),
        pltpu.make_async_copy(made.at[group], arrived.at[group], local.at[1]),
    ]
    for copy in kept:
        copy.start()
    kept[1].wait()
    for copy in nets:
        copy.wait()
    whole = arrived[0]
    for n in range(1, events):
        whole = whole + arrived[n]
    summed[...] = whole / events
    for hop in range(1, events):
        peer = lax.rem(group + hop, events)
        sums.append(
            push("event", peer, summed, portfolio.at[group], sent_sum.at[hop], got_sum.at[hop])
        )
    last = pltpu.make_async_copy(summed, portfolio.at[group], local.at[2])
    last.start()
    for k in range(1, chips):
        lows_sent[k - 1].wait()
        source = lax.rem(me + owners - 2 * k, owners)
        beside.append(
            push(
                "terrain", partner, net_loss.at[source], net_loss.at[source],
                sent_more.at[k], got_more.at[k],
            )
        )
    for copy in sums + beside + [kept[0], last]:
        copy.wait()


def settle(lows, bounds, values, ratio, spill, floor, roof, scale, number):
    account_count, bins = spill.shape
    owners, events = lax.axis_size("terrain"), lax.axis_size("event")
    share_rows = account_count // owners
    split = (events, share_rows // events, bins)
    dma = pltpu.SemaphoreType.DMA
    return pl.pallas_call(
        functools.partial(settle_kernel, scale),
        out_shape=(
            jax.ShapeDtypeStruct((owners, share_rows, bins), jnp.bfloat16),
            jax.ShapeDtypeStruct(split, jnp.float32),
        ),
        in_specs=[VMEM] * 5 + [HBM] * 2,
        out_specs=(VMEM, VMEM),
        scratch_shapes=[pltpu.VMEM(floor.shape, floor.dtype)] * 2
        + [
            pltpu.VMEM((account_count, bins), jnp.float32),
            pltpu.VMEM((owners, share_rows, bins), jnp.float32),
            pltpu.VMEM(split, jnp.float32),
            pltpu.VMEM((share_rows, bins), jnp.bfloat16),
            pltpu.VMEM(split, jnp.float32),
            pltpu.VMEM(split[1:], jnp.float32),
        ]
        + [dma((owners,))] * 2
        + [dma((owners // 2,))] * 4
        + [dma((events,))] * 4
        + [dma((5,))],
        compiler_params=pltpu.CompilerParams(
            collective_id=number, has_side_effects=True, vmem_limit_bytes=LIMIT
        ),
        name="settle",
    )(lows, bounds, values, ratio, spill, *far([floor, roof]))


def per_device(
    level_start,
    bed_depth,
    wet_bits,
    tile_owner,
    vuln_weight,
    vuln_bias,
    account_index,
    bin_index,
    exposure_value,
    deductible,
    limit,
):
    _, rows, width = level_start.shape
    tile_cells, bin_count = vuln_weight.shape
    account_count = deductible.shape[0]
    owners = lax.axis_size("terrain")
    events = lax.axis_size("event")
    share_rows = account_count // owners
    tiles = rows * width // tile_cells
    level, ratio, low, bound, value = front(
        [level_start[0], bed_depth, wet_bits[0]],
        [account_index, bin_index, exposure_value],
        tile_owner.reshape(1, tiles),
        vuln_weight,
        vuln_bias[None, :],
        1,
    )
    scale = account_count / (rows * width * owners)
    *sorted_cells, level = sort(low, bound, value, ratio, level, account_count)
    net_loss, portfolio = settle(
        *sorted_cells, deductible[None, :], limit[None, :], scale, 2
    )
    portfolio = portfolio.reshape(share_rows, bin_count)
    return (level[None], net_loss.reshape(1, account_count, bin_count), portfolio)


def solution(mesh):
    placed = (
        P("event", "terrain", None),
        P("terrain", None),
        P("event", "terrain", None),
        P("terrain", None),
        P(),
        P(),
        P("terrain", None),
        P("terrain", None),
        P("terrain", None),
        P(),
        P(),
    )
    return jax.shard_map(
        per_device,
        mesh=mesh,
        in_specs=placed,
        out_specs=(P("event", "terrain", None), P("event", None, None), P("terrain", None)),
        check_vma=False,
    )
```

```python
import functools

import jax
import jax.numpy as jnp
from jax import lax
from jax.experimental import pallas as pl
from jax.experimental.pallas import tpu as pltpu
from jax.sharding import PartitionSpec as P

SUBSTEPS = 8
CHUNK = 8
LAG = 2
LIMIT = 24 * 2**20
GROUPS = 8
SPAN = 32
UNROLL = 16

courant = 0.5
gravity = 1.0

VMEM = pl.BlockSpec(memory_space=pltpu.VMEM)
HBM = pl.BlockSpec(memory_space=pltpu.HBM)
MESH = pl.DeviceIdType.MESH


def far(arrays):
    return [pltpu.with_memory_space_constraint(a, pltpu.HBM) for a in arrays]


def padded(count, unit):
    return -(-count // unit) * unit


def front_kernel(
    level_far, bed_far, wet_far, account_far, threshold_far, value_far, owner_far, weight_far, bias_far,
    level_out, ratio_out, low_out, bin_out, value_out,
    level_here, bed_here, wet_here, account, threshold, value, owner_row, weight, bias, loads,
    made, kept, got, level_above, bed_above, wet_above, level_below, bed_below, wet_below,
    halo_sent, halo_got, cell_sent, cell_got, local,
):
    size = lax.axis_size("terrain")
    me = lax.axis_index("terrain")
    barrier = pltpu.get_barrier_semaphore()
    for hop in range(1, size):
        pl.semaphore_signal(
            barrier, inc=1, device_id={"terrain": lax.rem(me + hop, size)}, device_id_type=MESH
        )
    moved = (
        (account_far, account), (threshold_far, threshold), (value_far, value),
        (owner_far, owner_row), (level_far, level_here), (bed_far, bed_here), (wet_far, wet_here),
        (weight_far, weight), (bias_far, bias),
    )
    reads = [
        pltpu.make_async_copy(far, near, loads.at[n]) for n, (far, near) in enumerate(moved)
    ]
    for copy in reads:
        copy.start()
    for copy in reads[:4]:
        copy.wait()
    rows, width = level_here.shape
    capacity = account.shape[0] // size
    room = made.shape[2]

    accounts = account[...]
    low = (accounts & 255) - ((accounts >> 8) & 1) * 256
    bound = threshold[...] - (accounts >> 9) * 256
    fields = (low.astype(jnp.float32), bound.astype(jnp.float32), value[...].astype(jnp.float32))
    if room != capacity:
        made[...] = jnp.zeros(made.shape, made.dtype)
    for n in range(size):
        for f in range(3):
            made[n, f, :capacity, :] = fields[f][n * capacity : (n + 1) * capacity].astype(
                made.dtype
            )
    keep = pltpu.make_async_copy(made, kept, local.at[0])
    keep.start()
    pl.semaphore_wait(barrier, size - 1)

    later, earlier = lax.rem(me + 1, size), lax.rem(me + size - 1, size)
    strips = (level_far, bed_far, wet_far)
    above = (level_above, bed_above, wet_above)
    below = (level_below, bed_below, wet_below)
    edges = []
    for side, (peer, targets) in enumerate(((later, above), (earlier, below))):
        for i in range(3):
            first = 0 if side else rows - SUBSTEPS
            copy = pltpu.make_async_remote_copy(
                src_ref=strips[i].at[pl.ds(first, SUBSTEPS)],
                dst_ref=targets[i],
                send_sem=halo_sent.at[side * 3 + i],
                recv_sem=halo_got.at[side * 3 + i],
                device_id={"terrain": peer},
                device_id_type=MESH,
            )
            copy.start()
            edges.append(copy)
    keep.wait()
    cells = []
    for hop in range(1, size):
        peer = lax.rem(me + hop, size)
        copy = pltpu.make_async_remote_copy(
            src_ref=kept.at[peer],
            dst_ref=got.at[me],
            send_sem=cell_sent.at[hop],
            recv_sem=cell_got.at[hop],
            device_id={"terrain": peer},
            device_id_type=MESH,
        )
        copy.start()
        cells.append(copy)
    own = pltpu.make_async_copy(kept.at[me], got.at[me], local.at[1])
    own.start()
    cells.append(own)

    tile = weight.shape[0]
    blocks = width // tile
    tiles = rows * blocks
    number = lax.broadcasted_iota(jnp.int32, (tiles, tiles), 0)
    number = (number % rows) * blocks + number // rows
    along = lax.broadcasted_iota(jnp.int32, (tiles, tiles), 1)
    owner = owner_row[...].astype(jnp.float32)
    owner_column = jnp.sum(jnp.where(along == number, owner, 0.0), axis=1, keepdims=True)
    same = (owner_column == owner) & (along < number)
    rank = jnp.sum(jnp.where(same, 1.0, 0.0), axis=1, keepdims=True)
    slot = lax.broadcasted_iota(jnp.int32, (tiles, size * room), 1).astype(jnp.float32)
    chosen = jnp.where(slot == owner_column * room + rank, 1.0, 0.0).astype(jnp.bfloat16)

    for copy in reads[4:] + edges:
        copy.wait()
    first_row = me * rows - SUBSTEPS
    total_rows = rows * size
    level = jnp.concatenate([level_above[...], level_here[...], level_below[...]], axis=0)
    bed = jnp.concatenate([bed_above[...], bed_here[...], bed_below[...]], axis=0)
    wet = jnp.concatenate([wet_above[...], wet_here[...], wet_below[...]], axis=0)
    shape = level.shape
    tall = shape[0]
    row_id = first_row + lax.broadcasted_iota(jnp.int32, shape, 0)
    column = lax.broadcasted_iota(jnp.int32, shape, 1)
    inside = ((row_id >= 0) & (row_id < total_rows)).astype(jnp.float32)
    not_first = (column > 0).astype(jnp.float32)
    not_last = (column < width - 1).astype(jnp.float32)

    def down(field):
        return pltpu.roll(field, tall - 1, 0)

    def up(field):
        return pltpu.roll(field, 1, 0)

    def right(field):
        return pltpu.roll(field, width - 1, 1) * not_last

    def left(field):
        return pltpu.roll(field, 1, 1) * not_first

    quarter = 0.25
    assert courant * gravity == 0.5
    level = level * inside
    row_speed = jnp.zeros(shape, jnp.float32)
    col_speed = jnp.zeros(shape, jnp.float32)
    for step in range(SUBSTEPS):
        wet_factor = ((wet >> step) & 1).astype(jnp.float32) * (inside * quarter)
        if step:
            row_flow, col_flow = bed * row_speed, bed * col_speed
            new_level = (
                down(level - row_flow) + up(level + row_flow)
                + (right(level - col_flow) + left(level + col_flow))
            )
            new_row = (
                down(row_speed - level) + up(row_speed + level)
                + (right(row_speed) + left(row_speed))
            )
            new_col = (
                down(col_speed) + up(col_speed)
                + (right(col_speed - level) + left(col_speed + level))
            )
            row_speed, col_speed = new_row * wet_factor, new_col * wet_factor
        else:
            ld, lu, lr, ll = down(level), up(level), right(level), left(level)
            new_level = ld + lu + (lr + ll)
            row_speed = (lu - ld) * wet_factor
            col_speed = (ll - lr) * wet_factor
        level = new_level * (inside * quarter)
    level = level[SUBSTEPS : SUBSTEPS + rows]
    level_out[...] = level
    pieces = jnp.concatenate(
        [level[:, j * tile : (j + 1) * tile] for j in range(blocks)], axis=0
    ).astype(jnp.bfloat16)
    ratio_out[...] = jax.nn.sigmoid(
        jnp.dot(pieces, weight[...], preferred_element_type=jnp.float32) + bias[...]
    ).astype(jnp.bfloat16)
    for copy in cells:
        copy.wait()
    for f, target in enumerate((low_out, bin_out, value_out)):
        records = jnp.concatenate([got[n, f] for n in range(size)], axis=0)
        target[...] = jnp.dot(chosen, records, preferred_element_type=jnp.float32).astype(
            target.dtype
        )


def front(strips, records, owner_row, weight, bias, number):
    rows, width = strips[0].shape
    slots, cells = records[0].shape
    size = lax.axis_size("terrain")
    tiles = rows * width // cells
    packed = (size, 3, padded(slots // size, 16), cells)
    edge = (SUBSTEPS, width)
    inputs = strips + records + [owner_row, weight, bias]
    dma = pltpu.SemaphoreType.DMA
    edges = [pltpu.VMEM(edge, f.dtype) for f in strips]
    return pl.pallas_call(
        front_kernel,
        out_shape=(
            jax.ShapeDtypeStruct((rows, width), jnp.float32),
            jax.ShapeDtypeStruct((tiles, weight.shape[1]), jnp.bfloat16),
        )
        + (jax.ShapeDtypeStruct((tiles, cells), jnp.bfloat16),) * 3,
        in_specs=[HBM] * 9,
        out_specs=(VMEM,) * 5,
        scratch_shapes=[pltpu.VMEM(a.shape, a.dtype) for a in inputs]
        + [dma((9,))]
        + [pltpu.VMEM(packed, jnp.bfloat16)] * 3
        + edges * 2
        + [dma((6,))] * 2
        + [dma((size,))] * 2
        + [dma((2,))],
        compiler_params=pltpu.CompilerParams(
            collective_id=number, has_side_effects=True, vmem_limit_bytes=LIMIT
        ),
        name="front",
    )(*far(inputs))


def rowed(row, height):
    packed = jnp.broadcast_to(row, (16, row.shape[1])).astype(jnp.bfloat16)
    return jnp.concatenate([packed] * (height // 16), axis=0)


def numbered(height, width, axis):
    return (
        lax.broadcasted_iota(jnp.int32, (height, width), axis)
        .astype(jnp.float32)
        .astype(jnp.bfloat16)
    )


def sort_kernel(
    owners, low_in, bin_in, value_in, ratio_in, level_in,
    lows, bounds, values, ratio, total, level_out,
    ratio_all, low_all, bound_all, value_all, places,
):
    level_out[...] = level_in[...]
    total[...] = jnp.zeros(total.shape, jnp.float32)
    accounts, bins = total.shape
    tiles, cells = low_in.shape
    groups = lows.shape[0]
    group_size = accounts // groups
    capacity = 2 * cells // groups
    together = cells // capacity
    bundles = tiles // together
    zero = jnp.zeros((), jnp.bfloat16)
    one = jnp.ones((), jnp.bfloat16)

    low = low_in[...].astype(jnp.float32)
    bound = bin_in[...].astype(jnp.float32)
    high = jnp.where(low < 0, 256.0, 0.0) + jnp.where(bound < 0, 512.0, 0.0)
    low = jnp.where(low < 0, low + 256.0, low) + high
    account = low.astype(jnp.int32)
    share = accounts // owners
    rows = share // groups
    group = account % share // rows
    low_all[...] = (account // share * rows + account % rows).astype(jnp.float32)
    bound_all[...] = jnp.where(bound < 0, bound + 256.0, bound)
    ratio_all[...] = ratio_in[...].astype(jnp.float32)
    value_all[...] = value_in[...].astype(jnp.float32)
    earlier = jnp.where(
        lax.broadcasted_iota(jnp.int32, (cells, cells), 0)
        < lax.broadcasted_iota(jnp.int32, (cells, cells), 1),
        1.0,
        0.0,
    ).astype(jnp.bfloat16)
    turn = lax.broadcasted_iota(jnp.int32, (tiles, cells), 0) % together
    rank = jnp.zeros((tiles, cells), jnp.float32)
    for h in range(groups):
        mine = group == h
        count = jnp.dot(
            jnp.where(mine, 1.0, 0.0).astype(jnp.bfloat16),
            earlier,
            preferred_element_type=jnp.float32,
        )
        rank = jnp.where(mine, count, rank)
    base = (group // together) * cells + ((group + turn) % together) * capacity
    fits = rank < capacity
    places[...] = jnp.where(fits, base.astype(jnp.float32) + rank, -1.0 - group.astype(jnp.float32))

    place_id = numbered(2 * cells, cells, 0)
    lane = lax.broadcasted_iota(jnp.int32, (8, cells), 1) // capacity
    field = lax.broadcasted_iota(jnp.int32, (8, cells), 0)
    unroll = max(1, UNROLL // together)

    def spread(ref, t):
        return jnp.broadcast_to(ref[pl.ds(t, 1), :], (8, cells))

    def gather(number, _):
        for u in range(unroll):
            bundle = number * unroll + u
            for j in range(together):
                t = bundle * together + j
                ratio[bundle, j] = jnp.broadcast_to(
                    ratio_all[pl.ds(t, 1), :], (16, bins)
                ).astype(jnp.bfloat16)
            found = []
            for j in range(together):
                t = bundle * together + j
                here = rowed(places[pl.ds(t, 1), :], 2 * cells) == place_id
                fields = jnp.where(
                    field == 0,
                    spread(low_all, t),
                    jnp.where(field == 1, spread(bound_all, t), spread(value_all, t)),
                )
                found.append(
                    lax.dot_general(
                        fields.astype(jnp.bfloat16),
                        jnp.where(here, one, zero),
                        (((1,), (1,)), ((), ())),
                        preferred_element_type=jnp.float32,
                    )
                )
            for q in range(2):
                parts = [f[:, q * cells : (q + 1) * cells] for f in found]
                for r in range(together):
                    mixed = parts[(0 - r) % together]
                    for e in range(1, together):
                        mixed = jnp.where(lane == e, parts[(e - r) % together], mixed)
                    h = q * together + r
                    lows[h, pl.ds(bundle, 1), :] = mixed[0:1]
                    bounds[h, pl.ds(bundle, 1), :] = mixed[1:2]
                    values[h, pl.ds(bundle, 1), :] = mixed[2:3]
        return 0

    lax.fori_loop(0, bundles // unroll, gather, 0)

    spilled = jnp.max(rank) >= capacity

    @pl.when(spilled)
    def _():
        account_id = numbered(group_size, cells, 0)
        bin_id = jnp.concatenate([numbered(16, bins, 1)] * (cells // 16), axis=0)
        tile_id = lax.broadcasted_iota(jnp.int32, (tiles, cells), 0).astype(jnp.float32)

        def dense(left_over):
            t = left_over.astype(jnp.int32)
            place = places[pl.ds(t, 1), :]
            rest = jnp.where(place < 0, value_all[pl.ds(t, 1), :], 0.0)
            hit = rowed(low_all[pl.ds(t, 1), :], group_size) == account_id
            column = jnp.transpose(spread(bound_all, t)).astype(jnp.bfloat16)[:, 0:1]
            right = jnp.where(
                bin_id >= jnp.broadcast_to(column, (cells, bins)),
                rowed(ratio_all[pl.ds(t, 1), :], cells),
                zero,
            )
            for h in range(groups):
                part = jnp.where(place == -1.0 - h, rest, 0.0)
                left = jnp.where(hit, rowed(part, group_size), zero)
                total[pl.ds(h * group_size, group_size), :] += jnp.dot(
                    left, right, preferred_element_type=jnp.float32
                )
            return jnp.max(jnp.where((places[...] < 0) & (tile_id < left_over), tile_id, -1.0))

        lax.while_loop(
            lambda t: t >= 0, dense, jnp.max(jnp.where(places[...] < 0, tile_id, -1.0))
        )


def sort(low, bound, value, ratio, level, account_count):
    tiles, cells = low.shape
    bins = ratio.shape[1]
    together = GROUPS // 2
    bundles = tiles // together
    gathered = jax.ShapeDtypeStruct((GROUPS, bundles, cells), jnp.float32)
    whole = pltpu.VMEM((tiles, cells), jnp.float32)
    return pl.pallas_call(
        functools.partial(sort_kernel, lax.axis_size("terrain")),
        out_shape=(
            gathered,
            gathered,
            gathered,
            jax.ShapeDtypeStruct((bundles, together, 16, bins), jnp.bfloat16),
            jax.ShapeDtypeStruct((account_count, bins), jnp.float32),
            jax.ShapeDtypeStruct(level.shape, level.dtype),
        ),
        in_specs=[VMEM] * 5,
        out_specs=(VMEM,) * 6,
        scratch_shapes=[pltpu.VMEM((tiles, bins), jnp.float32)] + [whole] * 4,
        compiler_params=pltpu.CompilerParams(vmem_limit_bytes=LIMIT),
        name="sort",
    )(low, bound, value, ratio, level)


def settle_kernel(
    scale, lows, bounds, values, ratio, spill, floor_far, roof_far,
    net_loss, portfolio,
    floor, roof, least, most, total, parts, made, made_low, arrived,
    sent_part, got_part, sent_low, got_low, sent_net, got_net, local,
):
    groups, owners, share_rows, bins = total.shape
    _, bundles, cells = lows.shape
    group_size = owners * share_rows
    capacity = 2 * cells // groups
    together = cells // capacity
    zero = jnp.zeros((), jnp.bfloat16)
    events = lax.axis_size("event")
    me, group = lax.axis_index("terrain"), lax.axis_index("event")
    terms = [
        pltpu.make_async_copy(floor_far, floor, local.at[0]),
        pltpu.make_async_copy(roof_far, roof, local.at[1]),
    ]
    for copy in terms:
        copy.start()
    barrier = pltpu.get_barrier_semaphore()
    for axis, size, mine in (("terrain", owners, me), ("event", events, group)):
        for hop in range(1, size):
            pl.semaphore_signal(
                barrier, inc=1, device_id={axis: lax.rem(mine + hop, size)}, device_id_type=MESH
            )
    for copy in terms:
        copy.wait()
    picked = (groups * share_rows, floor.shape[1])
    account = lax.broadcasted_iota(jnp.int32, picked, 1)
    mine = account == lax.broadcasted_iota(jnp.int32, picked, 0) + me * picked[0]
    for near, wide in ((floor, least), (roof, most)):
        column = jnp.sum(jnp.where(mine, near[...], 0.0), axis=1, keepdims=True)
        column = jnp.broadcast_to(column, (picked[0], bins))
        for h in range(groups):
            wide[h] = column[h * share_rows : (h + 1) * share_rows]
    pl.semaphore_wait(barrier, owners + events - 2)

    def part_copy(h, hop):
        owner = lax.rem(me + hop, owners)
        return pltpu.make_async_remote_copy(
            src_ref=total.at[h, owner],
            dst_ref=parts.at[h, me],
            send_sem=sent_part.at[h, hop],
            recv_sem=got_part.at[h, hop],
            device_id={"terrain": owner},
            device_id_type=MESH,
        )

    def low_copy(h, hop):
        return pltpu.make_async_remote_copy(
            src_ref=made_low.at[h],
            dst_ref=net_loss.at[me, h],
            send_sem=sent_low.at[h, hop],
            recv_sem=got_low.at[h, hop],
            device_id={"terrain": lax.rem(me + hop, owners)},
            device_id_type=MESH,
        )

    def net_copy(h, hop):
        return pltpu.make_async_remote_copy(
            src_ref=made.at[h],
            dst_ref=arrived.at[group, h],
            send_sem=sent_net.at[h, hop],
            recv_sem=got_net.at[h, hop],
            device_id={"event": lax.rem(group + hop, events)},
            device_id_type=MESH,
        )

    def give(h):
        for hop in range(1, owners):
            part_copy(h, hop).start()

    def finish(h):
        whole = total[h, me]
        for hop in range(1, owners):
            part_copy(h, hop).wait()
            whole = whole + parts[h, lax.rem(me + owners - hop, owners)]
        net = jnp.minimum(jnp.maximum(whole * scale - least[h], 0.0), most[h])
        made[h] = net
        low = net.astype(made_low.dtype)
        made_low[h] = low
        net_loss[me, h] = low
        for hop in range(1, events):
            net_copy(h, hop).start()
        for hop in range(1, owners):
            low_copy(h, hop).start()

    account_id = numbered(group_size, cells, 0)
    bin_id = jnp.concatenate([numbered(16, bins, 1)] * (cells // 16), axis=0)
    span = min(SPAN, bundles)

    def one_group(h, _):
        rows = pl.ds(pl.multiple_of(h * group_size, group_size), group_size)
        turned = [lax.rem(e + groups - h, together) for e in range(together)]
        summed = None
        for c in range(bundles // span):
            if c == bundles // span // 2:

                @pl.when(h > 0)
                def _():
                    give(h - 1)

            left, right = [], []
            for block in range(span // CHUNK):
                first = c * span + block * CHUNK
                columns = jnp.transpose(bounds[h, first : first + CHUNK, :]).astype(jnp.bfloat16)
                for i in range(CHUNK):
                    bundle = first + i
                    left.append(
                        jnp.where(
                            rowed(lows[h, bundle : bundle + 1, :], group_size) == account_id,
                            rowed(values[h, bundle : bundle + 1, :], group_size),
                            zero,
                        )
                    )
                    shown = []
                    for e in range(together):
                        row = ratio[bundle, turned[e]]
                        shown.extend([row] * (capacity // 16))
                    bound = jnp.broadcast_to(columns[:, i : i + 1], (cells, bins))
                    right.append(
                        jnp.where(bin_id >= bound, jnp.concatenate(shown, axis=0), zero)
                    )
            part = jnp.dot(
                jnp.concatenate(left, axis=1),
                jnp.concatenate(right, axis=0),
                preferred_element_type=jnp.float32,
            )
            summed = part if summed is None else summed + part
        summed = summed + spill[rows, :]
        for t in range(owners):
            total[h, t] = summed[t * share_rows : (t + 1) * share_rows]

        @pl.when(h >= LAG)
        def _():
            finish(h - LAG)

        return 0

    lax.fori_loop(0, groups, one_group, 0)
    give(groups - 1)
    for h in range(groups - LAG, groups):
        finish(h)

    def close(h, _):
        whole = made[h]
        for hop in range(1, events):
            net_copy(h, hop).wait()
            whole = whole + arrived[lax.rem(group + events - hop, events), h]
        portfolio[h] = whole / events
        for hop in range(1, owners):
            low_copy(h, hop).wait()
        return 0

    lax.fori_loop(0, groups, close, 0)


def settle(lows, bounds, values, ratio, spill, floor, roof, scale, number):
    account_count, bins = spill.shape
    groups = lows.shape[0]
    owners, events = lax.axis_size("terrain"), lax.axis_size("event")
    share = (groups, account_count // owners // groups, bins)
    pieces = (groups, owners) + share[1:]
    dma = pltpu.SemaphoreType.DMA
    return pl.pallas_call(
        functools.partial(settle_kernel, scale),
        out_shape=(
            jax.ShapeDtypeStruct((owners,) + share, jnp.bfloat16),
            jax.ShapeDtypeStruct(share, jnp.float32),
        ),
        in_specs=[VMEM] * 5 + [HBM] * 2,
        out_specs=(VMEM, VMEM),
        scratch_shapes=[pltpu.VMEM(floor.shape, floor.dtype)] * 2
        + [pltpu.VMEM(share, jnp.float32)] * 2
        + [pltpu.VMEM(pieces, jnp.float32)] * 2
        + [
            pltpu.VMEM(share, jnp.float32),
            pltpu.VMEM(share, jnp.bfloat16),
            pltpu.VMEM((events,) + share, jnp.float32),
        ]
        + [dma((groups, owners))] * 4
        + [dma((groups, events))] * 2
        + [dma((2,))],
        compiler_params=pltpu.CompilerParams(
            collective_id=number, has_side_effects=True, vmem_limit_bytes=LIMIT
        ),
        name="settle",
    )(lows, bounds, values, ratio, spill, *far([floor, roof]))


def per_device(
    level_start,
    bed_depth,
    wet_bits,
    tile_owner,
    vuln_weight,
    vuln_bias,
    account_index,
    bin_index,
    exposure_value,
    deductible,
    limit,
):
    _, rows, width = level_start.shape
    tile_cells, bin_count = vuln_weight.shape
    account_count = deductible.shape[0]
    owners = lax.axis_size("terrain")
    events = lax.axis_size("event")
    share_rows = account_count // owners
    tiles = rows * width // tile_cells
    level, ratio, low, bound, value = front(
        [level_start[0], bed_depth, wet_bits[0]],
        [account_index, bin_index, exposure_value],
        tile_owner.reshape(1, tiles),
        vuln_weight,
        vuln_bias[None, :],
        1,
    )
    scale = account_count / (rows * width * owners)
    *sorted_cells, level = sort(low, bound, value, ratio, level, account_count)
    net_loss, portfolio = settle(
        *sorted_cells, deductible[None, :], limit[None, :], scale, 2
    )
    portfolio = portfolio.reshape(share_rows, bin_count)
    return (level[None], net_loss.reshape(1, account_count, bin_count), portfolio)


def solution(mesh):
    placed = (
        P("event", "terrain", None),
        P("terrain", None),
        P("event", "terrain", None),
        P("terrain", None),
        P(),
        P(),
        P("terrain", None),
        P("terrain", None),
        P("terrain", None),
        P(),
        P(),
    )
    return jax.shard_map(
        per_device,
        mesh=mesh,
        in_specs=placed,
        out_specs=(P("event", "terrain", None), P("event", None, None), P("terrain", None)),
        check_vma=False,
    )
```

```python
import functools

import jax
import jax.numpy as jnp
from jax import lax
from jax.experimental import pallas as pl
from jax.experimental.pallas import tpu as pltpu
from jax.sharding import PartitionSpec as P

SUBSTEPS = 8
CHUNK = 8
LIMIT = 24 * 2**20
GROUPS = 8
SPAN = 32
UNROLL = 16

courant = 0.5
gravity = 1.0

VMEM = pl.BlockSpec(memory_space=pltpu.VMEM)
HBM = pl.BlockSpec(memory_space=pltpu.HBM)
MESH = pl.DeviceIdType.MESH


def far(arrays):
    return [pltpu.with_memory_space_constraint(a, pltpu.HBM) for a in arrays]


def padded(count, unit):
    return -(-count // unit) * unit


def front_kernel(
    level_far, bed_far, wet_far, account_far, threshold_far, value_far, owner_far, weight_far, bias_far,
    level_out, ratio_out, low_out, bin_out, value_out,
    level_here, bed_here, wet_here, account, threshold, value, owner_row, weight, bias, loads,
    made, kept, got, level_above, bed_above, wet_above, level_below, bed_below, wet_below,
    halo_sent, halo_got, cell_sent, cell_got, local,
):
    size = lax.axis_size("terrain")
    me = lax.axis_index("terrain")
    barrier = pltpu.get_barrier_semaphore()
    for hop in range(1, size):
        pl.semaphore_signal(
            barrier, inc=1, device_id={"terrain": lax.rem(me + hop, size)}, device_id_type=MESH
        )
    moved = (
        (account_far, account), (threshold_far, threshold), (value_far, value),
        (owner_far, owner_row), (level_far, level_here), (bed_far, bed_here), (wet_far, wet_here),
        (weight_far, weight), (bias_far, bias),
    )
    reads = [
        pltpu.make_async_copy(far, near, loads.at[n]) for n, (far, near) in enumerate(moved)
    ]
    for copy in reads:
        copy.start()
    for copy in reads[:4]:
        copy.wait()
    rows, width = level_here.shape
    capacity = account.shape[0] // size
    room = made.shape[2]

    accounts = account[...]
    low = (accounts & 255) - ((accounts >> 8) & 1) * 256
    bound = threshold[...] - (accounts >> 9) * 256
    fields = (low.astype(jnp.float32), bound.astype(jnp.float32), value[...].astype(jnp.float32))
    if room != capacity:
        made[...] = jnp.zeros(made.shape, made.dtype)
    for n in range(size):
        for f in range(3):
            made[n, f, :capacity, :] = fields[f][n * capacity : (n + 1) * capacity].astype(
                made.dtype
            )
    keep = pltpu.make_async_copy(made, kept, local.at[0])
    keep.start()
    pl.semaphore_wait(barrier, size - 1)

    later, earlier = lax.rem(me + 1, size), lax.rem(me + size - 1, size)
    strips = (level_far, bed_far, wet_far)
    above = (level_above, bed_above, wet_above)
    below = (level_below, bed_below, wet_below)
    edges = []
    for side, (peer, targets) in enumerate(((later, above), (earlier, below))):
        for i in range(3):
            first = 0 if side else rows - SUBSTEPS
            copy = pltpu.make_async_remote_copy(
                src_ref=strips[i].at[pl.ds(first, SUBSTEPS)],
                dst_ref=targets[i],
                send_sem=halo_sent.at[side * 3 + i],
                recv_sem=halo_got.at[side * 3 + i],
                device_id={"terrain": peer},
                device_id_type=MESH,
            )
            copy.start()
            edges.append(copy)
    keep.wait()
    cells = []
    for hop in range(1, size):
        peer = lax.rem(me + hop, size)
        copy = pltpu.make_async_remote_copy(
            src_ref=kept.at[peer],
            dst_ref=got.at[me],
            send_sem=cell_sent.at[hop],
            recv_sem=cell_got.at[hop],
            device_id={"terrain": peer},
            device_id_type=MESH,
        )
        copy.start()
        cells.append(copy)
    own = pltpu.make_async_copy(kept.at[me], got.at[me], local.at[1])
    own.start()
    cells.append(own)

    tile = weight.shape[0]
    blocks = width // tile
    tiles = rows * blocks
    number = lax.broadcasted_iota(jnp.int32, (tiles, tiles), 0)
    number = (number % rows) * blocks + number // rows
    along = lax.broadcasted_iota(jnp.int32, (tiles, tiles), 1)
    owner = owner_row[...].astype(jnp.float32)
    owner_column = jnp.sum(jnp.where(along == number, owner, 0.0), axis=1, keepdims=True)
    same = (owner_column == owner) & (along < number)
    rank = jnp.sum(jnp.where(same, 1.0, 0.0), axis=1, keepdims=True)
    slot = lax.broadcasted_iota(jnp.int32, (tiles, size * room), 1).astype(jnp.float32)
    chosen = jnp.where(slot == owner_column * room + rank, 1.0, 0.0).astype(jnp.bfloat16)

    for copy in reads[4:] + edges:
        copy.wait()
    first_row = me * rows - SUBSTEPS
    total_rows = rows * size
    level = jnp.concatenate([level_above[...], level_here[...], level_below[...]], axis=0)
    bed = jnp.concatenate([bed_above[...], bed_here[...], bed_below[...]], axis=0)
    wet = jnp.concatenate([wet_above[...], wet_here[...], wet_below[...]], axis=0)
    shape = level.shape
    tall = shape[0]
    row_id = first_row + lax.broadcasted_iota(jnp.int32, shape, 0)
    column = lax.broadcasted_iota(jnp.int32, shape, 1)
    inside = ((row_id >= 0) & (row_id < total_rows)).astype(jnp.float32)
    not_first = (column > 0).astype(jnp.float32)
    not_last = (column < width - 1).astype(jnp.float32)

    def down(field):
        return pltpu.roll(field, tall - 1, 0)

    def up(field):
        return pltpu.roll(field, 1, 0)

    def right(field):
        return pltpu.roll(field, width - 1, 1) * not_last

    def left(field):
        return pltpu.roll(field, 1, 1) * not_first

    quarter = 0.25
    assert courant * gravity == 0.5
    level = level * inside
    row_speed = jnp.zeros(shape, jnp.float32)
    col_speed = jnp.zeros(shape, jnp.float32)
    for step in range(SUBSTEPS):
        wet_factor = ((wet >> step) & 1).astype(jnp.float32) * (inside * quarter)
        if step:
            row_flow, col_flow = bed * row_speed, bed * col_speed
            new_level = (
                down(level - row_flow) + up(level + row_flow)
                + (right(level - col_flow) + left(level + col_flow))
            )
            new_row = (
                down(row_speed - level) + up(row_speed + level)
                + (right(row_speed) + left(row_speed))
            )
            new_col = (
                down(col_speed) + up(col_speed)
                + (right(col_speed - level) + left(col_speed + level))
            )
            row_speed, col_speed = new_row * wet_factor, new_col * wet_factor
        else:
            ld, lu, lr, ll = down(level), up(level), right(level), left(level)
            new_level = ld + lu + (lr + ll)
            row_speed = (lu - ld) * wet_factor
            col_speed = (ll - lr) * wet_factor
        level = new_level * (inside * quarter)
    level = level[SUBSTEPS : SUBSTEPS + rows]
    level_out[...] = level
    pieces = jnp.concatenate(
        [level[:, j * tile : (j + 1) * tile] for j in range(blocks)], axis=0
    ).astype(jnp.bfloat16)
    ratio_out[...] = jax.nn.sigmoid(
        jnp.dot(pieces, weight[...], preferred_element_type=jnp.float32) + bias[...]
    ).astype(jnp.bfloat16)
    for copy in cells:
        copy.wait()
    for f, target in enumerate((low_out, bin_out, value_out)):
        records = jnp.concatenate([got[n, f] for n in range(size)], axis=0)
        target[...] = jnp.dot(chosen, records, preferred_element_type=jnp.float32).astype(
            target.dtype
        )


def front(strips, records, owner_row, weight, bias, number):
    rows, width = strips[0].shape
    slots, cells = records[0].shape
    size = lax.axis_size("terrain")
    tiles = rows * width // cells
    packed = (size, 3, padded(slots // size, 16), cells)
    edge = (SUBSTEPS, width)
    inputs = strips + records + [owner_row, weight, bias]
    dma = pltpu.SemaphoreType.DMA
    edges = [pltpu.VMEM(edge, f.dtype) for f in strips]
    return pl.pallas_call(
        front_kernel,
        out_shape=(
            jax.ShapeDtypeStruct((rows, width), jnp.float32),
            jax.ShapeDtypeStruct((tiles, weight.shape[1]), jnp.bfloat16),
        )
        + (jax.ShapeDtypeStruct((tiles, cells), jnp.bfloat16),) * 3,
        in_specs=[HBM] * 9,
        out_specs=(VMEM,) * 5,
        scratch_shapes=[pltpu.VMEM(a.shape, a.dtype) for a in inputs]
        + [dma((9,))]
        + [pltpu.VMEM(packed, jnp.bfloat16)] * 3
        + edges * 2
        + [dma((6,))] * 2
        + [dma((size,))] * 2
        + [dma((2,))],
        compiler_params=pltpu.CompilerParams(
            collective_id=number, has_side_effects=True, vmem_limit_bytes=LIMIT
        ),
        name="front",
    )(*far(inputs))


def rowed(row, height):
    packed = jnp.broadcast_to(row, (16, row.shape[1])).astype(jnp.bfloat16)
    return jnp.concatenate([packed] * (height // 16), axis=0)


def numbered(height, width, axis):
    return (
        lax.broadcasted_iota(jnp.int32, (height, width), axis)
        .astype(jnp.float32)
        .astype(jnp.bfloat16)
    )


def sort_kernel(
    owners, low_in, bin_in, value_in, ratio_in, level_in,
    lows, bounds, values, ratio, total, level_out,
    ratio_all, low_all, bound_all, value_all, places,
):
    level_out[...] = level_in[...]
    total[...] = jnp.zeros(total.shape, jnp.float32)
    accounts, bins = total.shape
    tiles, cells = low_in.shape
    groups = lows.shape[0]
    group_size = accounts // groups
    capacity = 2 * cells // groups
    together = cells // capacity
    bundles = tiles // together
    zero = jnp.zeros((), jnp.bfloat16)
    one = jnp.ones((), jnp.bfloat16)

    low = low_in[...].astype(jnp.float32)
    bound = bin_in[...].astype(jnp.float32)
    high = jnp.where(low < 0, 256.0, 0.0) + jnp.where(bound < 0, 512.0, 0.0)
    low = jnp.where(low < 0, low + 256.0, low) + high
    account = low.astype(jnp.int32)
    share = accounts // owners
    rows = share // groups
    group = account % share // rows
    low_all[...] = (account // share * rows + account % rows).astype(jnp.float32)
    bound_all[...] = jnp.where(bound < 0, bound + 256.0, bound)
    ratio_all[...] = ratio_in[...].astype(jnp.float32)
    value_all[...] = value_in[...].astype(jnp.float32)
    earlier = jnp.where(
        lax.broadcasted_iota(jnp.int32, (cells, cells), 0)
        < lax.broadcasted_iota(jnp.int32, (cells, cells), 1),
        1.0,
        0.0,
    ).astype(jnp.bfloat16)
    turn = lax.broadcasted_iota(jnp.int32, (tiles, cells), 0) % together
    rank = jnp.zeros((tiles, cells), jnp.float32)
    for h in range(groups):
        mine = group == h
        count = jnp.dot(
            jnp.where(mine, 1.0, 0.0).astype(jnp.bfloat16),
            earlier,
            preferred_element_type=jnp.float32,
        )
        rank = jnp.where(mine, count, rank)
    base = (group // together) * cells + ((group + turn) % together) * capacity
    fits = rank < capacity
    places[...] = jnp.where(fits, base.astype(jnp.float32) + rank, -1.0 - group.astype(jnp.float32))

    place_id = numbered(2 * cells, cells, 0)
    lane = lax.broadcasted_iota(jnp.int32, (8, cells), 1) // capacity
    field = lax.broadcasted_iota(jnp.int32, (8, cells), 0)
    unroll = max(1, UNROLL // together)

    def spread(ref, t):
        return jnp.broadcast_to(ref[pl.ds(t, 1), :], (8, cells))

    def gather(number, _):
        for u in range(unroll):
            bundle = number * unroll + u
            for j in range(together):
                t = bundle * together + j
                ratio[bundle, j] = jnp.broadcast_to(
                    ratio_all[pl.ds(t, 1), :], (16, bins)
                ).astype(jnp.bfloat16)
            found = []
            for j in range(together):
                t = bundle * together + j
                here = rowed(places[pl.ds(t, 1), :], 2 * cells) == place_id
                fields = jnp.where(
                    field == 0,
                    spread(low_all, t),
                    jnp.where(field == 1, spread(bound_all, t), spread(value_all, t)),
                )
                found.append(
                    lax.dot_general(
                        fields.astype(jnp.bfloat16),
                        jnp.where(here, one, zero),
                        (((1,), (1,)), ((), ())),
                        preferred_element_type=jnp.float32,
                    )
                )
            for q in range(2):
                parts = [f[:, q * cells : (q + 1) * cells] for f in found]
                for r in range(together):
                    mixed = parts[(0 - r) % together]
                    for e in range(1, together):
                        mixed = jnp.where(lane == e, parts[(e - r) % together], mixed)
                    h = q * together + r
                    lows[h, pl.ds(bundle, 1), :] = mixed[0:1]
                    bounds[h, pl.ds(bundle, 1), :] = mixed[1:2]
                    values[h, pl.ds(bundle, 1), :] = mixed[2:3]
        return 0

    lax.fori_loop(0, bundles // unroll, gather, 0)

    spilled = jnp.max(rank) >= capacity

    @pl.when(spilled)
    def _():
        account_id = numbered(group_size, cells, 0)
        bin_id = jnp.concatenate([numbered(16, bins, 1)] * (cells // 16), axis=0)
        tile_id = lax.broadcasted_iota(jnp.int32, (tiles, cells), 0).astype(jnp.float32)

        def dense(left_over):
            t = left_over.astype(jnp.int32)
            place = places[pl.ds(t, 1), :]
            rest = jnp.where(place < 0, value_all[pl.ds(t, 1), :], 0.0)
            hit = rowed(low_all[pl.ds(t, 1), :], group_size) == account_id
            column = jnp.transpose(spread(bound_all, t)).astype(jnp.bfloat16)[:, 0:1]
            right = jnp.where(
                bin_id >= jnp.broadcast_to(column, (cells, bins)),
                rowed(ratio_all[pl.ds(t, 1), :], cells),
                zero,
            )
            for h in range(groups):
                part = jnp.where(place == -1.0 - h, rest, 0.0)
                left = jnp.where(hit, rowed(part, group_size), zero)
                total[pl.ds(h * group_size, group_size), :] += jnp.dot(
                    left, right, preferred_element_type=jnp.float32
                )
            return jnp.max(jnp.where((places[...] < 0) & (tile_id < left_over), tile_id, -1.0))

        lax.while_loop(
            lambda t: t >= 0, dense, jnp.max(jnp.where(places[...] < 0, tile_id, -1.0))
        )


def sort(low, bound, value, ratio, level, account_count):
    tiles, cells = low.shape
    bins = ratio.shape[1]
    together = GROUPS // 2
    bundles = tiles // together
    gathered = jax.ShapeDtypeStruct((GROUPS, bundles, cells), jnp.float32)
    whole = pltpu.VMEM((tiles, cells), jnp.float32)
    return pl.pallas_call(
        functools.partial(sort_kernel, lax.axis_size("terrain")),
        out_shape=(
            gathered,
            gathered,
            gathered,
            jax.ShapeDtypeStruct((bundles, together, 16, bins), jnp.bfloat16),
            jax.ShapeDtypeStruct((account_count, bins), jnp.float32),
            jax.ShapeDtypeStruct(level.shape, level.dtype),
        ),
        in_specs=[VMEM] * 5,
        out_specs=(VMEM,) * 6,
        scratch_shapes=[pltpu.VMEM((tiles, bins), jnp.float32)] + [whole] * 4,
        compiler_params=pltpu.CompilerParams(vmem_limit_bytes=LIMIT),
        name="sort",
    )(low, bound, value, ratio, level)


def settle_kernel(
    scale, lows, bounds, values, ratio, spill, floor_far, roof_far,
    net_loss, portfolio,
    floor, roof, least, most, total, pairs, both, parts, made, made_low, arrived,
    sent_pair, got_pair, sent_part, got_part, sent_low, got_low, sent_more, got_more,
    sent_net, got_net, local,
):
    groups, _, chips, share_rows, bins = total.shape
    owners = 2 * chips
    _, bundles, cells = lows.shape
    group_size = owners * share_rows
    capacity = 2 * cells // groups
    together = cells // capacity
    zero = jnp.zeros((), jnp.bfloat16)
    events = lax.axis_size("event")
    me, group = lax.axis_index("terrain"), lax.axis_index("event")
    terms = [
        pltpu.make_async_copy(floor_far, floor, local.at[0]),
        pltpu.make_async_copy(roof_far, roof, local.at[1]),
    ]
    for copy in terms:
        copy.start()
    barrier = pltpu.get_barrier_semaphore()
    for axis, size, mine in (("terrain", owners, me), ("event", events, group)):
        for hop in range(1, size):
            pl.semaphore_signal(
                barrier, inc=1, device_id={axis: lax.rem(mine + hop, size)}, device_id_type=MESH
            )
    for copy in terms:
        copy.wait()
    picked = (groups * share_rows, floor.shape[1])
    account = lax.broadcasted_iota(jnp.int32, picked, 1)
    mine = account == lax.broadcasted_iota(jnp.int32, picked, 0) + me * picked[0]
    for near, wide in ((floor, least), (roof, most)):
        column = jnp.sum(jnp.where(mine, near[...], 0.0), axis=1, keepdims=True)
        column = jnp.broadcast_to(column, (picked[0], bins))
        for h in range(groups):
            wide[h] = column[h * share_rows : (h + 1) * share_rows]
    pl.semaphore_wait(barrier, owners + events - 2)

    core, chip = lax.rem(me, 2), me // 2
    partner = me + 1 - 2 * core

    def remote(source, target, sent, received, axis, peer):
        return pltpu.make_async_remote_copy(
            src_ref=source,
            dst_ref=target,
            send_sem=sent,
            recv_sem=received,
            device_id={axis: peer},
            device_id_type=MESH,
        )

    def behind(k):
        return lax.rem(chip + chips - k, chips)

    def pair_copy(h):
        return remote(
            total.at[h, 1 - core], pairs.at[h], sent_pair.at[h], got_pair.at[h], "terrain", partner
        )

    def part_copy(h, k):
        to = lax.rem(chip + k, chips)
        return remote(
            both.at[h, to], parts.at[h, chip], sent_part.at[h, k], got_part.at[h, k],
            "terrain", 2 * to + core,
        )

    def low_copy(h, k):
        peer = 2 * lax.rem(chip + k, chips) + core if k else partner
        return remote(
            made_low.at[h], net_loss.at[me, h], sent_low.at[h, k], got_low.at[h, k],
            "terrain", peer,
        )

    def more_copy(h, k):
        block = net_loss.at[2 * behind(k) + core, h]
        return remote(block, block, sent_more.at[h, k], got_more.at[h, k], "terrain", partner)

    def net_copy(h, hop):
        return remote(
            made.at[h], arrived.at[group, h], sent_net.at[h, hop], got_net.at[h, hop],
            "event", lax.rem(group + hop, events),
        )

    def give(h):
        pair_copy(h).start()

    def spread(h):
        pair_copy(h).wait()
        both[h] = total[h, core] + pairs[h]
        for k in range(1, chips):
            part_copy(h, k).start()

    def finish(h):
        whole = both[h, chip]
        for k in range(1, chips):
            part_copy(h, k).wait()
            whole = whole + parts[h, behind(k)]
        net = jnp.minimum(jnp.maximum(whole * scale - least[h], 0.0), most[h])
        made[h] = net
        low = net.astype(made_low.dtype)
        made_low[h] = low
        net_loss[me, h] = low
        for hop in range(1, events):
            net_copy(h, hop).start()
        for k in range(1, chips):
            low_copy(h, k).start()
        low_copy(h, 0).start()

    def forward(h):
        for k in range(1, chips):
            low_copy(h, k).wait()
            more_copy(h, k).start()

    stages = ((give, 1), (spread, 2), (finish, 4), (forward, 6))

    account_id = numbered(group_size, cells, 0)
    bin_id = jnp.concatenate([numbered(16, bins, 1)] * (cells // 16), axis=0)
    span = min(SPAN, bundles)

    def one_group(h, _):
        for stage, lag in stages[::-1]:

            @pl.when(h >= lag)
            def _(stage=stage, lag=lag):
                stage(h - lag)

        rows = pl.ds(pl.multiple_of(h * group_size, group_size), group_size)
        turned = [lax.rem(e + groups - h, together) for e in range(together)]
        summed = None
        for c in range(bundles // span):
            left, right = [], []
            for block in range(span // CHUNK):
                first = c * span + block * CHUNK
                columns = jnp.transpose(bounds[h, first : first + CHUNK, :]).astype(jnp.bfloat16)
                for i in range(CHUNK):
                    bundle = first + i
                    left.append(
                        jnp.where(
                            rowed(lows[h, bundle : bundle + 1, :], group_size) == account_id,
                            rowed(values[h, bundle : bundle + 1, :], group_size),
                            zero,
                        )
                    )
                    shown = []
                    for e in range(together):
                        row = ratio[bundle, turned[e]]
                        shown.extend([row] * (capacity // 16))
                    bound = jnp.broadcast_to(columns[:, i : i + 1], (cells, bins))
                    right.append(
                        jnp.where(bin_id >= bound, jnp.concatenate(shown, axis=0), zero)
                    )
            part = jnp.dot(
                jnp.concatenate(left, axis=1),
                jnp.concatenate(right, axis=0),
                preferred_element_type=jnp.float32,
            )
            summed = part if summed is None else summed + part
        summed = summed + spill[rows, :]
        for t in range(owners):
            total[h, t % 2, t // 2] = summed[t * share_rows : (t + 1) * share_rows]

        return 0

    lax.fori_loop(0, groups, one_group, 0)
    for stage, lag in stages:
        for h in range(groups - lag, groups):
            stage(h)

    def close(h, _):
        whole = made[h]
        for hop in range(1, events):
            net_copy(h, hop).wait()
            whole = whole + arrived[lax.rem(group + events - hop, events), h]
        portfolio[h] = whole / events
        low_copy(h, 0).wait()
        for k in range(1, chips):
            more_copy(h, k).wait()
        return 0

    lax.fori_loop(0, groups, close, 0)


def settle(lows, bounds, values, ratio, spill, floor, roof, scale, number):
    account_count, bins = spill.shape
    groups = lows.shape[0]
    owners, events = lax.axis_size("terrain"), lax.axis_size("event")
    share = (groups, account_count // owners // groups, bins)
    chips = owners // 2
    pieces = (groups, chips) + share[1:]
    dma = pltpu.SemaphoreType.DMA
    return pl.pallas_call(
        functools.partial(settle_kernel, scale),
        out_shape=(
            jax.ShapeDtypeStruct((owners,) + share, jnp.bfloat16),
            jax.ShapeDtypeStruct(share, jnp.float32),
        ),
        in_specs=[VMEM] * 5 + [HBM] * 2,
        out_specs=(VMEM, VMEM),
        scratch_shapes=[pltpu.VMEM(floor.shape, floor.dtype)] * 2
        + [pltpu.VMEM(share, jnp.float32)] * 2
        + [pltpu.VMEM((groups, 2, chips) + share[1:], jnp.float32)]
        + [pltpu.VMEM(pieces, jnp.float32)] * 3
        + [
            pltpu.VMEM(share, jnp.float32),
            pltpu.VMEM(share, jnp.bfloat16),
            pltpu.VMEM((events,) + share, jnp.float32),
        ]
        + [dma((groups,))] * 2
        + [dma((groups, chips))] * 6
        + [dma((groups, events))] * 2
        + [dma((2,))],
        compiler_params=pltpu.CompilerParams(
            collective_id=number, has_side_effects=True, vmem_limit_bytes=LIMIT
        ),
        name="settle",
    )(lows, bounds, values, ratio, spill, *far([floor, roof]))


def per_device(
    level_start,
    bed_depth,
    wet_bits,
    tile_owner,
    vuln_weight,
    vuln_bias,
    account_index,
    bin_index,
    exposure_value,
    deductible,
    limit,
):
    _, rows, width = level_start.shape
    tile_cells, bin_count = vuln_weight.shape
    account_count = deductible.shape[0]
    owners = lax.axis_size("terrain")
    events = lax.axis_size("event")
    share_rows = account_count // owners
    tiles = rows * width // tile_cells
    level, ratio, low, bound, value = front(
        [level_start[0], bed_depth, wet_bits[0]],
        [account_index, bin_index, exposure_value],
        tile_owner.reshape(1, tiles),
        vuln_weight,
        vuln_bias[None, :],
        1,
    )
    scale = account_count / (rows * width * owners)
    *sorted_cells, level = sort(low, bound, value, ratio, level, account_count)
    net_loss, portfolio = settle(
        *sorted_cells, deductible[None, :], limit[None, :], scale, 2
    )
    portfolio = portfolio.reshape(share_rows, bin_count)
    return (level[None], net_loss.reshape(1, account_count, bin_count), portfolio)


def solution(mesh):
    placed = (
        P("event", "terrain", None),
        P("terrain", None),
        P("event", "terrain", None),
        P("terrain", None),
        P(),
        P(),
        P("terrain", None),
        P("terrain", None),
        P("terrain", None),
        P(),
        P(),
    )
    return jax.shard_map(
        per_device,
        mesh=mesh,
        in_specs=placed,
        out_specs=(P("event", "terrain", None), P("event", None, None), P("terrain", None)),
        check_vma=False,
    )
```

```python
import functools

import jax
import jax.numpy as jnp
from jax import lax
from jax.experimental import pallas as pl
from jax.experimental.pallas import tpu as pltpu
from jax.sharding import PartitionSpec as P

SUBSTEPS = 8
CHUNK = 8
LIMIT = 24 * 2**20
GROUPS = 8
SPAN = 32

courant = 0.5
gravity = 1.0

VMEM = pl.BlockSpec(memory_space=pltpu.VMEM)
HBM = pl.BlockSpec(memory_space=pltpu.HBM)
MESH = pl.DeviceIdType.MESH
PICK = lax.GatherDimensionNumbers(
    offset_dims=(),
    collapsed_slice_dims=(1,),
    start_index_map=(1,),
    operand_batching_dims=(0,),
    start_indices_batching_dims=(0,),
)


def far(arrays):
    return [pltpu.with_memory_space_constraint(a, pltpu.HBM) for a in arrays]


def padded(count, unit):
    return -(-count // unit) * unit


def front_kernel(
    level_far, bed_far, wet_far, account_far, threshold_far, value_far, owner_far, weight_far, bias_far,
    level_out, ratio_out, low_out, bin_out, value_out,
    level_here, bed_here, wet_here, account, threshold, value, owner_row, weight, bias, loads,
    made, kept, got, level_above, bed_above, wet_above, level_below, bed_below, wet_below,
    halo_sent, halo_got, cell_sent, cell_got, local,
):
    size = lax.axis_size("terrain")
    me = lax.axis_index("terrain")
    barrier = pltpu.get_barrier_semaphore()
    for hop in range(1, size):
        pl.semaphore_signal(
            barrier, inc=1, device_id={"terrain": lax.rem(me + hop, size)}, device_id_type=MESH
        )
    moved = (
        (account_far, account), (threshold_far, threshold), (value_far, value),
        (owner_far, owner_row), (level_far, level_here), (bed_far, bed_here), (wet_far, wet_here),
        (weight_far, weight), (bias_far, bias),
    )
    reads = [
        pltpu.make_async_copy(far, near, loads.at[n]) for n, (far, near) in enumerate(moved)
    ]
    for copy in reads:
        copy.start()
    for copy in reads[:4]:
        copy.wait()
    rows, width = level_here.shape
    capacity = account.shape[0] // size
    room = made.shape[2]

    accounts = account[...]
    low = (accounts & 255) - ((accounts >> 8) & 1) * 256
    bound = threshold[...] - (accounts >> 9) * 256
    fields = (low.astype(jnp.float32), bound.astype(jnp.float32), value[...].astype(jnp.float32))
    if room != capacity:
        made[...] = jnp.zeros(made.shape, made.dtype)
    for n in range(size):
        for f in range(3):
            made[n, f, :capacity, :] = fields[f][n * capacity : (n + 1) * capacity].astype(
                made.dtype
            )
    keep = pltpu.make_async_copy(made, kept, local.at[0])
    keep.start()
    pl.semaphore_wait(barrier, size - 1)

    later, earlier = lax.rem(me + 1, size), lax.rem(me + size - 1, size)
    strips = (level_far, bed_far, wet_far)
    above = (level_above, bed_above, wet_above)
    below = (level_below, bed_below, wet_below)
    edges = []
    for side, (peer, targets) in enumerate(((later, above), (earlier, below))):
        for i in range(3):
            first = 0 if side else rows - SUBSTEPS
            copy = pltpu.make_async_remote_copy(
                src_ref=strips[i].at[pl.ds(first, SUBSTEPS)],
                dst_ref=targets[i],
                send_sem=halo_sent.at[side * 3 + i],
                recv_sem=halo_got.at[side * 3 + i],
                device_id={"terrain": peer},
                device_id_type=MESH,
            )
            copy.start()
            edges.append(copy)
    keep.wait()
    cells = []
    for hop in range(1, size):
        peer = lax.rem(me + hop, size)
        copy = pltpu.make_async_remote_copy(
            src_ref=kept.at[peer],
            dst_ref=got.at[me],
            send_sem=cell_sent.at[hop],
            recv_sem=cell_got.at[hop],
            device_id={"terrain": peer},
            device_id_type=MESH,
        )
        copy.start()
        cells.append(copy)
    own = pltpu.make_async_copy(kept.at[me], got.at[me], local.at[1])
    own.start()
    cells.append(own)

    tile = weight.shape[0]
    blocks = width // tile
    tiles = rows * blocks
    number = lax.broadcasted_iota(jnp.int32, (tiles, tiles), 0)
    number = (number % rows) * blocks + number // rows
    along = lax.broadcasted_iota(jnp.int32, (tiles, tiles), 1)
    owner = owner_row[...].astype(jnp.float32)
    owner_column = jnp.sum(jnp.where(along == number, owner, 0.0), axis=1, keepdims=True)
    same = (owner_column == owner) & (along < number)
    rank = jnp.sum(jnp.where(same, 1.0, 0.0), axis=1, keepdims=True)
    slot = lax.broadcasted_iota(jnp.int32, (tiles, size * room), 1).astype(jnp.float32)
    chosen = jnp.where(slot == owner_column * room + rank, 1.0, 0.0).astype(jnp.bfloat16)

    for copy in reads[4:] + edges:
        copy.wait()
    first_row = me * rows - SUBSTEPS
    total_rows = rows * size
    level = jnp.concatenate([level_above[...], level_here[...], level_below[...]], axis=0)
    bed = jnp.concatenate([bed_above[...], bed_here[...], bed_below[...]], axis=0)
    wet = jnp.concatenate([wet_above[...], wet_here[...], wet_below[...]], axis=0)
    shape = level.shape
    tall = shape[0]
    row_id = first_row + lax.broadcasted_iota(jnp.int32, shape, 0)
    column = lax.broadcasted_iota(jnp.int32, shape, 1)
    inside = ((row_id >= 0) & (row_id < total_rows)).astype(jnp.float32)
    not_first = (column > 0).astype(jnp.float32)
    not_last = (column < width - 1).astype(jnp.float32)

    def down(field):
        return pltpu.roll(field, tall - 1, 0)

    def up(field):
        return pltpu.roll(field, 1, 0)

    def right(field):
        return pltpu.roll(field, width - 1, 1) * not_last

    def left(field):
        return pltpu.roll(field, 1, 1) * not_first

    quarter = 0.25
    assert courant * gravity == 0.5
    level = level * inside
    row_speed = jnp.zeros(shape, jnp.float32)
    col_speed = jnp.zeros(shape, jnp.float32)
    for step in range(SUBSTEPS):
        wet_factor = ((wet >> step) & 1).astype(jnp.float32) * (inside * quarter)
        if step:
            row_flow, col_flow = bed * row_speed, bed * col_speed
            new_level = (
                down(level - row_flow) + up(level + row_flow)
                + (right(level - col_flow) + left(level + col_flow))
            )
            new_row = (
                down(row_speed - level) + up(row_speed + level)
                + (right(row_speed) + left(row_speed))
            )
            new_col = (
                down(col_speed) + up(col_speed)
                + (right(col_speed - level) + left(col_speed + level))
            )
            row_speed, col_speed = new_row * wet_factor, new_col * wet_factor
        else:
            ld, lu, lr, ll = down(level), up(level), right(level), left(level)
            new_level = ld + lu + (lr + ll)
            row_speed = (lu - ld) * wet_factor
            col_speed = (ll - lr) * wet_factor
        level = new_level * (inside * quarter)
    level = level[SUBSTEPS : SUBSTEPS + rows]
    level_out[...] = level
    pieces = jnp.concatenate(
        [level[:, j * tile : (j + 1) * tile] for j in range(blocks)], axis=0
    ).astype(jnp.bfloat16)
    ratio_out[...] = jax.nn.sigmoid(
        jnp.dot(pieces, weight[...], preferred_element_type=jnp.float32) + bias[...]
    ).astype(jnp.bfloat16)
    for copy in cells:
        copy.wait()
    for f, target in enumerate((low_out, bin_out, value_out)):
        records = jnp.concatenate([got[n, f] for n in range(size)], axis=0)
        target[...] = jnp.dot(chosen, records, preferred_element_type=jnp.float32).astype(
            target.dtype
        )


def front(strips, records, owner_row, weight, bias, number):
    rows, width = strips[0].shape
    slots, cells = records[0].shape
    size = lax.axis_size("terrain")
    tiles = rows * width // cells
    packed = (size, 3, padded(slots // size, 16), cells)
    edge = (SUBSTEPS, width)
    inputs = strips + records + [owner_row, weight, bias]
    dma = pltpu.SemaphoreType.DMA
    edges = [pltpu.VMEM(edge, f.dtype) for f in strips]
    return pl.pallas_call(
        front_kernel,
        out_shape=(
            jax.ShapeDtypeStruct((rows, width), jnp.float32),
            jax.ShapeDtypeStruct((tiles, weight.shape[1]), jnp.bfloat16),
        )
        + (jax.ShapeDtypeStruct((tiles, cells), jnp.bfloat16),) * 3,
        in_specs=[HBM] * 9,
        out_specs=(VMEM,) * 5,
        scratch_shapes=[pltpu.VMEM(a.shape, a.dtype) for a in inputs]
        + [dma((9,))]
        + [pltpu.VMEM(packed, jnp.bfloat16)] * 3
        + edges * 2
        + [dma((6,))] * 2
        + [dma((size,))] * 2
        + [dma((2,))],
        compiler_params=pltpu.CompilerParams(
            collective_id=number, has_side_effects=True, vmem_limit_bytes=LIMIT
        ),
        name="front",
    )(*far(inputs))


def rowed(row, height):
    packed = jnp.broadcast_to(row, (16, row.shape[1])).astype(jnp.bfloat16)
    return jnp.concatenate([packed] * (height // 16), axis=0)


def over(number, power):
    assert power & (power - 1) == 0
    return number >> (power.bit_length() - 1)


def rest(number, power):
    assert power & (power - 1) == 0
    return number & (power - 1)


def numbered(height, width, axis):
    return (
        lax.broadcasted_iota(jnp.int32, (height, width), axis)
        .astype(jnp.float32)
        .astype(jnp.bfloat16)
    )


def sort_kernel(
    owners, low_in, bin_in, value_in, ratio_in, level_in,
    lows, bounds, values, ratio, total, level_out,
    ratio_all, low_all, bound_all, value_all, places, keys, worths,
):
    level_out[...] = level_in[...]
    total[...] = jnp.zeros(total.shape, jnp.float32)
    accounts, bins = total.shape
    tiles, cells = low_in.shape
    groups = lows.shape[0]
    group_size = accounts // groups
    capacity = 2 * cells // groups
    together = cells // capacity
    bundles = tiles // together
    zero = jnp.zeros((), jnp.bfloat16)

    ratio_all[...] = ratio_in[...].astype(jnp.float32)

    def widen(number, _):
        for u in range(8):
            for j in range(together):
                row = ratio_all[pl.ds((number * 8 + u) * together + j, 1), :]
                ratio[number * 8 + u, j] = jnp.broadcast_to(row, (16, bins)).astype(jnp.bfloat16)
        return 0

    lax.fori_loop(0, bundles // 8, widen, 0)

    low = low_in[...].astype(jnp.float32)
    bound = bin_in[...].astype(jnp.float32)
    value = value_in[...].astype(jnp.float32)
    high = jnp.where(low < 0, 256.0, 0.0) + jnp.where(bound < 0, 512.0, 0.0)
    account = (jnp.where(low < 0, low + 256.0, low) + high).astype(jnp.int32)
    bound = jnp.where(bound < 0, bound + 256.0, bound).astype(jnp.int32)
    share = accounts // owners
    rows = share // groups
    group = over(rest(account, share), rows)
    low = over(account, share) * rows + rest(account, rows)
    key = low * 256 + bound
    first = lax.broadcasted_iota(jnp.int32, (cells, cells), 0)
    second = lax.broadcasted_iota(jnp.int32, (cells, cells), 1)
    upto = jnp.where(first <= second, 1.0, 0.0).astype(jnp.bfloat16)

    def counted(h):
        mine = jnp.where(group == h, 1.0, 0.0).astype(jnp.bfloat16)
        return jnp.dot(mine, upto, preferred_element_type=jnp.float32)

    lane = lax.broadcasted_iota(jnp.int32, (tiles, cells), 1)
    turn = rest(lax.broadcasted_iota(jnp.int32, (tiles, cells), 0), together)
    wanted = rest(lane, capacity)
    shift = rest(over(lane, capacity) + together - turn, together) * 8
    largest = jnp.zeros((tiles, cells), jnp.float32)

    def taken(table, place):
        return lax.gather(
            table, place[..., None], PICK, (1, 1), mode=lax.GatherScatterMode.PROMISE_IN_BOUNDS
        )

    for q in range(2):
        table = jnp.zeros((tiles, cells), jnp.int32)
        for r in range(together):
            count = counted(q * together + r)
            largest = jnp.maximum(largest, count)
            table = table + lax.shift_left(count.astype(jnp.int32), 8 * r)

        def count_at(place):
            return lax.shift_right_logical(taken(table, place), shift) & 255

        place = jnp.zeros((tiles, cells), jnp.int32)
        step = cells // 2
        while step:
            place = jnp.where(count_at(place + (step - 1)) <= wanted, place + step, place)
            step //= 2
        keys[q] = taken(key, place)
        worths[q] = jnp.where(count_at(place) > wanted, taken(value, place), 0.0)

    block = over(lax.broadcasted_iota(jnp.int32, (bundles, cells), 1), capacity)
    for q in range(2):
        for r in range(together):
            for source, targets in ((keys, (lows, bounds)), (worths, (values,))):
                mixed = source[q, pl.ds((0 - r) % together, bundles, stride=together), :]
                for e in range(1, together):
                    part = source[q, pl.ds((e - r) % together, bundles, stride=together), :]
                    mixed = jnp.where(block == e, part, mixed)
                if len(targets) == 1:
                    values[q * together + r] = mixed
                else:
                    lows[q * together + r] = (mixed >> 8).astype(jnp.float32)
                    bounds[q * together + r] = (mixed & 255).astype(jnp.float32)

    @pl.when(jnp.max(largest) > capacity)
    def _():
        late = jnp.zeros((tiles, cells), jnp.float32)
        for h in range(groups):
            late = jnp.where((group == h) & (counted(h) > capacity), -1.0 - h, late)
        places[...] = late
        low_all[...] = low.astype(jnp.float32)
        bound_all[...] = bound.astype(jnp.float32)
        value_all[...] = value
        account_id = numbered(group_size, cells, 0)
        bin_id = jnp.concatenate([numbered(16, bins, 1)] * (cells // 16), axis=0)
        tile_id = lax.broadcasted_iota(jnp.int32, (tiles, cells), 0).astype(jnp.float32)

        def dense(left_over):
            t = left_over.astype(jnp.int32)
            place = places[pl.ds(t, 1), :]
            worth = jnp.where(place < 0, value_all[pl.ds(t, 1), :], 0.0)
            hit = rowed(low_all[pl.ds(t, 1), :], group_size) == account_id
            columns = jnp.transpose(jnp.broadcast_to(bound_all[pl.ds(t, 1), :], (8, cells)))
            right = jnp.where(
                bin_id >= jnp.broadcast_to(columns.astype(jnp.bfloat16)[:, 0:1], (cells, bins)),
                rowed(ratio_all[pl.ds(t, 1), :], cells),
                zero,
            )
            for h in range(groups):
                part = jnp.where(place == -1.0 - h, worth, 0.0)
                left = jnp.where(hit, rowed(part, group_size), zero)
                total[pl.ds(h * group_size, group_size), :] += jnp.dot(
                    left, right, preferred_element_type=jnp.float32
                )
            return jnp.max(jnp.where((places[...] < 0) & (tile_id < left_over), tile_id, -1.0))

        lax.while_loop(
            lambda t: t >= 0, dense, jnp.max(jnp.where(places[...] < 0, tile_id, -1.0))
        )


def sort(low, bound, value, ratio, level, account_count):
    tiles, cells = low.shape
    bins = ratio.shape[1]
    together = GROUPS // 2
    bundles = tiles // together
    gathered = jax.ShapeDtypeStruct((GROUPS, bundles, cells), jnp.float32)
    whole = pltpu.VMEM((tiles, cells), jnp.float32)
    return pl.pallas_call(
        functools.partial(sort_kernel, lax.axis_size("terrain")),
        out_shape=(
            gathered,
            gathered,
            gathered,
            jax.ShapeDtypeStruct((bundles, together, 16, bins), jnp.bfloat16),
            jax.ShapeDtypeStruct((account_count, bins), jnp.float32),
            jax.ShapeDtypeStruct(level.shape, level.dtype),
        ),
        in_specs=[VMEM] * 5,
        out_specs=(VMEM,) * 6,
        scratch_shapes=[pltpu.VMEM((tiles, bins), jnp.float32)]
        + [whole] * 4
        + [pltpu.VMEM((2, tiles, cells), dtype) for dtype in (jnp.int32, jnp.float32)],
        compiler_params=pltpu.CompilerParams(vmem_limit_bytes=LIMIT),
        name="sort",
    )(low, bound, value, ratio, level)


def settle_kernel(
    scale, lows, bounds, values, ratio, spill, floor_far, roof_far,
    net_loss, portfolio,
    floor, roof, least, most, total, pairs, both, parts, made, made_low, arrived,
    sent_pair, got_pair, sent_part, got_part, sent_low, got_low, sent_more, got_more,
    sent_net, got_net, local,
):
    groups, _, chips, share_rows, bins = total.shape
    owners = 2 * chips
    _, bundles, cells = lows.shape
    group_size = owners * share_rows
    capacity = 2 * cells // groups
    together = cells // capacity
    zero = jnp.zeros((), jnp.bfloat16)
    events = lax.axis_size("event")
    me, group = lax.axis_index("terrain"), lax.axis_index("event")
    terms = [
        pltpu.make_async_copy(floor_far, floor, local.at[0]),
        pltpu.make_async_copy(roof_far, roof, local.at[1]),
    ]
    for copy in terms:
        copy.start()
    barrier = pltpu.get_barrier_semaphore()
    for axis, size, mine in (("terrain", owners, me), ("event", events, group)):
        for hop in range(1, size):
            pl.semaphore_signal(
                barrier, inc=1, device_id={axis: lax.rem(mine + hop, size)}, device_id_type=MESH
            )
    for copy in terms:
        copy.wait()
    picked = (groups * share_rows, floor.shape[1])
    account = lax.broadcasted_iota(jnp.int32, picked, 1)
    mine = account == lax.broadcasted_iota(jnp.int32, picked, 0) + me * picked[0]
    for near, wide in ((floor, least), (roof, most)):
        column = jnp.sum(jnp.where(mine, near[...], 0.0), axis=1, keepdims=True)
        column = jnp.broadcast_to(column, (picked[0], bins))
        for h in range(groups):
            wide[h] = column[h * share_rows : (h + 1) * share_rows]
    pl.semaphore_wait(barrier, owners + events - 2)

    core, chip = lax.rem(me, 2), me // 2
    partner = me + 1 - 2 * core

    def remote(source, target, sent, received, axis, peer):
        return pltpu.make_async_remote_copy(
            src_ref=source,
            dst_ref=target,
            send_sem=sent,
            recv_sem=received,
            device_id={axis: peer},
            device_id_type=MESH,
        )

    def behind(k):
        return lax.rem(chip + chips - k, chips)

    def pair_copy(h):
        return remote(
            total.at[h, 1 - core], pairs.at[h], sent_pair.at[h], got_pair.at[h], "terrain", partner
        )

    def part_copy(h, k):
        to = lax.rem(chip + k, chips)
        return remote(
            both.at[h, to], parts.at[h, chip], sent_part.at[h, k], got_part.at[h, k],
            "terrain", 2 * to + core,
        )

    def low_copy(h, k):
        peer = 2 * lax.rem(chip + k, chips) + core if k else partner
        return remote(
            made_low.at[h], net_loss.at[me, h], sent_low.at[h, k], got_low.at[h, k],
            "terrain", peer,
        )

    def more_copy(h, k):
        block = net_loss.at[2 * behind(k) + core, h]
        return remote(block, block, sent_more.at[h, k], got_more.at[h, k], "terrain", partner)

    def net_copy(h, hop):
        return remote(
            made.at[h], arrived.at[group, h], sent_net.at[h, hop], got_net.at[h, hop],
            "event", lax.rem(group + hop, events),
        )

    def give(h):
        pair_copy(h).start()

    def spread(h):
        pair_copy(h).wait()
        both[h] = total[h, core] + pairs[h]
        for k in range(1, chips):
            part_copy(h, k).start()

    def finish(h):
        whole = both[h, chip]
        for k in range(1, chips):
            part_copy(h, k).wait()
            whole = whole + parts[h, behind(k)]
        net = jnp.minimum(jnp.maximum(whole * scale - least[h], 0.0), most[h])
        made[h] = net
        low = net.astype(made_low.dtype)
        made_low[h] = low
        net_loss[me, h] = low
        for hop in range(1, events):
            net_copy(h, hop).start()
        for k in range(1, chips):
            low_copy(h, k).start()
        low_copy(h, 0).start()

    def forward(h):
        for k in range(1, chips):
            low_copy(h, k).wait()
            more_copy(h, k).start()

    stages = ((give, 1), (spread, 2), (finish, 4), (forward, 6))

    account_id = numbered(group_size, cells, 0)
    bin_id = jnp.concatenate([numbered(16, bins, 1)] * (cells // 16), axis=0)
    span = min(SPAN, bundles)

    def one_group(h, _):
        for stage, lag in stages[::-1]:

            @pl.when(h >= lag)
            def _(stage=stage, lag=lag):
                stage(h - lag)

        rows = pl.ds(pl.multiple_of(h * group_size, group_size), group_size)
        turned = [lax.rem(e + groups - h, together) for e in range(together)]
        summed = None
        for c in range(bundles // span):
            left, right = [], []
            for block in range(span // CHUNK):
                first = c * span + block * CHUNK
                columns = jnp.transpose(bounds[h, first : first + CHUNK, :]).astype(jnp.bfloat16)
                for i in range(CHUNK):
                    bundle = first + i
                    left.append(
                        jnp.where(
                            rowed(lows[h, bundle : bundle + 1, :], group_size) == account_id,
                            rowed(values[h, bundle : bundle + 1, :], group_size),
                            zero,
                        )
                    )
                    shown = []
                    for e in range(together):
                        row = ratio[bundle, turned[e]]
                        shown.extend([row] * (capacity // 16))
                    bound = jnp.broadcast_to(columns[:, i : i + 1], (cells, bins))
                    right.append(
                        jnp.where(bin_id >= bound, jnp.concatenate(shown, axis=0), zero)
                    )
            part = jnp.dot(
                jnp.concatenate(left, axis=1),
                jnp.concatenate(right, axis=0),
                preferred_element_type=jnp.float32,
            )
            summed = part if summed is None else summed + part
        summed = summed + spill[rows, :]
        for t in range(owners):
            total[h, t % 2, t // 2] = summed[t * share_rows : (t + 1) * share_rows]

        return 0

    lax.fori_loop(0, groups, one_group, 0)
    for stage, lag in stages:
        for h in range(groups - lag, groups):
            stage(h)

    def close(h, _):
        whole = made[h]
        for hop in range(1, events):
            net_copy(h, hop).wait()
            whole = whole + arrived[lax.rem(group + events - hop, events), h]
        portfolio[h] = whole / events
        low_copy(h, 0).wait()
        for k in range(1, chips):
            more_copy(h, k).wait()
        return 0

    lax.fori_loop(0, groups, close, 0)


def settle(lows, bounds, values, ratio, spill, floor, roof, scale, number):
    account_count, bins = spill.shape
    groups = lows.shape[0]
    owners, events = lax.axis_size("terrain"), lax.axis_size("event")
    share = (groups, account_count // owners // groups, bins)
    chips = owners // 2
    pieces = (groups, chips) + share[1:]
    dma = pltpu.SemaphoreType.DMA
    return pl.pallas_call(
        functools.partial(settle_kernel, scale),
        out_shape=(
            jax.ShapeDtypeStruct((owners,) + share, jnp.bfloat16),
            jax.ShapeDtypeStruct(share, jnp.float32),
        ),
        in_specs=[VMEM] * 5 + [HBM] * 2,
        out_specs=(VMEM, VMEM),
        scratch_shapes=[pltpu.VMEM(floor.shape, floor.dtype)] * 2
        + [pltpu.VMEM(share, jnp.float32)] * 2
        + [pltpu.VMEM((groups, 2, chips) + share[1:], jnp.float32)]
        + [pltpu.VMEM(pieces, jnp.float32)] * 3
        + [
            pltpu.VMEM(share, jnp.float32),
            pltpu.VMEM(share, jnp.bfloat16),
            pltpu.VMEM((events,) + share, jnp.float32),
        ]
        + [dma((groups,))] * 2
        + [dma((groups, chips))] * 6
        + [dma((groups, events))] * 2
        + [dma((2,))],
        compiler_params=pltpu.CompilerParams(
            collective_id=number, has_side_effects=True, vmem_limit_bytes=LIMIT
        ),
        name="settle",
    )(lows, bounds, values, ratio, spill, *far([floor, roof]))


def per_device(
    level_start,
    bed_depth,
    wet_bits,
    tile_owner,
    vuln_weight,
    vuln_bias,
    account_index,
    bin_index,
    exposure_value,
    deductible,
    limit,
):
    _, rows, width = level_start.shape
    tile_cells, bin_count = vuln_weight.shape
    account_count = deductible.shape[0]
    owners = lax.axis_size("terrain")
    events = lax.axis_size("event")
    share_rows = account_count // owners
    tiles = rows * width // tile_cells
    level, ratio, low, bound, value = front(
        [level_start[0], bed_depth, wet_bits[0]],
        [account_index, bin_index, exposure_value],
        tile_owner.reshape(1, tiles),
        vuln_weight,
        vuln_bias[None, :],
        1,
    )
    scale = account_count / (rows * width * owners)
    *sorted_cells, level = sort(low, bound, value, ratio, level, account_count)
    net_loss, portfolio = settle(
        *sorted_cells, deductible[None, :], limit[None, :], scale, 2
    )
    portfolio = portfolio.reshape(share_rows, bin_count)
    return (level[None], net_loss.reshape(1, account_count, bin_count), portfolio)


def solution(mesh):
    placed = (
        P("event", "terrain", None),
        P("terrain", None),
        P("event", "terrain", None),
        P("terrain", None),
        P(),
        P(),
        P("terrain", None),
        P("terrain", None),
        P("terrain", None),
        P(),
        P(),
    )
    return jax.shard_map(
        per_device,
        mesh=mesh,
        in_specs=placed,
        out_specs=(P("event", "terrain", None), P("event", None, None), P("terrain", None)),
        check_vma=False,
    )
```

```python
import functools

import jax
import jax.numpy as jnp
from jax import lax
from jax.experimental import pallas as pl
from jax.experimental.pallas import tpu as pltpu
from jax.sharding import PartitionSpec as P

SUBSTEPS = 8
CHUNK = 8
LIMIT = 24 * 2**20
GROUPS = 8
SPAN = 32

courant = 0.5
gravity = 1.0

VMEM = pl.BlockSpec(memory_space=pltpu.VMEM)
HBM = pl.BlockSpec(memory_space=pltpu.HBM)
MESH = pl.DeviceIdType.MESH
PICK = lax.GatherDimensionNumbers(
    offset_dims=(),
    collapsed_slice_dims=(1,),
    start_index_map=(1,),
    operand_batching_dims=(0,),
    start_indices_batching_dims=(0,),
)


def far(arrays):
    return [pltpu.with_memory_space_constraint(a, pltpu.HBM) for a in arrays]


def padded(count, unit):
    return -(-count // unit) * unit


def front_kernel(
    level_far, bed_far, wet_far, account_far, threshold_far, value_far, owner_far, weight_far, bias_far,
    level_out, ratio_out, low_out, bin_out, value_out,
    level_here, bed_here, wet_here, account, threshold, value, owner_row, weight, bias, loads,
    made, kept, got, level_above, bed_above, wet_above, level_below, bed_below, wet_below,
    halo_sent, halo_got, cell_sent, cell_got, local,
):
    size = lax.axis_size("terrain")
    me = lax.axis_index("terrain")
    barrier = pltpu.get_barrier_semaphore()
    for hop in range(1, size):
        pl.semaphore_signal(
            barrier, inc=1, device_id={"terrain": lax.rem(me + hop, size)}, device_id_type=MESH
        )
    moved = (
        (account_far, account), (threshold_far, threshold), (value_far, value),
        (owner_far, owner_row), (level_far, level_here), (bed_far, bed_here), (wet_far, wet_here),
        (weight_far, weight), (bias_far, bias),
    )
    reads = [
        pltpu.make_async_copy(far, near, loads.at[n]) for n, (far, near) in enumerate(moved)
    ]
    for copy in reads:
        copy.start()
    for copy in reads[:4]:
        copy.wait()
    rows, width = level_here.shape
    capacity = account.shape[0] // size
    room = made.shape[2]

    accounts = account[...]
    low = (accounts & 255) - ((accounts >> 8) & 1) * 256
    bound = threshold[...] - (accounts >> 9) * 256
    fields = (low.astype(jnp.float32), bound.astype(jnp.float32), value[...].astype(jnp.float32))
    if room != capacity:
        made[...] = jnp.zeros(made.shape, made.dtype)
    for n in range(size):
        for f in range(3):
            made[n, f, :capacity, :] = fields[f][n * capacity : (n + 1) * capacity].astype(
                made.dtype
            )
    keep = pltpu.make_async_copy(made, kept, local.at[0])
    keep.start()
    pl.semaphore_wait(barrier, size - 1)

    later, earlier = lax.rem(me + 1, size), lax.rem(me + size - 1, size)
    strips = (level_far, bed_far, wet_far)
    above = (level_above, bed_above, wet_above)
    below = (level_below, bed_below, wet_below)
    edges = []
    for side, (peer, targets) in enumerate(((later, above), (earlier, below))):
        for i in range(3):
            first = 0 if side else rows - SUBSTEPS
            copy = pltpu.make_async_remote_copy(
                src_ref=strips[i].at[pl.ds(first, SUBSTEPS)],
                dst_ref=targets[i],
                send_sem=halo_sent.at[side * 3 + i],
                recv_sem=halo_got.at[side * 3 + i],
                device_id={"terrain": peer},
                device_id_type=MESH,
            )
            copy.start()
            edges.append(copy)
    keep.wait()
    cells = []
    for hop in range(1, size):
        peer = lax.rem(me + hop, size)
        copy = pltpu.make_async_remote_copy(
            src_ref=kept.at[peer],
            dst_ref=got.at[me],
            send_sem=cell_sent.at[hop],
            recv_sem=cell_got.at[hop],
            device_id={"terrain": peer},
            device_id_type=MESH,
        )
        copy.start()
        cells.append(copy)
    own = pltpu.make_async_copy(kept.at[me], got.at[me], local.at[1])
    own.start()
    cells.append(own)

    tile = weight.shape[0]
    blocks = width // tile
    tiles = rows * blocks
    number = lax.broadcasted_iota(jnp.int32, (tiles, tiles), 0)
    number = (number % rows) * blocks + number // rows
    along = lax.broadcasted_iota(jnp.int32, (tiles, tiles), 1)
    owner = owner_row[...].astype(jnp.float32)
    owner_column = jnp.sum(jnp.where(along == number, owner, 0.0), axis=1, keepdims=True)
    same = (owner_column == owner) & (along < number)
    rank = jnp.sum(jnp.where(same, 1.0, 0.0), axis=1, keepdims=True)
    slot = lax.broadcasted_iota(jnp.int32, (tiles, size * room), 1).astype(jnp.float32)
    chosen = jnp.where(slot == owner_column * room + rank, 1.0, 0.0).astype(jnp.bfloat16)

    for copy in reads[4:] + edges:
        copy.wait()
    first_row = me * rows - SUBSTEPS
    total_rows = rows * size
    level = jnp.concatenate([level_above[...], level_here[...], level_below[...]], axis=0)
    bed = jnp.concatenate([bed_above[...], bed_here[...], bed_below[...]], axis=0)
    wet = jnp.concatenate([wet_above[...], wet_here[...], wet_below[...]], axis=0)
    shape = level.shape
    tall = shape[0]
    row_id = first_row + lax.broadcasted_iota(jnp.int32, shape, 0)
    column = lax.broadcasted_iota(jnp.int32, shape, 1)
    inside = ((row_id >= 0) & (row_id < total_rows)).astype(jnp.float32)
    not_first = (column > 0).astype(jnp.float32)
    not_last = (column < width - 1).astype(jnp.float32)

    def down(field):
        return pltpu.roll(field, tall - 1, 0)

    def up(field):
        return pltpu.roll(field, 1, 0)

    def right(field):
        return pltpu.roll(field, width - 1, 1) * not_last

    def left(field):
        return pltpu.roll(field, 1, 1) * not_first

    quarter = 0.25
    assert courant * gravity == 0.5
    level = level * inside
    row_speed = jnp.zeros(shape, jnp.float32)
    col_speed = jnp.zeros(shape, jnp.float32)
    for step in range(SUBSTEPS):
        wet_factor = ((wet >> step) & 1).astype(jnp.float32) * (inside * quarter)
        if step:
            row_flow, col_flow = bed * row_speed, bed * col_speed
            new_level = (
                down(level - row_flow) + up(level + row_flow)
                + (right(level - col_flow) + left(level + col_flow))
            )
            new_row = (
                down(row_speed - level) + up(row_speed + level)
                + (right(row_speed) + left(row_speed))
            )
            new_col = (
                down(col_speed) + up(col_speed)
                + (right(col_speed - level) + left(col_speed + level))
            )
            row_speed, col_speed = new_row * wet_factor, new_col * wet_factor
        else:
            ld, lu, lr, ll = down(level), up(level), right(level), left(level)
            new_level = ld + lu + (lr + ll)
            row_speed = (lu - ld) * wet_factor
            col_speed = (ll - lr) * wet_factor
        level = new_level * (inside * quarter)
    level = level[SUBSTEPS : SUBSTEPS + rows]
    level_out[...] = level
    pieces = jnp.concatenate(
        [level[:, j * tile : (j + 1) * tile] for j in range(blocks)], axis=0
    ).astype(jnp.bfloat16)
    ratio_out[...] = jax.nn.sigmoid(
        jnp.dot(pieces, weight[...], preferred_element_type=jnp.float32) + bias[...]
    ).astype(jnp.bfloat16)
    for copy in cells:
        copy.wait()
    for f, target in enumerate((low_out, bin_out, value_out)):
        records = jnp.concatenate([got[n, f] for n in range(size)], axis=0)
        target[...] = jnp.dot(chosen, records, preferred_element_type=jnp.float32).astype(
            target.dtype
        )


def front(strips, records, owner_row, weight, bias, number):
    rows, width = strips[0].shape
    slots, cells = records[0].shape
    size = lax.axis_size("terrain")
    tiles = rows * width // cells
    packed = (size, 3, padded(slots // size, 16), cells)
    edge = (SUBSTEPS, width)
    inputs = strips + records + [owner_row, weight, bias]
    dma = pltpu.SemaphoreType.DMA
    edges = [pltpu.VMEM(edge, f.dtype) for f in strips]
    return pl.pallas_call(
        front_kernel,
        out_shape=(
            jax.ShapeDtypeStruct((rows, width), jnp.float32),
            jax.ShapeDtypeStruct((tiles, weight.shape[1]), jnp.bfloat16),
        )
        + (jax.ShapeDtypeStruct((tiles, cells), jnp.bfloat16),) * 3,
        in_specs=[HBM] * 9,
        out_specs=(VMEM,) * 5,
        scratch_shapes=[pltpu.VMEM(a.shape, a.dtype) for a in inputs]
        + [dma((9,))]
        + [pltpu.VMEM(packed, jnp.bfloat16)] * 3
        + edges * 2
        + [dma((6,))] * 2
        + [dma((size,))] * 2
        + [dma((2,))],
        compiler_params=pltpu.CompilerParams(
            collective_id=number, has_side_effects=True, vmem_limit_bytes=LIMIT
        ),
        name="front",
    )(*far(inputs))


def rowed(row, height):
    packed = jnp.broadcast_to(row, (16, row.shape[1])).astype(jnp.bfloat16)
    return jnp.concatenate([packed] * (height // 16), axis=0)


def over(number, power):
    assert power & (power - 1) == 0
    return number >> (power.bit_length() - 1)


def rest(number, power):
    assert power & (power - 1) == 0
    return number & (power - 1)


def numbered(height, width, axis):
    return (
        lax.broadcasted_iota(jnp.int32, (height, width), axis)
        .astype(jnp.float32)
        .astype(jnp.bfloat16)
    )


def sort_kernel(
    owners, low_in, bin_in, value_in, ratio_in, level_in,
    lows, bounds, values, ratio, total, level_out,
    ratio_all, low_all, bound_all, value_all, places, keys, worths,
):
    level_out[...] = level_in[...]
    total[...] = jnp.zeros(total.shape, jnp.float32)
    accounts, bins = total.shape
    tiles, cells = low_in.shape
    groups = lows.shape[0]
    group_size = accounts // groups
    capacity = 2 * cells // groups
    together = cells // capacity
    bundles = tiles // together
    zero = jnp.zeros((), jnp.bfloat16)

    ratio_all[...] = ratio_in[...].astype(jnp.float32)

    def widen(number, _):
        for u in range(8):
            for j in range(together):
                row = ratio_all[pl.ds((number * 8 + u) * together + j, 1), :]
                ratio[number * 8 + u, j] = jnp.broadcast_to(row, (16, bins)).astype(jnp.bfloat16)
        return 0

    lax.fori_loop(0, bundles // 8, widen, 0)

    low = low_in[...].astype(jnp.float32)
    bound = bin_in[...].astype(jnp.float32)
    value = value_in[...].astype(jnp.float32)
    high = jnp.where(low < 0, 256.0, 0.0) + jnp.where(bound < 0, 512.0, 0.0)
    account = (jnp.where(low < 0, low + 256.0, low) + high).astype(jnp.int32)
    bound = jnp.where(bound < 0, bound + 256.0, bound).astype(jnp.int32)
    share = accounts // owners
    rows = share // groups
    group = over(rest(account, share), rows)
    low = over(account, share) * rows + rest(account, rows)
    key = low * 256 + bound
    first = lax.broadcasted_iota(jnp.int32, (cells, cells), 0)
    second = lax.broadcasted_iota(jnp.int32, (cells, cells), 1)
    upto = jnp.where(first <= second, 1.0, 0.0).astype(jnp.bfloat16)

    def counted(h):
        mine = jnp.where(group == h, 1.0, 0.0).astype(jnp.bfloat16)
        return jnp.dot(mine, upto, preferred_element_type=jnp.float32)

    lane = lax.broadcasted_iota(jnp.int32, (tiles, cells), 1)
    turn = rest(lax.broadcasted_iota(jnp.int32, (tiles, cells), 0), together)
    wanted = rest(lane, capacity)
    shift = rest(over(lane, capacity) + together - turn, together) * 8
    largest = jnp.zeros((tiles, cells), jnp.float32)

    def taken(table, place):
        return lax.gather(
            table, place[..., None], PICK, (1, 1), mode=lax.GatherScatterMode.PROMISE_IN_BOUNDS
        )

    for q in range(2):
        table = jnp.zeros((tiles, cells), jnp.int32)
        for r in range(together):
            count = counted(q * together + r)
            largest = jnp.maximum(largest, count)
            table = table + lax.shift_left(count.astype(jnp.int32), 8 * r)

        def count_at(place):
            return lax.shift_right_logical(taken(table, place), shift) & 255

        place = jnp.zeros((tiles, cells), jnp.int32)
        step = cells // 2
        while step:
            place = jnp.where(count_at(place + (step - 1)) <= wanted, place + step, place)
            step //= 2
        keys[q] = taken(key, place)
        worths[q] = jnp.where(count_at(place) > wanted, taken(value, place), 0.0)

    block = over(lax.broadcasted_iota(jnp.int32, (bundles, cells), 1), capacity)
    for q in range(2):
        for r in range(together):
            for source, targets in ((keys, (lows, bounds)), (worths, (values,))):
                mixed = source[q, pl.ds((0 - r) % together, bundles, stride=together), :]
                for e in range(1, together):
                    part = source[q, pl.ds((e - r) % together, bundles, stride=together), :]
                    mixed = jnp.where(block == e, part, mixed)
                if len(targets) == 1:
                    values[q * together + r] = mixed
                else:
                    lows[q * together + r] = (mixed >> 8).astype(jnp.float32)
                    bounds[q * together + r] = (mixed & 255).astype(jnp.float32)

    @pl.when(jnp.max(largest) > capacity)
    def _():
        late = jnp.zeros((tiles, cells), jnp.float32)
        for h in range(groups):
            late = jnp.where((group == h) & (counted(h) > capacity), -1.0 - h, late)
        places[...] = late
        low_all[...] = low.astype(jnp.float32)
        bound_all[...] = bound.astype(jnp.float32)
        value_all[...] = value
        account_id = numbered(group_size, cells, 0)
        bin_id = jnp.concatenate([numbered(16, bins, 1)] * (cells // 16), axis=0)
        tile_id = lax.broadcasted_iota(jnp.int32, (tiles, cells), 0).astype(jnp.float32)

        def dense(left_over):
            t = left_over.astype(jnp.int32)
            place = places[pl.ds(t, 1), :]
            worth = jnp.where(place < 0, value_all[pl.ds(t, 1), :], 0.0)
            hit = rowed(low_all[pl.ds(t, 1), :], group_size) == account_id
            columns = jnp.transpose(jnp.broadcast_to(bound_all[pl.ds(t, 1), :], (8, cells)))
            right = jnp.where(
                bin_id >= jnp.broadcast_to(columns.astype(jnp.bfloat16)[:, 0:1], (cells, bins)),
                rowed(ratio_all[pl.ds(t, 1), :], cells),
                zero,
            )
            for h in range(groups):
                part = jnp.where(place == -1.0 - h, worth, 0.0)
                left = jnp.where(hit, rowed(part, group_size), zero)
                total[pl.ds(h * group_size, group_size), :] += jnp.dot(
                    left, right, preferred_element_type=jnp.float32
                )
            return jnp.max(jnp.where((places[...] < 0) & (tile_id < left_over), tile_id, -1.0))

        lax.while_loop(
            lambda t: t >= 0, dense, jnp.max(jnp.where(places[...] < 0, tile_id, -1.0))
        )


def sort(low, bound, value, ratio, level, account_count):
    tiles, cells = low.shape
    bins = ratio.shape[1]
    together = GROUPS // 2
    bundles = tiles // together
    gathered = jax.ShapeDtypeStruct((GROUPS, bundles, cells), jnp.float32)
    whole = pltpu.VMEM((tiles, cells), jnp.float32)
    return pl.pallas_call(
        functools.partial(sort_kernel, lax.axis_size("terrain")),
        out_shape=(
            gathered,
            gathered,
            gathered,
            jax.ShapeDtypeStruct((bundles, together, 16, bins), jnp.bfloat16),
            jax.ShapeDtypeStruct((account_count, bins), jnp.float32),
            jax.ShapeDtypeStruct(level.shape, level.dtype),
        ),
        in_specs=[VMEM] * 5,
        out_specs=(VMEM,) * 6,
        scratch_shapes=[pltpu.VMEM((tiles, bins), jnp.float32)]
        + [whole] * 4
        + [pltpu.VMEM((2, tiles, cells), dtype) for dtype in (jnp.int32, jnp.float32)],
        compiler_params=pltpu.CompilerParams(vmem_limit_bytes=LIMIT),
        name="sort",
    )(low, bound, value, ratio, level)


def settle_kernel(
    scale, lows, bounds, values, ratio, spill, floor_far, roof_far,
    net_loss, portfolio,
    floor, roof, least, most, total, pairs, both, parts, made, made_low, arrived,
    sent_pair, got_pair, sent_part, got_part, sent_low, got_low, sent_more, got_more,
    sent_net, got_net, local,
):
    groups, _, chips, share_rows, bins = total.shape
    owners = 2 * chips
    _, bundles, cells = lows.shape
    group_size = owners * share_rows
    capacity = 2 * cells // groups
    together = cells // capacity
    zero = jnp.zeros((), jnp.bfloat16)
    events = lax.axis_size("event")
    me, group = lax.axis_index("terrain"), lax.axis_index("event")
    terms = [
        pltpu.make_async_copy(floor_far, floor, local.at[0]),
        pltpu.make_async_copy(roof_far, roof, local.at[1]),
    ]
    for copy in terms:
        copy.start()
    barrier = pltpu.get_barrier_semaphore()
    for axis, size, mine in (("terrain", owners, me), ("event", events, group)):
        for hop in range(1, size):
            pl.semaphore_signal(
                barrier, inc=1, device_id={axis: lax.rem(mine + hop, size)}, device_id_type=MESH
            )
    for copy in terms:
        copy.wait()
    picked = (groups * share_rows, floor.shape[1])
    account = lax.broadcasted_iota(jnp.int32, picked, 1)
    mine = account == lax.broadcasted_iota(jnp.int32, picked, 0) + me * picked[0]
    for near, wide in ((floor, least), (roof, most)):
        column = jnp.sum(jnp.where(mine, near[...], 0.0), axis=1, keepdims=True)
        column = jnp.broadcast_to(column, (picked[0], bins))
        for h in range(groups):
            wide[h] = column[h * share_rows : (h + 1) * share_rows]
    core, chip = lax.rem(me, 2), me // 2
    partner = me + 1 - 2 * core

    def remote(source, target, sent, received, axis, peer):
        return pltpu.make_async_remote_copy(
            src_ref=source,
            dst_ref=target,
            send_sem=sent,
            recv_sem=received,
            device_id={axis: peer},
            device_id_type=MESH,
        )

    def behind(k):
        return lax.rem(chip + chips - k, chips)

    def pair_copy(h):
        return remote(
            total.at[h, 1 - core], pairs.at[h], sent_pair.at[h], got_pair.at[h], "terrain", partner
        )

    def part_copy(h, k):
        to = lax.rem(chip + k, chips)
        return remote(
            both.at[h, to], parts.at[h, chip], sent_part.at[h, k], got_part.at[h, k],
            "terrain", 2 * to + core,
        )

    def low_copy(h, k):
        peer = 2 * lax.rem(chip + k, chips) + core if k else partner
        return remote(
            made_low.at[h], net_loss.at[me, h], sent_low.at[h, k], got_low.at[h, k],
            "terrain", peer,
        )

    def more_copy(h, k):
        block = net_loss.at[2 * behind(k) + core, h]
        return remote(block, block, sent_more.at[h, k], got_more.at[h, k], "terrain", partner)

    def net_copy(h, hop):
        return remote(
            made.at[h], arrived.at[group, h], sent_net.at[h, hop], got_net.at[h, hop],
            "event", lax.rem(group + hop, events),
        )

    def give(h):
        pair_copy(h).start()

    def spread(h):
        pair_copy(h).wait()
        both[h] = total[h, core] + pairs[h]
        for k in range(1, chips):
            part_copy(h, k).start()

    def finish(h):
        whole = both[h, chip]
        for k in range(1, chips):
            part_copy(h, k).wait()
            whole = whole + parts[h, behind(k)]
        net = jnp.minimum(jnp.maximum(whole * scale - least[h], 0.0), most[h])
        made[h] = net
        low = net.astype(made_low.dtype)
        made_low[h] = low
        net_loss[me, h] = low
        for hop in range(1, events):
            net_copy(h, hop).start()
        for k in range(1, chips):
            low_copy(h, k).start()
        low_copy(h, 0).start()

    def forward(h):
        for k in range(1, chips):
            low_copy(h, k).wait()
            more_copy(h, k).start()

    stages = ((give, 1), (spread, 2), (finish, 4), (forward, 6))

    account_id = numbered(group_size, cells, 0)
    bin_id = jnp.concatenate([numbered(16, bins, 1)] * (cells // 16), axis=0)
    span = min(SPAN, bundles)

    def one_group(h, _):
        @pl.when(h == 1)
        def _():
            pl.semaphore_wait(barrier, owners + events - 2)

        for stage, lag in stages[::-1]:

            @pl.when(h >= lag)
            def _(stage=stage, lag=lag):
                stage(h - lag)

        rows = pl.ds(pl.multiple_of(h * group_size, group_size), group_size)
        turned = [lax.rem(e + groups - h, together) for e in range(together)]
        summed = None
        for c in range(bundles // span):
            left, right = [], []
            for block in range(span // CHUNK):
                first = c * span + block * CHUNK
                columns = jnp.transpose(bounds[h, first : first + CHUNK, :]).astype(jnp.bfloat16)
                for i in range(CHUNK):
                    bundle = first + i
                    left.append(
                        jnp.where(
                            rowed(lows[h, bundle : bundle + 1, :], group_size) == account_id,
                            rowed(values[h, bundle : bundle + 1, :], group_size),
                            zero,
                        )
                    )
                    shown = []
                    for e in range(together):
                        row = ratio[bundle, turned[e]]
                        shown.extend([row] * (capacity // 16))
                    bound = jnp.broadcast_to(columns[:, i : i + 1], (cells, bins))
                    right.append(
                        jnp.where(bin_id >= bound, jnp.concatenate(shown, axis=0), zero)
                    )
            part = jnp.dot(
                jnp.concatenate(left, axis=1),
                jnp.concatenate(right, axis=0),
                preferred_element_type=jnp.float32,
            )
            summed = part if summed is None else summed + part
        summed = summed + spill[rows, :]
        for t in range(owners):
            total[h, t % 2, t // 2] = summed[t * share_rows : (t + 1) * share_rows]

        return 0

    lax.fori_loop(0, groups, one_group, 0)
    for stage, lag in stages:
        for h in range(groups - lag, groups):
            stage(h)

    def close(h, _):
        whole = made[h]
        for hop in range(1, events):
            net_copy(h, hop).wait()
            whole = whole + arrived[lax.rem(group + events - hop, events), h]
        portfolio[h] = whole / events
        low_copy(h, 0).wait()
        for k in range(1, chips):
            more_copy(h, k).wait()
        return 0

    lax.fori_loop(0, groups, close, 0)


def settle(lows, bounds, values, ratio, spill, floor, roof, scale, number):
    account_count, bins = spill.shape
    groups = lows.shape[0]
    owners, events = lax.axis_size("terrain"), lax.axis_size("event")
    share = (groups, account_count // owners // groups, bins)
    chips = owners // 2
    pieces = (groups, chips) + share[1:]
    dma = pltpu.SemaphoreType.DMA
    return pl.pallas_call(
        functools.partial(settle_kernel, scale),
        out_shape=(
            jax.ShapeDtypeStruct((owners,) + share, jnp.bfloat16),
            jax.ShapeDtypeStruct(share, jnp.float32),
        ),
        in_specs=[VMEM] * 5 + [HBM] * 2,
        out_specs=(VMEM, VMEM),
        scratch_shapes=[pltpu.VMEM(floor.shape, floor.dtype)] * 2
        + [pltpu.VMEM(share, jnp.float32)] * 2
        + [pltpu.VMEM((groups, 2, chips) + share[1:], jnp.float32)]
        + [pltpu.VMEM(pieces, jnp.float32)] * 3
        + [
            pltpu.VMEM(share, jnp.float32),
            pltpu.VMEM(share, jnp.bfloat16),
            pltpu.VMEM((events,) + share, jnp.float32),
        ]
        + [dma((groups,))] * 2
        + [dma((groups, chips))] * 6
        + [dma((groups, events))] * 2
        + [dma((2,))],
        compiler_params=pltpu.CompilerParams(
            collective_id=number, has_side_effects=True, vmem_limit_bytes=LIMIT
        ),
        name="settle",
    )(lows, bounds, values, ratio, spill, *far([floor, roof]))


def place_kernel(*refs):
    sems = refs[-1]
    count = len(refs) // 2
    copies = [
        pltpu.make_async_copy(refs[n], refs[count + n], sems.at[n]) for n in range(count)
    ]
    for copy in copies:
        copy.start()
    for copy in copies:
        copy.wait()


def place(arrays):
    return pl.pallas_call(
        place_kernel,
        out_shape=[jax.ShapeDtypeStruct(a.shape, a.dtype) for a in arrays],
        in_specs=[pl.BlockSpec(memory_space=pl.ANY)] * len(arrays),
        out_specs=[HBM] * len(arrays),
        scratch_shapes=[pltpu.SemaphoreType.DMA((len(arrays),))],
        compiler_params=pltpu.CompilerParams(vmem_limit_bytes=2**20),
        name="place",
    )(*arrays)


def per_device(
    level_start,
    bed_depth,
    wet_bits,
    tile_owner,
    vuln_weight,
    vuln_bias,
    account_index,
    bin_index,
    exposure_value,
    deductible,
    limit,
):
    _, rows, width = level_start.shape
    tile_cells, bin_count = vuln_weight.shape
    account_count = deductible.shape[0]
    owners = lax.axis_size("terrain")
    events = lax.axis_size("event")
    share_rows = account_count // owners
    tiles = rows * width // tile_cells
    level, ratio, low, bound, value = front(
        [level_start[0], bed_depth, wet_bits[0]],
        [account_index, bin_index, exposure_value],
        tile_owner.reshape(1, tiles),
        vuln_weight,
        vuln_bias[None, :],
        1,
    )
    scale = account_count / (rows * width * owners)
    *sorted_cells, level = sort(low, bound, value, ratio, level, account_count)
    net_loss, portfolio = settle(
        *sorted_cells, deductible[None, :], limit[None, :], scale, 2
    )
    net_loss, portfolio = place([net_loss, portfolio])
    portfolio = portfolio.reshape(share_rows, bin_count)
    return (level[None], net_loss.reshape(1, account_count, bin_count), portfolio)


def solution(mesh):
    placed = (
        P("event", "terrain", None),
        P("terrain", None),
        P("event", "terrain", None),
        P("terrain", None),
        P(),
        P(),
        P("terrain", None),
        P("terrain", None),
        P("terrain", None),
        P(),
        P(),
    )
    return jax.shard_map(
        per_device,
        mesh=mesh,
        in_specs=placed,
        out_specs=(P("event", "terrain", None), P("event", None, None), P("terrain", None)),
        check_vma=False,
    )
```

```python
import functools

import jax
import jax.numpy as jnp
from jax import lax
from jax.experimental import pallas as pl
from jax.experimental.pallas import tpu as pltpu
from jax.sharding import PartitionSpec as P

SUBSTEPS = 8
CHUNK = 8
LIMIT = 24 * 2**20
GROUPS = 8
SPAN = 32

courant = 0.5
gravity = 1.0

VMEM = pl.BlockSpec(memory_space=pltpu.VMEM)
HBM = pl.BlockSpec(memory_space=pltpu.HBM)
MESH = pl.DeviceIdType.MESH
PICK = lax.GatherDimensionNumbers(
    offset_dims=(),
    collapsed_slice_dims=(1,),
    start_index_map=(1,),
    operand_batching_dims=(0,),
    start_indices_batching_dims=(0,),
)


def far(arrays):
    return [pltpu.with_memory_space_constraint(a, pltpu.HBM) for a in arrays]


def padded(count, unit):
    return -(-count // unit) * unit


def front_kernel(
    level_far, bed_far, wet_far, account_far, threshold_far, value_far, owner_far, weight_far, bias_far,
    level_out, ratio_out, low_out, bin_out, value_out,
    level_here, bed_here, wet_here, account, threshold, value, owner_row, weight, bias, loads,
    made, kept, got, level_above, bed_above, wet_above, level_below, bed_below, wet_below,
    factors, halo_sent, halo_got, cell_sent, cell_got, local,
):
    size = lax.axis_size("terrain")
    me = lax.axis_index("terrain")
    barrier = pltpu.get_barrier_semaphore()
    for hop in range(1, size):
        pl.semaphore_signal(
            barrier, inc=1, device_id={"terrain": lax.rem(me + hop, size)}, device_id_type=MESH
        )
    moved = (
        (account_far, account), (threshold_far, threshold), (value_far, value),
        (owner_far, owner_row), (level_far, level_here), (bed_far, bed_here), (wet_far, wet_here),
        (weight_far, weight), (bias_far, bias),
    )
    reads = [
        pltpu.make_async_copy(far, near, loads.at[n]) for n, (far, near) in enumerate(moved)
    ]
    for copy in reads:
        copy.start()
    for copy in reads[:4]:
        copy.wait()
    rows, width = level_here.shape
    capacity = account.shape[0] // size
    room = made.shape[2]

    accounts = account[...]
    low = (accounts & 255) - ((accounts >> 8) & 1) * 256
    bound = threshold[...] - (accounts >> 9) * 256
    fields = (low.astype(jnp.float32), bound.astype(jnp.float32), value[...].astype(jnp.float32))
    if room != capacity:
        made[...] = jnp.zeros(made.shape, made.dtype)
    for n in range(size):
        for f in range(3):
            made[n, f, :capacity, :] = fields[f][n * capacity : (n + 1) * capacity].astype(
                made.dtype
            )
    keep = pltpu.make_async_copy(made, kept, local.at[0])
    keep.start()
    pl.semaphore_wait(barrier, size - 1)

    later, earlier = lax.rem(me + 1, size), lax.rem(me + size - 1, size)
    strips = (level_far, bed_far, wet_far)
    above = (level_above, bed_above, wet_above)
    below = (level_below, bed_below, wet_below)
    edges = []
    for side, (peer, targets) in enumerate(((later, above), (earlier, below))):
        for i in range(3):
            first = 0 if side else rows - SUBSTEPS
            copy = pltpu.make_async_remote_copy(
                src_ref=strips[i].at[pl.ds(first, SUBSTEPS)],
                dst_ref=targets[i],
                send_sem=halo_sent.at[side * 3 + i],
                recv_sem=halo_got.at[side * 3 + i],
                device_id={"terrain": peer},
                device_id_type=MESH,
            )
            copy.start()
            edges.append(copy)
    keep.wait()
    cells = []
    for hop in range(1, size):
        peer = lax.rem(me + hop, size)
        copy = pltpu.make_async_remote_copy(
            src_ref=kept.at[peer],
            dst_ref=got.at[me],
            send_sem=cell_sent.at[hop],
            recv_sem=cell_got.at[hop],
            device_id={"terrain": peer},
            device_id_type=MESH,
        )
        copy.start()
        cells.append(copy)
    own = pltpu.make_async_copy(kept.at[me], got.at[me], local.at[1])
    own.start()
    cells.append(own)

    tile = weight.shape[0]
    blocks = width // tile
    tiles = rows * blocks
    number = lax.broadcasted_iota(jnp.int32, (tiles, tiles), 0)
    number = (number % rows) * blocks + number // rows
    along = lax.broadcasted_iota(jnp.int32, (tiles, tiles), 1)
    owner = owner_row[...].astype(jnp.float32)
    owner_column = jnp.sum(jnp.where(along == number, owner, 0.0), axis=1, keepdims=True)
    same = (owner_column == owner) & (along < number)
    rank = jnp.sum(jnp.where(same, 1.0, 0.0), axis=1, keepdims=True)
    slot = lax.broadcasted_iota(jnp.int32, (tiles, size * room), 1).astype(jnp.float32)
    chosen = jnp.where(slot == owner_column * room + rank, 1.0, 0.0).astype(jnp.bfloat16)

    for copy in reads[4:]:
        copy.wait()
    assert courant * gravity == 0.5
    quarter = 0.25
    tall = rows + 2 * SUBSTEPS
    first_row = me * rows - SUBSTEPS
    total_rows = rows * size

    def inner(first, count):
        row = first_row + first + lax.broadcasted_iota(jnp.int32, (count, tile), 0)
        return jnp.where((row >= 0) & (row < total_rows), quarter, 0.0)

    def mark(bits, first):
        for j in range(blocks):
            span = slice(j * tile, (j + 1) * tile)
            here = bits[:, span]
            weight_here = inner(first, bits.shape[0])
            for step in range(SUBSTEPS):
                factor = jnp.where((here & (1 << step)) != 0, weight_here, 0.0)
                factors[step, j, first : first + bits.shape[0], :] = factor

    mark(wet_here, SUBSTEPS)
    for copy in edges:
        copy.wait()
    mark(wet_above, 0)
    mark(wet_below, SUBSTEPS + rows)
    lane = lax.broadcasted_iota(jnp.int32, (tall, tile), 1)
    at_first, at_last = lane == 0, lane == tile - 1
    inside = inner(0, tall)

    def stacked(above, here, below):
        whole = jnp.concatenate([above[...], here[...], below[...]], axis=0)
        return [whole[:, j * tile : (j + 1) * tile] for j in range(blocks)]

    level = stacked(level_above, level_here, level_below)
    bed = stacked(bed_above, bed_here, bed_below)
    level = [jnp.where(inside > 0, field, 0.0) for field in level]

    def down(field):
        return pltpu.roll(field, tall - 1, 0)

    def up(field):
        return pltpu.roll(field, 1, 0)

    def right(fields):
        turned = [pltpu.roll(field, tile - 1, 1) for field in fields] + [0.0]
        return [jnp.where(at_last, turned[j + 1], turned[j]) for j in range(blocks)]

    def left(fields):
        turned = [0.0] + [pltpu.roll(field, 1, 1) for field in fields]
        return [jnp.where(at_first, turned[j], turned[j + 1]) for j in range(blocks)]

    def each(function, *fields):
        return [function(*of_block) for of_block in zip(*fields)]

    def plus(one, other):
        return each(lambda a, b: a + b, one, other)

    def minus(one, other):
        return each(lambda a, b: a - b, one, other)

    for step in range(SUBSTEPS):
        factor = [factors[step, j] for j in range(blocks)]
        if step:
            row_flow = each(lambda a, b: a * b, bed, row_speed)
            col_flow = each(lambda a, b: a * b, bed, col_speed)
            new_level = each(
                lambda d, u, r, l: (down(d) + up(u) + (r + l)) * inside,
                minus(level, row_flow), plus(level, row_flow),
                right(minus(level, col_flow)), left(plus(level, col_flow)),
            )
            new_row = each(
                lambda d, u, r, l, f: (down(d) + up(u) + (r + l)) * f,
                minus(row_speed, level), plus(row_speed, level),
                right(row_speed), left(row_speed), factor,
            )
            col_speed = each(
                lambda c, r, l, f: (down(c) + up(c) + (r + l)) * f,
                col_speed, right(minus(col_speed, level)), left(plus(col_speed, level)), factor,
            )
            row_speed = new_row
        else:
            beside, before = right(level), left(level)
            new_level = each(
                lambda c, r, l: (down(c) + up(c) + (r + l)) * inside, level, beside, before
            )
            row_speed = each(lambda c, f: (up(c) - down(c)) * f, level, factor)
            col_speed = each(lambda r, l, f: (l - r) * f, beside, before, factor)
        level = new_level
    level = [field[SUBSTEPS : SUBSTEPS + rows] for field in level]
    for j in range(blocks):
        level_out[:, j * tile : (j + 1) * tile] = level[j]
    pieces = jnp.concatenate(level, axis=0).astype(jnp.bfloat16)
    ratio_out[...] = jax.nn.sigmoid(
        jnp.dot(pieces, weight[...], preferred_element_type=jnp.float32) + bias[...]
    ).astype(jnp.bfloat16)
    for copy in cells:
        copy.wait()
    for f, target in enumerate((low_out, bin_out, value_out)):
        records = jnp.concatenate([got[n, f] for n in range(size)], axis=0)
        target[...] = jnp.dot(chosen, records, preferred_element_type=jnp.float32).astype(
            target.dtype
        )


def front(strips, records, owner_row, weight, bias, number):
    rows, width = strips[0].shape
    slots, cells = records[0].shape
    size = lax.axis_size("terrain")
    tiles = rows * width // cells
    packed = (size, 3, padded(slots // size, 16), cells)
    edge = (SUBSTEPS, width)
    inputs = strips + records + [owner_row, weight, bias]
    dma = pltpu.SemaphoreType.DMA
    edges = [pltpu.VMEM(edge, f.dtype) for f in strips]
    return pl.pallas_call(
        front_kernel,
        out_shape=(
            jax.ShapeDtypeStruct((rows, width), jnp.float32),
            jax.ShapeDtypeStruct((tiles, weight.shape[1]), jnp.bfloat16),
        )
        + (jax.ShapeDtypeStruct((tiles, cells), jnp.bfloat16),) * 3,
        in_specs=[HBM] * 9,
        out_specs=(VMEM,) * 5,
        scratch_shapes=[pltpu.VMEM(a.shape, a.dtype) for a in inputs]
        + [dma((9,))]
        + [pltpu.VMEM(packed, jnp.bfloat16)] * 3
        + edges * 2
        + [pltpu.VMEM((SUBSTEPS, width // cells, rows + 2 * SUBSTEPS, cells), jnp.float32)]
        + [dma((6,))] * 2
        + [dma((size,))] * 2
        + [dma((2,))],
        compiler_params=pltpu.CompilerParams(
            collective_id=number, has_side_effects=True, vmem_limit_bytes=LIMIT
        ),
        name="front",
    )(*far(inputs))


def rowed(row, height):
    packed = jnp.broadcast_to(row, (16, row.shape[1])).astype(jnp.bfloat16)
    return jnp.concatenate([packed] * (height // 16), axis=0)


def over(number, power):
    assert power & (power - 1) == 0
    return number >> (power.bit_length() - 1)


def rest(number, power):
    assert power & (power - 1) == 0
    return number & (power - 1)


def numbered(height, width, axis):
    return (
        lax.broadcasted_iota(jnp.int32, (height, width), axis)
        .astype(jnp.float32)
        .astype(jnp.bfloat16)
    )


def sort_kernel(
    owners, low_in, bin_in, value_in, ratio_in, level_in,
    lows, bounds, values, ratio, total, level_out,
    ratio_all, low_all, bound_all, value_all, places, keys, worths,
):
    level_out[...] = level_in[...]
    total[...] = jnp.zeros(total.shape, jnp.float32)
    accounts, bins = total.shape
    tiles, cells = low_in.shape
    groups = lows.shape[0]
    group_size = accounts // groups
    capacity = 2 * cells // groups
    together = cells // capacity
    bundles = tiles // together
    zero = jnp.zeros((), jnp.bfloat16)

    ratio_all[...] = ratio_in[...].astype(jnp.float32)

    def widen(number, _):
        for u in range(8):
            for j in range(together):
                row = ratio_all[pl.ds((number * 8 + u) * together + j, 1), :]
                ratio[number * 8 + u, j] = jnp.broadcast_to(row, (16, bins)).astype(jnp.bfloat16)
        return 0

    lax.fori_loop(0, bundles // 8, widen, 0)

    low = low_in[...].astype(jnp.float32)
    bound = bin_in[...].astype(jnp.float32)
    value = value_in[...].astype(jnp.float32)
    high = jnp.where(low < 0, 256.0, 0.0) + jnp.where(bound < 0, 512.0, 0.0)
    account = (jnp.where(low < 0, low + 256.0, low) + high).astype(jnp.int32)
    bound = jnp.where(bound < 0, bound + 256.0, bound).astype(jnp.int32)
    share = accounts // owners
    rows = share // groups
    group = over(rest(account, share), rows)
    low = over(account, share) * rows + rest(account, rows)
    key = low * 256 + bound
    first = lax.broadcasted_iota(jnp.int32, (cells, cells), 0)
    second = lax.broadcasted_iota(jnp.int32, (cells, cells), 1)
    upto = jnp.where(first <= second, 1.0, 0.0).astype(jnp.bfloat16)

    def counted(h):
        mine = jnp.where(group == h, 1.0, 0.0).astype(jnp.bfloat16)
        return jnp.dot(mine, upto, preferred_element_type=jnp.float32)

    lane = lax.broadcasted_iota(jnp.int32, (tiles, cells), 1)
    turn = rest(lax.broadcasted_iota(jnp.int32, (tiles, cells), 0), together)
    wanted = rest(lane, capacity)
    shift = rest(over(lane, capacity) + together - turn, together) * 8
    largest = jnp.zeros((tiles, cells), jnp.float32)

    def taken(table, place):
        return lax.gather(
            table, place[..., None], PICK, (1, 1), mode=lax.GatherScatterMode.PROMISE_IN_BOUNDS
        )

    for q in range(2):
        table = jnp.zeros((tiles, cells), jnp.int32)
        for r in range(together):
            count = counted(q * together + r)
            largest = jnp.maximum(largest, count)
            table = table + lax.shift_left(count.astype(jnp.int32), 8 * r)

        def count_at(place):
            return lax.shift_right_logical(taken(table, place), shift) & 255

        place = jnp.zeros((tiles, cells), jnp.int32)
        step = cells // 2
        while step:
            place = jnp.where(count_at(place + (step - 1)) <= wanted, place + step, place)
            step //= 2
        keys[q] = taken(key, place)
        worths[q] = jnp.where(count_at(place) > wanted, taken(value, place), 0.0)

    block = over(lax.broadcasted_iota(jnp.int32, (bundles, cells), 1), capacity)
    for q in range(2):
        for r in range(together):
            for source, targets in ((keys, (lows, bounds)), (worths, (values,))):
                mixed = source[q, pl.ds((0 - r) % together, bundles, stride=together), :]
                for e in range(1, together):
                    part = source[q, pl.ds((e - r) % together, bundles, stride=together), :]
                    mixed = jnp.where(block == e, part, mixed)
                if len(targets) == 1:
                    values[q * together + r] = mixed
                else:
                    lows[q * together + r] = (mixed >> 8).astype(jnp.float32)
                    bounds[q * together + r] = (mixed & 255).astype(jnp.float32)

    @pl.when(jnp.max(largest) > capacity)
    def _():
        late = jnp.zeros((tiles, cells), jnp.float32)
        for h in range(groups):
            late = jnp.where((group == h) & (counted(h) > capacity), -1.0 - h, late)
        places[...] = late
        low_all[...] = low.astype(jnp.float32)
        bound_all[...] = bound.astype(jnp.float32)
        value_all[...] = value
        account_id = numbered(group_size, cells, 0)
        bin_id = jnp.concatenate([numbered(16, bins, 1)] * (cells // 16), axis=0)
        tile_id = lax.broadcasted_iota(jnp.int32, (tiles, cells), 0).astype(jnp.float32)

        def dense(left_over):
            t = left_over.astype(jnp.int32)
            place = places[pl.ds(t, 1), :]
            worth = jnp.where(place < 0, value_all[pl.ds(t, 1), :], 0.0)
            hit = rowed(low_all[pl.ds(t, 1), :], group_size) == account_id
            columns = jnp.transpose(jnp.broadcast_to(bound_all[pl.ds(t, 1), :], (8, cells)))
            right = jnp.where(
                bin_id >= jnp.broadcast_to(columns.astype(jnp.bfloat16)[:, 0:1], (cells, bins)),
                rowed(ratio_all[pl.ds(t, 1), :], cells),
                zero,
            )
            for h in range(groups):
                part = jnp.where(place == -1.0 - h, worth, 0.0)
                left = jnp.where(hit, rowed(part, group_size), zero)
                total[pl.ds(h * group_size, group_size), :] += jnp.dot(
                    left, right, preferred_element_type=jnp.float32
                )
            return jnp.max(jnp.where((places[...] < 0) & (tile_id < left_over), tile_id, -1.0))

        lax.while_loop(
            lambda t: t >= 0, dense, jnp.max(jnp.where(places[...] < 0, tile_id, -1.0))
        )


def sort(low, bound, value, ratio, level, account_count):
    tiles, cells = low.shape
    bins = ratio.shape[1]
    together = GROUPS // 2
    bundles = tiles // together
    gathered = jax.ShapeDtypeStruct((GROUPS, bundles, cells), jnp.float32)
    whole = pltpu.VMEM((tiles, cells), jnp.float32)
    return pl.pallas_call(
        functools.partial(sort_kernel, lax.axis_size("terrain")),
        out_shape=(
            gathered,
            gathered,
            gathered,
            jax.ShapeDtypeStruct((bundles, together, 16, bins), jnp.bfloat16),
            jax.ShapeDtypeStruct((account_count, bins), jnp.float32),
            jax.ShapeDtypeStruct(level.shape, level.dtype),
        ),
        in_specs=[VMEM] * 5,
        out_specs=(VMEM,) * 6,
        scratch_shapes=[pltpu.VMEM((tiles, bins), jnp.float32)]
        + [whole] * 4
        + [pltpu.VMEM((2, tiles, cells), dtype) for dtype in (jnp.int32, jnp.float32)],
        compiler_params=pltpu.CompilerParams(vmem_limit_bytes=LIMIT),
        name="sort",
    )(low, bound, value, ratio, level)


def settle_kernel(
    scale, lows, bounds, values, ratio, spill, floor_far, roof_far,
    net_loss, portfolio,
    floor, roof, least, most, total, pairs, both, parts, made, made_low, arrived,
    sent_pair, got_pair, sent_part, got_part, sent_low, got_low, sent_more, got_more,
    sent_net, got_net, local,
):
    groups, _, chips, share_rows, bins = total.shape
    owners = 2 * chips
    _, bundles, cells = lows.shape
    group_size = owners * share_rows
    capacity = 2 * cells // groups
    together = cells // capacity
    zero = jnp.zeros((), jnp.bfloat16)
    events = lax.axis_size("event")
    me, group = lax.axis_index("terrain"), lax.axis_index("event")
    terms = [
        pltpu.make_async_copy(floor_far, floor, local.at[0]),
        pltpu.make_async_copy(roof_far, roof, local.at[1]),
    ]
    for copy in terms:
        copy.start()
    barrier = pltpu.get_barrier_semaphore()
    for axis, size, mine in (("terrain", owners, me), ("event", events, group)):
        for hop in range(1, size):
            pl.semaphore_signal(
                barrier, inc=1, device_id={axis: lax.rem(mine + hop, size)}, device_id_type=MESH
            )
    for copy in terms:
        copy.wait()
    picked = (groups * share_rows, floor.shape[1])
    account = lax.broadcasted_iota(jnp.int32, picked, 1)
    mine = account == lax.broadcasted_iota(jnp.int32, picked, 0) + me * picked[0]
    for near, wide in ((floor, least), (roof, most)):
        column = jnp.sum(jnp.where(mine, near[...], 0.0), axis=1, keepdims=True)
        column = jnp.broadcast_to(column, (picked[0], bins))
        for h in range(groups):
            wide[h] = column[h * share_rows : (h + 1) * share_rows]
    core, chip = lax.rem(me, 2), me // 2
    partner = me + 1 - 2 * core

    def remote(source, target, sent, received, axis, peer):
        return pltpu.make_async_remote_copy(
            src_ref=source,
            dst_ref=target,
            send_sem=sent,
            recv_sem=received,
            device_id={axis: peer},
            device_id_type=MESH,
        )

    def behind(k):
        return lax.rem(chip + chips - k, chips)

    def pair_copy(h):
        return remote(
            total.at[h, 1 - core], pairs.at[h], sent_pair.at[h], got_pair.at[h], "terrain", partner
        )

    def part_copy(h, k):
        to = lax.rem(chip + k, chips)
        return remote(
            both.at[h, to], parts.at[h, chip], sent_part.at[h, k], got_part.at[h, k],
            "terrain", 2 * to + core,
        )

    def low_copy(h, k):
        peer = 2 * lax.rem(chip + k, chips) + core if k else partner
        return remote(
            made_low.at[h], net_loss.at[me, h], sent_low.at[h, k], got_low.at[h, k],
            "terrain", peer,
        )

    def more_copy(h, k):
        block = net_loss.at[2 * behind(k) + core, h]
        return remote(block, block, sent_more.at[h, k], got_more.at[h, k], "terrain", partner)

    def net_copy(h, hop):
        return remote(
            made.at[h], arrived.at[group, h], sent_net.at[h, hop], got_net.at[h, hop],
            "event", lax.rem(group + hop, events),
        )

    def give(h):
        pair_copy(h).start()

    def spread(h):
        pair_copy(h).wait()
        both[h] = total[h, core] + pairs[h]
        for k in range(1, chips):
            part_copy(h, k).start()

    def finish(h):
        whole = both[h, chip]
        for k in range(1, chips):
            part_copy(h, k).wait()
            whole = whole + parts[h, behind(k)]
        net = jnp.minimum(jnp.maximum(whole * scale - least[h], 0.0), most[h])
        made[h] = net
        low = net.astype(made_low.dtype)
        made_low[h] = low
        net_loss[me, h] = low
        for hop in range(1, events):
            net_copy(h, hop).start()
        for k in range(1, chips):
            low_copy(h, k).start()
        low_copy(h, 0).start()

    def forward(h):
        for k in range(1, chips):
            low_copy(h, k).wait()
            more_copy(h, k).start()

    stages = ((give, 1), (spread, 2), (finish, 4), (forward, 6))

    account_id = numbered(group_size, cells, 0)
    bin_id = jnp.concatenate([numbered(16, bins, 1)] * (cells // 16), axis=0)
    span = min(SPAN, bundles)

    def one_group(h, _):
        @pl.when(h == 1)
        def _():
            pl.semaphore_wait(barrier, owners + events - 2)

        for stage, lag in stages[::-1]:

            @pl.when(h >= lag)
            def _(stage=stage, lag=lag):
                stage(h - lag)

        rows = pl.ds(pl.multiple_of(h * group_size, group_size), group_size)
        turned = [lax.rem(e + groups - h, together) for e in range(together)]
        summed = None
        for c in range(bundles // span):
            left, right = [], []
            for block in range(span // CHUNK):
                first = c * span + block * CHUNK
                columns = jnp.transpose(bounds[h, first : first + CHUNK, :]).astype(jnp.bfloat16)
                for i in range(CHUNK):
                    bundle = first + i
                    left.append(
                        jnp.where(
                            rowed(lows[h, bundle : bundle + 1, :], group_size) == account_id,
                            rowed(values[h, bundle : bundle + 1, :], group_size),
                            zero,
                        )
                    )
                    shown = []
                    for e in range(together):
                        row = ratio[bundle, turned[e]]
                        shown.extend([row] * (capacity // 16))
                    bound = jnp.broadcast_to(columns[:, i : i + 1], (cells, bins))
                    right.append(
                        jnp.where(bin_id >= bound, jnp.concatenate(shown, axis=0), zero)
                    )
            part = jnp.dot(
                jnp.concatenate(left, axis=1),
                jnp.concatenate(right, axis=0),
                preferred_element_type=jnp.float32,
            )
            summed = part if summed is None else summed + part
        summed = summed + spill[rows, :]
        for t in range(owners):
            total[h, t % 2, t // 2] = summed[t * share_rows : (t + 1) * share_rows]

        return 0

    lax.fori_loop(0, groups, one_group, 0)
    for stage, lag in stages:
        for h in range(groups - lag, groups):
            stage(h)

    def close(h, _):
        whole = made[h]
        for hop in range(1, events):
            net_copy(h, hop).wait()
            whole = whole + arrived[lax.rem(group + events - hop, events), h]
        portfolio[h] = whole / events
        low_copy(h, 0).wait()
        for k in range(1, chips):
            more_copy(h, k).wait()
        return 0

    lax.fori_loop(0, groups, close, 0)


def settle(lows, bounds, values, ratio, spill, floor, roof, scale, number):
    account_count, bins = spill.shape
    groups = lows.shape[0]
    owners, events = lax.axis_size("terrain"), lax.axis_size("event")
    share = (groups, account_count // owners // groups, bins)
    chips = owners // 2
    pieces = (groups, chips) + share[1:]
    dma = pltpu.SemaphoreType.DMA
    return pl.pallas_call(
        functools.partial(settle_kernel, scale),
        out_shape=(
            jax.ShapeDtypeStruct((owners,) + share, jnp.bfloat16),
            jax.ShapeDtypeStruct(share, jnp.float32),
        ),
        in_specs=[VMEM] * 5 + [HBM] * 2,
        out_specs=(VMEM, VMEM),
        scratch_shapes=[pltpu.VMEM(floor.shape, floor.dtype)] * 2
        + [pltpu.VMEM(share, jnp.float32)] * 2
        + [pltpu.VMEM((groups, 2, chips) + share[1:], jnp.float32)]
        + [pltpu.VMEM(pieces, jnp.float32)] * 3
        + [
            pltpu.VMEM(share, jnp.float32),
            pltpu.VMEM(share, jnp.bfloat16),
            pltpu.VMEM((events,) + share, jnp.float32),
        ]
        + [dma((groups,))] * 2
        + [dma((groups, chips))] * 6
        + [dma((groups, events))] * 2
        + [dma((2,))],
        compiler_params=pltpu.CompilerParams(
            collective_id=number, has_side_effects=True, vmem_limit_bytes=LIMIT
        ),
        name="settle",
    )(lows, bounds, values, ratio, spill, *far([floor, roof]))


def place_kernel(*refs):
    sems = refs[-1]
    count = len(refs) // 2
    copies = [
        pltpu.make_async_copy(refs[n], refs[count + n], sems.at[n]) for n in range(count)
    ]
    for copy in copies:
        copy.start()
    for copy in copies:
        copy.wait()


def place(arrays):
    return pl.pallas_call(
        place_kernel,
        out_shape=[jax.ShapeDtypeStruct(a.shape, a.dtype) for a in arrays],
        in_specs=[pl.BlockSpec(memory_space=pl.ANY)] * len(arrays),
        out_specs=[HBM] * len(arrays),
        scratch_shapes=[pltpu.SemaphoreType.DMA((len(arrays),))],
        compiler_params=pltpu.CompilerParams(vmem_limit_bytes=2**20),
        name="place",
    )(*arrays)


def per_device(
    level_start,
    bed_depth,
    wet_bits,
    tile_owner,
    vuln_weight,
    vuln_bias,
    account_index,
    bin_index,
    exposure_value,
    deductible,
    limit,
):
    _, rows, width = level_start.shape
    tile_cells, bin_count = vuln_weight.shape
    account_count = deductible.shape[0]
    owners = lax.axis_size("terrain")
    events = lax.axis_size("event")
    share_rows = account_count // owners
    tiles = rows * width // tile_cells
    level, ratio, low, bound, value = front(
        [level_start[0], bed_depth, wet_bits[0]],
        [account_index, bin_index, exposure_value],
        tile_owner.reshape(1, tiles),
        vuln_weight,
        vuln_bias[None, :],
        1,
    )
    scale = account_count / (rows * width * owners)
    *sorted_cells, level = sort(low, bound, value, ratio, level, account_count)
    net_loss, portfolio = settle(
        *sorted_cells, deductible[None, :], limit[None, :], scale, 2
    )
    net_loss, portfolio = place([net_loss, portfolio])
    portfolio = portfolio.reshape(share_rows, bin_count)
    return (level[None], net_loss.reshape(1, account_count, bin_count), portfolio)


def solution(mesh):
    placed = (
        P("event", "terrain", None),
        P("terrain", None),
        P("event", "terrain", None),
        P("terrain", None),
        P(),
        P(),
        P("terrain", None),
        P("terrain", None),
        P("terrain", None),
        P(),
        P(),
    )
    return jax.shard_map(
        per_device,
        mesh=mesh,
        in_specs=placed,
        out_specs=(P("event", "terrain", None), P("event", None, None), P("terrain", None)),
        check_vma=False,
    )
```

```python
import functools

import jax
import jax.numpy as jnp
from jax import lax
from jax.experimental import pallas as pl
from jax.experimental.pallas import tpu as pltpu
from jax.sharding import PartitionSpec as P

SUBSTEPS = 8
CHUNK = 8
LIMIT = 24 * 2**20
GROUPS = 8
SPAN = 32

courant = 0.5
gravity = 1.0

VMEM = pl.BlockSpec(memory_space=pltpu.VMEM)
HBM = pl.BlockSpec(memory_space=pltpu.HBM)
MESH = pl.DeviceIdType.MESH
PICK = lax.GatherDimensionNumbers(
    offset_dims=(),
    collapsed_slice_dims=(1,),
    start_index_map=(1,),
    operand_batching_dims=(0,),
    start_indices_batching_dims=(0,),
)


def far(arrays):
    return [pltpu.with_memory_space_constraint(a, pltpu.HBM) for a in arrays]


def padded(count, unit):
    return -(-count // unit) * unit


def front_kernel(
    level_far, bed_far, wet_far, account_far, threshold_far, value_far, owner_far, weight_far, bias_far,
    level_out, ratio_out, low_out, bin_out, value_out,
    level_here, bed_here, wet_here, account, threshold, value, owner_row, weight, bias, loads,
    made, kept, got, level_above, bed_above, wet_above, level_below, bed_below, wet_below,
    factors, halo_sent, halo_got, cell_sent, cell_got, local,
):
    size = lax.axis_size("terrain")
    me = lax.axis_index("terrain")
    barrier = pltpu.get_barrier_semaphore()
    for hop in range(1, size):
        pl.semaphore_signal(
            barrier, inc=1, device_id={"terrain": lax.rem(me + hop, size)}, device_id_type=MESH
        )
    moved = (
        (account_far, account), (threshold_far, threshold), (value_far, value),
        (owner_far, owner_row), (level_far, level_here), (bed_far, bed_here), (wet_far, wet_here),
        (weight_far, weight), (bias_far, bias),
    )
    reads = [
        pltpu.make_async_copy(far, near, loads.at[n]) for n, (far, near) in enumerate(moved)
    ]
    for copy in reads:
        copy.start()
    for copy in reads[:4]:
        copy.wait()
    rows, width = level_here.shape
    capacity = account.shape[0] // size
    room = made.shape[2]

    accounts = account[...]
    low = (accounts & 255) - ((accounts >> 8) & 1) * 256
    bound = threshold[...] - (accounts >> 9) * 256
    fields = (low.astype(jnp.float32), bound.astype(jnp.float32), value[...].astype(jnp.float32))
    if room != capacity:
        made[...] = jnp.zeros(made.shape, made.dtype)
    for n in range(size):
        for f in range(3):
            made[n, f, :capacity, :] = fields[f][n * capacity : (n + 1) * capacity].astype(
                made.dtype
            )
    keep = pltpu.make_async_copy(made, kept, local.at[0])
    keep.start()
    pl.semaphore_wait(barrier, size - 1)

    later, earlier = lax.rem(me + 1, size), lax.rem(me + size - 1, size)
    strips = (level_far, bed_far, wet_far)
    above = (level_above, bed_above, wet_above)
    below = (level_below, bed_below, wet_below)
    edges = []
    for side, (peer, targets) in enumerate(((later, above), (earlier, below))):
        for i in range(3):
            first = 0 if side else rows - SUBSTEPS
            copy = pltpu.make_async_remote_copy(
                src_ref=strips[i].at[pl.ds(first, SUBSTEPS)],
                dst_ref=targets[i],
                send_sem=halo_sent.at[side * 3 + i],
                recv_sem=halo_got.at[side * 3 + i],
                device_id={"terrain": peer},
                device_id_type=MESH,
            )
            copy.start()
            edges.append(copy)
    keep.wait()
    cells = []
    for hop in range(1, size):
        peer = lax.rem(me + hop, size)
        copy = pltpu.make_async_remote_copy(
            src_ref=kept.at[peer],
            dst_ref=got.at[me],
            send_sem=cell_sent.at[hop],
            recv_sem=cell_got.at[hop],
            device_id={"terrain": peer},
            device_id_type=MESH,
        )
        copy.start()
        cells.append(copy)
    own = pltpu.make_async_copy(kept.at[me], got.at[me], local.at[1])
    own.start()
    cells.append(own)

    tile = weight.shape[0]
    blocks = width // tile
    tiles = rows * blocks
    number = lax.broadcasted_iota(jnp.int32, (tiles, tiles), 0)
    number = (number % rows) * blocks + number // rows
    along = lax.broadcasted_iota(jnp.int32, (tiles, tiles), 1)
    owner = owner_row[...].astype(jnp.float32)
    owner_column = jnp.sum(jnp.where(along == number, owner, 0.0), axis=1, keepdims=True)
    same = (owner_column == owner) & (along < number)
    rank = jnp.sum(jnp.where(same, 1.0, 0.0), axis=1, keepdims=True)
    slot = lax.broadcasted_iota(jnp.int32, (tiles, size * room), 1).astype(jnp.float32)
    chosen = jnp.where(slot == owner_column * room + rank, 1.0, 0.0).astype(jnp.bfloat16)

    for copy in reads[4:]:
        copy.wait()
    assert courant * gravity == 0.5
    quarter = 0.25
    tall = rows + 2 * SUBSTEPS
    first_row = me * rows - SUBSTEPS
    total_rows = rows * size

    def inner(first, count):
        row = first_row + first + lax.broadcasted_iota(jnp.int32, (count, tile), 0)
        return jnp.where((row >= 0) & (row < total_rows), quarter, 0.0)

    def mark(bits, first):
        for j in range(blocks):
            span = slice(j * tile, (j + 1) * tile)
            here = bits[:, span]
            weight_here = inner(first, bits.shape[0])
            for step in range(SUBSTEPS):
                factor = jnp.where((here & (1 << step)) != 0, weight_here, 0.0)
                factors[step, j, first : first + bits.shape[0], :] = factor

    mark(wet_here, SUBSTEPS)
    for copy in edges:
        copy.wait()
    mark(wet_above, 0)
    mark(wet_below, SUBSTEPS + rows)
    lane = lax.broadcasted_iota(jnp.int32, (tall, tile), 1)
    at_first, at_last = lane == 0, lane == tile - 1
    inside = inner(0, tall)

    def stacked(above, here, below):
        whole = jnp.concatenate([above[...], here[...], below[...]], axis=0)
        return [whole[:, j * tile : (j + 1) * tile] for j in range(blocks)]

    level = stacked(level_above, level_here, level_below)
    bed = stacked(bed_above, bed_here, bed_below)
    level = [jnp.where(inside > 0, field, 0.0) for field in level]

    def down(field):
        return pltpu.roll(field, tall - 1, 0)

    def up(field):
        return pltpu.roll(field, 1, 0)

    def right(fields):
        turned = [pltpu.roll(field, tile - 1, 1) for field in fields] + [0.0]
        return [jnp.where(at_last, turned[j + 1], turned[j]) for j in range(blocks)]

    def left(fields):
        turned = [0.0] + [pltpu.roll(field, 1, 1) for field in fields]
        return [jnp.where(at_first, turned[j], turned[j + 1]) for j in range(blocks)]

    def each(function, *fields):
        return [function(*of_block) for of_block in zip(*fields)]

    def plus(one, other):
        return each(lambda a, b: a + b, one, other)

    def minus(one, other):
        return each(lambda a, b: a - b, one, other)

    for step in range(SUBSTEPS):
        factor = [factors[step, j] for j in range(blocks)]
        if step:
            row_flow = each(lambda a, b: a * b, bed, row_speed)
            col_flow = each(lambda a, b: a * b, bed, col_speed)
            new_level = each(
                lambda d, u, r, l: (down(d) + up(u) + (r + l)) * inside,
                minus(level, row_flow), plus(level, row_flow),
                right(minus(level, col_flow)), left(plus(level, col_flow)),
            )
            new_row = each(
                lambda d, u, r, l, f: (down(d) + up(u) + (r + l)) * f,
                minus(row_speed, level), plus(row_speed, level),
                right(row_speed), left(row_speed), factor,
            )
            col_speed = each(
                lambda c, r, l, f: (down(c) + up(c) + (r + l)) * f,
                col_speed, right(minus(col_speed, level)), left(plus(col_speed, level)), factor,
            )
            row_speed = new_row
        else:
            beside, before = right(level), left(level)
            new_level = each(
                lambda c, r, l: (down(c) + up(c) + (r + l)) * inside, level, beside, before
            )
            row_speed = each(lambda c, f: (up(c) - down(c)) * f, level, factor)
            col_speed = each(lambda r, l, f: (l - r) * f, beside, before, factor)
        level = new_level
    level = [field[SUBSTEPS : SUBSTEPS + rows] for field in level]
    for j in range(blocks):
        level_out[:, j * tile : (j + 1) * tile] = level[j]
    pieces = jnp.concatenate(level, axis=0).astype(jnp.bfloat16)
    ratio_out[...] = jax.nn.sigmoid(
        jnp.dot(pieces, weight[...], preferred_element_type=jnp.float32) + bias[...]
    ).astype(jnp.bfloat16)
    for copy in cells:
        copy.wait()
    for f, target in enumerate((low_out, bin_out, value_out)):
        records = jnp.concatenate([got[n, f] for n in range(size)], axis=0)
        target[...] = jnp.dot(chosen, records, preferred_element_type=jnp.float32).astype(
            target.dtype
        )


def front(strips, records, owner_row, weight, bias, number):
    rows, width = strips[0].shape
    slots, cells = records[0].shape
    size = lax.axis_size("terrain")
    tiles = rows * width // cells
    packed = (size, 3, padded(slots // size, 16), cells)
    edge = (SUBSTEPS, width)
    inputs = strips + records + [owner_row, weight, bias]
    dma = pltpu.SemaphoreType.DMA
    edges = [pltpu.VMEM(edge, f.dtype) for f in strips]
    return pl.pallas_call(
        front_kernel,
        out_shape=(
            jax.ShapeDtypeStruct((rows, width), jnp.float32),
            jax.ShapeDtypeStruct((tiles, weight.shape[1]), jnp.bfloat16),
        )
        + (jax.ShapeDtypeStruct((tiles, cells), jnp.bfloat16),) * 3,
        in_specs=[HBM] * 9,
        out_specs=(VMEM,) * 5,
        scratch_shapes=[pltpu.VMEM(a.shape, a.dtype) for a in inputs]
        + [dma((9,))]
        + [pltpu.VMEM(packed, jnp.bfloat16)] * 3
        + edges * 2
        + [pltpu.VMEM((SUBSTEPS, width // cells, rows + 2 * SUBSTEPS, cells), jnp.float32)]
        + [dma((6,))] * 2
        + [dma((size,))] * 2
        + [dma((2,))],
        compiler_params=pltpu.CompilerParams(
            collective_id=number, has_side_effects=True, vmem_limit_bytes=LIMIT
        ),
        name="front",
    )(*far(inputs))


def rowed(row, height):
    packed = jnp.broadcast_to(row, (16, row.shape[1])).astype(jnp.bfloat16)
    return jnp.concatenate([packed] * (height // 16), axis=0)


def over(number, power):
    assert power & (power - 1) == 0
    return number >> (power.bit_length() - 1)


def rest(number, power):
    assert power & (power - 1) == 0
    return number & (power - 1)


def numbered(height, width, axis):
    return (
        lax.broadcasted_iota(jnp.int32, (height, width), axis)
        .astype(jnp.float32)
        .astype(jnp.bfloat16)
    )


def sort_kernel(
    owners, low_in, bin_in, value_in, ratio_in, level_in,
    lows, bounds, values, ratio, total, level_out,
    ratio_all, low_all, bound_all, value_all, places, keys, worths,
):
    level_out[...] = level_in[...]
    total[...] = jnp.zeros(total.shape, jnp.float32)
    accounts, bins = total.shape
    tiles, cells = low_in.shape
    groups = lows.shape[0]
    group_size = accounts // groups
    capacity = 2 * cells // groups
    together = cells // capacity
    bundles = tiles // together
    zero = jnp.zeros((), jnp.bfloat16)

    ratio_all[...] = ratio_in[...].astype(jnp.float32)

    def widen(number, _):
        for u in range(8):
            for j in range(together):
                row = ratio_all[pl.ds((number * 8 + u) * together + j, 1), :]
                ratio[number * 8 + u, j] = jnp.broadcast_to(row, (16, bins)).astype(jnp.bfloat16)
        return 0

    lax.fori_loop(0, bundles // 8, widen, 0)

    low = low_in[...].astype(jnp.float32)
    bound = bin_in[...].astype(jnp.float32)
    value = value_in[...].astype(jnp.float32)
    high = jnp.where(low < 0, 256.0, 0.0) + jnp.where(bound < 0, 512.0, 0.0)
    account = (jnp.where(low < 0, low + 256.0, low) + high).astype(jnp.int32)
    bound = jnp.where(bound < 0, bound + 256.0, bound).astype(jnp.int32)
    share = accounts // owners
    rows = share // groups
    group = over(rest(account, share), rows)
    low = over(account, share) * rows + rest(account, rows)
    key = low * 256 + bound
    first = lax.broadcasted_iota(jnp.int32, (cells, cells), 0)
    second = lax.broadcasted_iota(jnp.int32, (cells, cells), 1)
    upto = jnp.where(first <= second, 1.0, 0.0).astype(jnp.bfloat16)

    lane = lax.broadcasted_iota(jnp.int32, (tiles, cells), 1)
    turn = rest(lax.broadcasted_iota(jnp.int32, (tiles, cells), 0), together)
    wanted = rest(lane, capacity)
    shift = rest(over(lane, capacity) + together - turn, together) * 8
    order = jnp.zeros((tiles, cells), jnp.float32)

    def taken(table, place):
        return lax.gather(
            table, place[..., None], PICK, (1, 1), mode=lax.GatherScatterMode.PROMISE_IN_BOUNDS
        )

    for q in range(2):
        table = jnp.zeros((tiles, cells), jnp.int32)
        for r in range(together):
            mine = group == q * together + r
            count = jnp.dot(
                jnp.where(mine, 1.0, 0.0).astype(jnp.bfloat16),
                upto,
                preferred_element_type=jnp.float32,
            )
            order = jnp.where(mine, count, order)
            table = table + lax.shift_left(count.astype(jnp.int32), 8 * r)

        def count_at(place):
            return lax.shift_right_logical(taken(table, place), shift) & 255

        place = jnp.zeros((tiles, cells), jnp.int32)
        step = cells // 2
        while step:
            place = jnp.where(count_at(place + (step - 1)) <= wanted, place + step, place)
            step //= 2
        keys[q] = taken(key, place)
        worths[q] = jnp.where(count_at(place) > wanted, taken(value, place), 0.0)

    block = over(lax.broadcasted_iota(jnp.int32, (bundles, cells), 1), capacity)
    for q in range(2):
        for r in range(together):
            for source, targets in ((keys, (lows, bounds)), (worths, (values,))):
                mixed = source[q, pl.ds((0 - r) % together, bundles, stride=together), :]
                for e in range(1, together):
                    part = source[q, pl.ds((e - r) % together, bundles, stride=together), :]
                    mixed = jnp.where(block == e, part, mixed)
                if len(targets) == 1:
                    values[q * together + r] = mixed
                else:
                    lows[q * together + r] = (mixed >> 8).astype(jnp.float32)
                    bounds[q * together + r] = (mixed & 255).astype(jnp.float32)

    @pl.when(jnp.max(order) > capacity)
    def _():
        tile_id = lax.broadcasted_iota(jnp.int32, (tiles, cells), 0)
        late = (tile_id * groups + group).astype(jnp.float32)
        places[...] = jnp.where(order > capacity, late, -1.0)
        low_all[...] = low.astype(jnp.float32)
        bound_all[...] = bound.astype(jnp.float32)
        value_all[...] = value
        account_id = numbered(group_size, cells, 0)
        bin_id = jnp.concatenate([numbered(16, bins, 1)] * (cells // 16), axis=0)

        def dense(left_over):
            t = over(left_over.astype(jnp.int32), groups)
            h = rest(left_over.astype(jnp.int32), groups)
            worth = jnp.where(
                places[pl.ds(t, 1), :] == left_over, value_all[pl.ds(t, 1), :], 0.0
            )
            left = jnp.where(
                rowed(low_all[pl.ds(t, 1), :], group_size) == account_id,
                rowed(worth, group_size),
                zero,
            )
            columns = jnp.transpose(jnp.broadcast_to(bound_all[pl.ds(t, 1), :], (8, cells)))
            right = jnp.where(
                bin_id >= jnp.broadcast_to(columns.astype(jnp.bfloat16)[:, 0:1], (cells, bins)),
                rowed(ratio_all[pl.ds(t, 1), :], cells),
                zero,
            )
            spot = pl.ds(pl.multiple_of(h * group_size, group_size), group_size)
            total[spot, :] += jnp.dot(left, right, preferred_element_type=jnp.float32)
            return jnp.max(jnp.where(places[...] < left_over, places[...], -1.0))

        lax.while_loop(
            lambda left_over: left_over >= 0, dense, jnp.max(places[...])
        )


def sort(low, bound, value, ratio, level, account_count):
    tiles, cells = low.shape
    bins = ratio.shape[1]
    together = GROUPS // 2
    bundles = tiles // together
    gathered = jax.ShapeDtypeStruct((GROUPS, bundles, cells), jnp.float32)
    whole = pltpu.VMEM((tiles, cells), jnp.float32)
    return pl.pallas_call(
        functools.partial(sort_kernel, lax.axis_size("terrain")),
        out_shape=(
            gathered,
            gathered,
            gathered,
            jax.ShapeDtypeStruct((bundles, together, 16, bins), jnp.bfloat16),
            jax.ShapeDtypeStruct((account_count, bins), jnp.float32),
            jax.ShapeDtypeStruct(level.shape, level.dtype),
        ),
        in_specs=[VMEM] * 5,
        out_specs=(VMEM,) * 6,
        scratch_shapes=[pltpu.VMEM((tiles, bins), jnp.float32)]
        + [whole] * 4
        + [pltpu.VMEM((2, tiles, cells), dtype) for dtype in (jnp.int32, jnp.float32)],
        compiler_params=pltpu.CompilerParams(vmem_limit_bytes=LIMIT),
        name="sort",
    )(low, bound, value, ratio, level)


def settle_kernel(
    scale, lows, bounds, values, ratio, spill, floor_far, roof_far,
    net_loss, portfolio,
    floor, roof, least, most, total, pairs, both, parts, made, made_low, arrived,
    sent_pair, got_pair, sent_part, got_part, sent_low, got_low, sent_more, got_more,
    sent_net, got_net, local,
):
    groups, _, chips, share_rows, bins = total.shape
    owners = 2 * chips
    _, bundles, cells = lows.shape
    group_size = owners * share_rows
    capacity = 2 * cells // groups
    together = cells // capacity
    zero = jnp.zeros((), jnp.bfloat16)
    events = lax.axis_size("event")
    me, group = lax.axis_index("terrain"), lax.axis_index("event")
    terms = [
        pltpu.make_async_copy(floor_far, floor, local.at[0]),
        pltpu.make_async_copy(roof_far, roof, local.at[1]),
    ]
    for copy in terms:
        copy.start()
    barrier = pltpu.get_barrier_semaphore()
    for axis, size, mine in (("terrain", owners, me), ("event", events, group)):
        for hop in range(1, size):
            pl.semaphore_signal(
                barrier, inc=1, device_id={axis: lax.rem(mine + hop, size)}, device_id_type=MESH
            )
    for copy in terms:
        copy.wait()
    picked = (groups * share_rows, floor.shape[1])
    account = lax.broadcasted_iota(jnp.int32, picked, 1)
    mine = account == lax.broadcasted_iota(jnp.int32, picked, 0) + me * picked[0]
    for near, wide in ((floor, least), (roof, most)):
        column = jnp.sum(jnp.where(mine, near[...], 0.0), axis=1, keepdims=True)
        column = jnp.broadcast_to(column, (picked[0], bins))
        for h in range(groups):
            wide[h] = column[h * share_rows : (h + 1) * share_rows]
    core, chip = lax.rem(me, 2), me // 2
    partner = me + 1 - 2 * core

    def remote(source, target, sent, received, axis, peer):
        return pltpu.make_async_remote_copy(
            src_ref=source,
            dst_ref=target,
            send_sem=sent,
            recv_sem=received,
            device_id={axis: peer},
            device_id_type=MESH,
        )

    def behind(k):
        return lax.rem(chip + chips - k, chips)

    def pair_copy(h):
        return remote(
            total.at[h, 1 - core], pairs.at[h], sent_pair.at[h], got_pair.at[h], "terrain", partner
        )

    def part_copy(h, k):
        to = lax.rem(chip + k, chips)
        return remote(
            both.at[h, to], parts.at[h, chip], sent_part.at[h, k], got_part.at[h, k],
            "terrain", 2 * to + core,
        )

    def low_copy(h, k):
        peer = 2 * lax.rem(chip + k, chips) + core if k else partner
        return remote(
            made_low.at[h], net_loss.at[me, h], sent_low.at[h, k], got_low.at[h, k],
            "terrain", peer,
        )

    def more_copy(h, k):
        block = net_loss.at[2 * behind(k) + core, h]
        return remote(block, block, sent_more.at[h, k], got_more.at[h, k], "terrain", partner)

    def net_copy(h, hop):
        return remote(
            made.at[h], arrived.at[group, h], sent_net.at[h, hop], got_net.at[h, hop],
            "event", lax.rem(group + hop, events),
        )

    def give(h):
        pair_copy(h).start()

    def spread(h):
        pair_copy(h).wait()
        both[h] = total[h, core] + pairs[h]
        for k in range(1, chips):
            part_copy(h, k).start()

    def finish(h):
        whole = both[h, chip]
        for k in range(1, chips):
            part_copy(h, k).wait()
            whole = whole + parts[h, behind(k)]
        net = jnp.minimum(jnp.maximum(whole * scale - least[h], 0.0), most[h])
        made[h] = net
        low = net.astype(made_low.dtype)
        made_low[h] = low
        net_loss[me, h] = low
        for hop in range(1, events):
            net_copy(h, hop).start()
        for k in range(1, chips):
            low_copy(h, k).start()
        low_copy(h, 0).start()

    def forward(h):
        for k in range(1, chips):
            low_copy(h, k).wait()
            more_copy(h, k).start()

    stages = ((give, 1), (spread, 2), (finish, 4), (forward, 6))

    account_id = numbered(group_size, cells, 0)
    bin_id = jnp.concatenate([numbered(16, bins, 1)] * (cells // 16), axis=0)
    span = min(SPAN, bundles)

    def one_group(h, _):
        @pl.when(h == 1)
        def _():
            pl.semaphore_wait(barrier, owners + events - 2)

        for stage, lag in (stages[1], stages[0], stages[2], stages[3]):

            @pl.when(h >= lag)
            def _(stage=stage, lag=lag):
                stage(h - lag)

        rows = pl.ds(pl.multiple_of(h * group_size, group_size), group_size)
        turned = [lax.rem(e + groups - h, together) for e in range(together)]
        summed = None
        for c in range(bundles // span):
            left, right = [], []
            for block in range(span // CHUNK):
                first = c * span + block * CHUNK
                columns = jnp.transpose(bounds[h, first : first + CHUNK, :]).astype(jnp.bfloat16)
                for i in range(CHUNK):
                    bundle = first + i
                    left.append(
                        jnp.where(
                            rowed(lows[h, bundle : bundle + 1, :], group_size) == account_id,
                            rowed(values[h, bundle : bundle + 1, :], group_size),
                            zero,
                        )
                    )
                    shown = []
                    for e in range(together):
                        row = ratio[bundle, turned[e]]
                        shown.extend([row] * (capacity // 16))
                    bound = jnp.broadcast_to(columns[:, i : i + 1], (cells, bins))
                    right.append(
                        jnp.where(bin_id >= bound, jnp.concatenate(shown, axis=0), zero)
                    )
            part = jnp.dot(
                jnp.concatenate(left, axis=1),
                jnp.concatenate(right, axis=0),
                preferred_element_type=jnp.float32,
            )
            summed = part if summed is None else summed + part
        summed = summed + spill[rows, :]
        for t in range(owners):
            total[h, t % 2, t // 2] = summed[t * share_rows : (t + 1) * share_rows]

        return 0

    lax.fori_loop(0, groups, one_group, 0)
    for stage, lag in stages:
        for h in range(groups - lag, groups):
            stage(h)

    def close(h, _):
        whole = made[h]
        for hop in range(1, events):
            net_copy(h, hop).wait()
            whole = whole + arrived[lax.rem(group + events - hop, events), h]
        portfolio[h] = whole / events
        low_copy(h, 0).wait()
        for k in range(1, chips):
            more_copy(h, k).wait()
        return 0

    lax.fori_loop(0, groups, close, 0)


def settle(lows, bounds, values, ratio, spill, floor, roof, scale, number):
    account_count, bins = spill.shape
    groups = lows.shape[0]
    owners, events = lax.axis_size("terrain"), lax.axis_size("event")
    share = (groups, account_count // owners // groups, bins)
    chips = owners // 2
    pieces = (groups, chips) + share[1:]
    dma = pltpu.SemaphoreType.DMA
    return pl.pallas_call(
        functools.partial(settle_kernel, scale),
        out_shape=(
            jax.ShapeDtypeStruct((owners,) + share, jnp.bfloat16),
            jax.ShapeDtypeStruct(share, jnp.float32),
        ),
        in_specs=[VMEM] * 5 + [HBM] * 2,
        out_specs=(VMEM, VMEM),
        scratch_shapes=[pltpu.VMEM(floor.shape, floor.dtype)] * 2
        + [pltpu.VMEM(share, jnp.float32)] * 2
        + [pltpu.VMEM((groups, 2, chips) + share[1:], jnp.float32)]
        + [pltpu.VMEM(pieces, jnp.float32)] * 3
        + [
            pltpu.VMEM(share, jnp.float32),
            pltpu.VMEM(share, jnp.bfloat16),
            pltpu.VMEM((events,) + share, jnp.float32),
        ]
        + [dma((groups,))] * 2
        + [dma((groups, chips))] * 6
        + [dma((groups, events))] * 2
        + [dma((2,))],
        compiler_params=pltpu.CompilerParams(
            collective_id=number, has_side_effects=True, vmem_limit_bytes=LIMIT
        ),
        name="settle",
    )(lows, bounds, values, ratio, spill, *far([floor, roof]))


def place_kernel(*refs):
    sems = refs[-1]
    count = len(refs) // 2
    copies = [
        pltpu.make_async_copy(refs[n], refs[count + n], sems.at[n]) for n in range(count)
    ]
    for copy in copies:
        copy.start()
    for copy in copies:
        copy.wait()


def place(arrays):
    return pl.pallas_call(
        place_kernel,
        out_shape=[jax.ShapeDtypeStruct(a.shape, a.dtype) for a in arrays],
        in_specs=[pl.BlockSpec(memory_space=pl.ANY)] * len(arrays),
        out_specs=[HBM] * len(arrays),
        scratch_shapes=[pltpu.SemaphoreType.DMA((len(arrays),))],
        compiler_params=pltpu.CompilerParams(vmem_limit_bytes=2**20),
        name="place",
    )(*arrays)


def per_device(
    level_start,
    bed_depth,
    wet_bits,
    tile_owner,
    vuln_weight,
    vuln_bias,
    account_index,
    bin_index,
    exposure_value,
    deductible,
    limit,
):
    _, rows, width = level_start.shape
    tile_cells, bin_count = vuln_weight.shape
    account_count = deductible.shape[0]
    owners = lax.axis_size("terrain")
    events = lax.axis_size("event")
    share_rows = account_count // owners
    tiles = rows * width // tile_cells
    level, ratio, low, bound, value = front(
        [level_start[0], bed_depth, wet_bits[0]],
        [account_index, bin_index, exposure_value],
        tile_owner.reshape(1, tiles),
        vuln_weight,
        vuln_bias[None, :],
        1,
    )
    scale = account_count / (rows * width * owners)
    *sorted_cells, level = sort(low, bound, value, ratio, level, account_count)
    net_loss, portfolio = settle(
        *sorted_cells, deductible[None, :], limit[None, :], scale, 2
    )
    net_loss, portfolio = place([net_loss, portfolio])
    portfolio = portfolio.reshape(share_rows, bin_count)
    return (level[None], net_loss.reshape(1, account_count, bin_count), portfolio)


def solution(mesh):
    placed = (
        P("event", "terrain", None),
        P("terrain", None),
        P("event", "terrain", None),
        P("terrain", None),
        P(),
        P(),
        P("terrain", None),
        P("terrain", None),
        P("terrain", None),
        P(),
        P(),
    )
    return jax.shard_map(
        per_device,
        mesh=mesh,
        in_specs=placed,
        out_specs=(P("event", "terrain", None), P("event", None, None), P("terrain", None)),
        check_vma=False,
    )
```
